512 devices in a mesh: clip: 16 (over y_lo, z), seq: 32 (over x, y_hi, core).
Axes of the slice: x: 4, y: 8 (y_hi: 4, y_lo: 2; y = y_hi * 2 + y_lo), z: 8, core: 2. Of those that a mesh axis runs over, the one named last changes fastest.
Arguments:
- patches: bfloat16 [16, 6272, 1024], P('clip', 'seq'), may hold values from -6 to 12
- segment: int32 [16, 6272], P('clip', 'seq'), may hold values from 0 to 191, as said below
- dest_shard: int32 [16, 6144], P('clip', 'seq'), may hold values from -1 to 31, as said below
- dest_slot: int32 [16, 6144], P('clip', 'seq'), may hold values from -1 to 63, as said below
- w_qkv: bfloat16 [1024, 1536], replicated, may hold values from -1 to 4
- out_grad: bfloat16 [16, 2048, 512], P('clip', 'seq'), may hold values from -6 to 6
Outputs:
- attended: bfloat16 [16, 2048, 512], P('clip', 'seq')
- patch_grad: bfloat16 [16, 6272, 1024], P('clip', 'seq')
- weight_grad: float32 [1024, 1536], P('seq', 'clip')
The draws below stay inside these ranges and needn't reach their ends.
Inputs may be any that keep to these rules, and one draw needn't show every extreme that they name: `segment`: within each block of 196 patches the ids start at 0, never fall and skip no value; every id names one or more patches. The number of tokens of a block is one more than its largest id. `dest_shard`: -1 exactly on the rows of a block past its number of tokens. A block of 192 rows sends at most 6 rows to each receiving block of its clip, and every receiving block gets exactly 64 rows. `dest_slot`: -1 exactly where dest_shard is -1; the rows sent to one receiving block take its rows 0 to 63 once each.
All inputs are finite; a program needn't handle non-finite values.
Results may differ from the reference program's by a relative error of at most 0.024.
Values may be sent and summed in bfloat16 or wider, within the bound.
A program may use at most 64 MiB of HBM per device.

```python
import jax
import jax.numpy as jnp
from jax import lax

D = 1024
HEADS = 8
HEAD_DIM = 64
R_DEV = 64
INNER = 512
P_DEV = 196
TOK_MAX = 192
CLIPS = 16
PATCHES = 6272
ROWS = 2048
TOK_ROWS = 6144
N_SEQ = 32


base_tokens = 16


def clip_plan(key):
    shard_count = PATCHES // P_DEV
    total_rows = shard_count * R_DEV
    shard_index = jnp.arange(shard_count, dtype=jnp.int32)
    planted = jax.random.randint(jax.random.fold_in(key, 1), (), 0, shard_count)
    raw_weight = jax.random.randint(jax.random.fold_in(key, 2), (shard_count,), 1, 4)
    weighting = jnp.where(shard_index == planted, 0, raw_weight)
    surplus = total_rows - TOK_MAX - (shard_count - 1) * base_tokens
    upper = jnp.cumsum(weighting)
    lower = upper - weighting
    weight_sum = upper[-1]
    shares = surplus * upper // weight_sum - surplus * lower // weight_sum
    loads = jnp.where(shard_index == planted, TOK_MAX, base_tokens + shares).astype(jnp.int32)

    def shard_segments(index):
        ranking = jnp.argsort(jax.random.permutation(jax.random.fold_in(key, 100 + index), P_DEV - 1))
        cutting = (ranking < loads[index] - 1).astype(jnp.int32)
        return jnp.concatenate([jnp.zeros((1,), jnp.int32), jnp.cumsum(cutting).astype(jnp.int32)])
    segments = jax.vmap(shard_segments)(shard_index).reshape(-1)
    offsets = jnp.cumsum(loads) - loads
    local_rows = jnp.arange(TOK_MAX, dtype=jnp.int32)
    global_rows = offsets[:, None] + local_rows[None, :]
    living = local_rows[None, :] < loads[:, None]
    turning = jax.random.randint(jax.random.fold_in(key, 3), (), 0, shard_count)
    targets = (global_rows + turning) % shard_count
    ranks = (global_rows - (targets - turning) % shard_count) // shard_count
    ranks = jnp.clip(ranks, 0, R_DEV - 1)

    def slot_order(subkey):
        return jax.random.permutation(subkey, R_DEV)
    orders = jax.vmap(slot_order)(jax.random.split(jax.random.fold_in(key, 4), shard_count))
    slots = orders[targets, ranks]
    shard_dest = jnp.where(living, targets, -1).reshape(-1).astype(jnp.int32)
    shard_slot = jnp.where(living, slots, -1).reshape(-1).astype(jnp.int32)
    return (segments.astype(jnp.int32), shard_dest, shard_slot)


def plan_all(key):
    clip_keys = jax.random.split(jax.random.fold_in(key, 7), CLIPS)
    return jax.vmap(clip_plan)(clip_keys)


def plant_plan(key):
    features = jax.random.permutation(jax.random.fold_in(key, 11), D)[:HEADS].astype(jnp.int32)
    columns = jax.random.randint(jax.random.fold_in(key, 12), (HEADS,), 0, HEAD_DIM).astype(jnp.int32)
    return (features, columns)


def draw_segment(key, part):
    return plan_all(key)[0]


def draw_dest_shard(key, part):
    return plan_all(key)[1]


def draw_dest_slot(key, part):
    return plan_all(key)[2]


def draw_w_qkv(key, part):
    features, columns = plant_plan(key)
    weight_key = jax.random.fold_in(key, 13)
    random_part = jax.random.truncated_normal(weight_key, -6.0, 6.0, (D, 3 * INNER), jnp.float32)
    random_part = random_part * D ** (-0.5)
    strength = 4.0
    head_columns = jnp.arange(HEADS, dtype=jnp.int32) * HEAD_DIM + columns
    special = jnp.concatenate([head_columns, head_columns + INNER])
    special_rows = jnp.concatenate([features, features])
    matching = jnp.arange(3 * INNER, dtype=jnp.int32)[:, None] == special[None, :]
    is_special = jnp.any(matching, axis=1)
    row_of = jnp.sum(jnp.where(matching, special_rows[None, :], 0), axis=1)
    planted = jnp.where(jnp.arange(D, dtype=jnp.int32)[:, None] == row_of[None, :], strength, 0.0)
    return jnp.where(is_special[None, :], planted, random_part).astype(jnp.bfloat16)


def draw_patches(key, part):
    segments = plan_all(key)[0]
    features, columns = plant_plan(key)
    shard_count = PATCHES // P_DEV
    feature_ids = jnp.arange(D, dtype=jnp.int32)
    marked = jnp.any(feature_ids[:, None] == features[None, :], axis=1)
    feature_scale = jnp.where(marked, 1.0 / 64.0, 1.0)
    block_of = jnp.arange(PATCHES, dtype=jnp.int32) // P_DEV
    clip_keys = jax.random.split(jax.random.fold_in(key, 14), CLIPS)

    def one_clip(inputs):
        clip_key, clip_segments = inputs
        noise_rows = jax.random.truncated_normal(clip_key, -6.0, 6.0, (PATCHES, D), jnp.float32)
        item_index = clip_segments * shard_count + block_of
        planted = item_index < 6 * HEADS
        head_of = jnp.minimum(item_index // 6, HEADS - 1)
        strength = item_index % 6 // 2
        partner = (item_index % 2).astype(jnp.float32)
        amount = 8.0 + 2.0 * strength.astype(jnp.float32) - partner * jnp.where(strength == 0, 0.125, 0.0625)
        row_scale = jnp.where(planted, 0.5, 1.0)
        noisy_rows = noise_rows * feature_scale[None, :] * row_scale[:, None]
        planted_cell = planted[:, None] & (feature_ids[None, :] == features[head_of][:, None])
        return jnp.where(planted_cell, amount[:, None], noisy_rows)
    return lax.map(one_clip, (clip_keys, segments)).astype(jnp.bfloat16)


def draw_out_grad(key, part):
    segments, dests, slots = plan_all(key)
    shard_count = PATCHES // P_DEV
    token_rows = jnp.arange(TOK_ROWS, dtype=jnp.int32)
    item_index = token_rows % TOK_MAX * shard_count + token_rows // TOK_MAX
    clip_keys = jax.random.split(jax.random.fold_in(key, 21), CLIPS)

    def one_clip(inputs):
        clip_key, clip_dest, clip_slot = inputs
        planted = (item_index < 6 * HEADS) & (clip_dest >= 0)
        target = jnp.where(clip_dest >= 0, clip_dest * R_DEV + clip_slot, -1)
        hit = jnp.any((target[None, :] == jnp.arange(ROWS, dtype=jnp.int32)[:, None]) & planted[None, :], axis=1)
        row_scale = jnp.where(hit, 1.0 / 16.0, 1.0)
        noise_rows = jax.random.truncated_normal(clip_key, -6.0, 6.0, (ROWS, INNER), jnp.float32)
        return noise_rows * row_scale[:, None]
    return lax.map(one_clip, (clip_keys, dests, slots)).astype(jnp.bfloat16)


def setup_inputs(seed: int = 0) -> dict:
    splits = jax.random.split(jax.random.key(seed), 7)
    patches = draw_patches(jax.random.fold_in(splits[6], 71), 0)
    segment = draw_segment(jax.random.fold_in(splits[6], 71), 0)
    dest_shard = draw_dest_shard(jax.random.fold_in(splits[6], 71), 0)
    dest_slot = draw_dest_slot(jax.random.fold_in(splits[6], 71), 0)
    w_qkv = draw_w_qkv(jax.random.fold_in(splits[6], 71), 0)
    out_grad = draw_out_grad(jax.random.fold_in(splits[6], 71), 0)
    return dict(patches=patches, segment=segment, dest_shard=dest_shard, dest_slot=dest_slot, w_qkv=w_qkv, out_grad=out_grad)


def one_clip(w_qkv, clip_patches, clip_segment, clip_dest, clip_slot, clip_grad):
    scaling = HEAD_DIM ** -0.5
    shard_of = jnp.arange(PATCHES, dtype=jnp.int32) // P_DEV
    token_id = (shard_of * TOK_MAX + clip_segment).astype(jnp.int32)
    token_sums = jax.ops.segment_sum(clip_patches.astype(jnp.float32), token_id, num_segments=TOK_ROWS)
    counts = jax.ops.segment_sum(jnp.ones((PATCHES,), jnp.float32), token_id, num_segments=TOK_ROWS)
    tokens = (token_sums / jnp.maximum(counts, 1.0)[:, None]).astype(jnp.bfloat16)
    target = jnp.where(clip_dest >= 0, clip_dest * R_DEV + clip_slot, ROWS).astype(jnp.int32)
    placed = jnp.zeros((ROWS, D), jnp.bfloat16).at[target].set(tokens, mode="drop")
    projected = jnp.dot(placed, w_qkv, preferred_element_type=jnp.float32).astype(jnp.bfloat16)

    def by_heads(matrix):
        return matrix.reshape(ROWS, HEADS, HEAD_DIM).transpose(1, 0, 2)

    head_query = by_heads(projected[:, :INNER])
    head_key = by_heads(projected[:, INNER:2 * INNER])
    head_value = by_heads(projected[:, 2 * INNER:])
    head_grad = by_heads(clip_grad)

    def per_head(inputs):
        query, keys_in, values, grads = inputs
        scores = jnp.dot(query, keys_in.T, preferred_element_type=jnp.float32) * scaling
        row_max = jnp.max(scores, axis=1, keepdims=True)
        weights = jnp.exp(scores - row_max)
        row_total = jnp.sum(weights, axis=1, keepdims=True)
        output = jnp.dot(weights.astype(jnp.bfloat16), values, preferred_element_type=jnp.float32)
        output = (output / row_total).astype(jnp.bfloat16)
        log_total = row_max + jnp.log(row_total)
        grad_dot = jnp.sum(grads.astype(jnp.float32) * output.astype(jnp.float32), axis=1, keepdims=True)
        probability = jnp.exp(scores - log_total)
        prob_grad = jnp.dot(grads, values.T, preferred_element_type=jnp.float32)
        score_grad = (probability * (prob_grad - grad_dot)).astype(jnp.bfloat16)
        query_grad = jnp.dot(score_grad, keys_in, preferred_element_type=jnp.float32) * scaling
        key_grad = jnp.dot(score_grad.T, query, preferred_element_type=jnp.float32) * scaling
        value_grad = jnp.dot(probability.astype(jnp.bfloat16).T, grads, preferred_element_type=jnp.float32)
        return output, query_grad, key_grad, value_grad

    results = lax.map(per_head, (head_query, head_key, head_value, head_grad))

    def to_rows(matrix):
        return matrix.transpose(1, 0, 2).reshape(ROWS, INNER)

    attended = to_rows(results[0])
    proj_grad = jnp.concatenate([to_rows(results[1]), to_rows(results[2]), to_rows(results[3])], axis=1).astype(jnp.bfloat16)
    placed_grad = jnp.dot(proj_grad, w_qkv.T, preferred_element_type=jnp.float32).astype(jnp.bfloat16)

    def add_shard(running, inputs):
        shard_rows, shard_grads = inputs
        partial_value = jnp.dot(shard_rows.T, shard_grads, preferred_element_type=jnp.float32).astype(jnp.bfloat16)
        return running + partial_value.astype(jnp.float32), None

    clip_weight, _ = lax.scan(add_shard, jnp.zeros((D, 3 * INNER), jnp.float32),
                              (placed.reshape(N_SEQ, R_DEV, D), proj_grad.reshape(N_SEQ, R_DEV, 3 * INNER)))
    fetched = jnp.take(placed_grad, jnp.minimum(target, ROWS - 1), axis=0)
    token_grad = jnp.where((clip_dest >= 0)[:, None], fetched, jnp.zeros_like(fetched))
    patch_grad = (token_grad[token_id].astype(jnp.float32) / counts[token_id][:, None]).astype(jnp.bfloat16)
    return attended, patch_grad, clip_weight


def reference(patches, segment, dest_shard, dest_slot, w_qkv, out_grad):
    def per_clip(running, inputs):
        attended, patch_grad, clip_weight = one_clip(w_qkv, *inputs)
        return running + clip_weight, (attended, patch_grad)

    weight_grad, (attended, patch_grad) = lax.scan(
        per_clip, jnp.zeros((D, 3 * INNER), jnp.float32), (patches, segment, dest_shard, dest_slot, out_grad))
    return attended, patch_grad, weight_grad
```

```python
import functools

import jax
import jax.numpy as jnp
from jax import lax
from jax.experimental import pallas as pl
from jax.experimental.pallas import tpu as pltpu
from jax.sharding import PartitionSpec as P

BF = jnp.bfloat16
F32 = jnp.float32
I32 = jnp.int32
MESH = pl.DeviceIdType.MESH

D = 1024
INNER = 512
R = 64
NSEQ = 32
CAP = 8
NMSG = NSEQ * CAP
QROWS = 512
QC = 256


def iota(shape, dim):
    return lax.broadcasted_iota(I32, shape, dim)


def onehot(cond):
    return jnp.where(cond, 1.0, 0.0).astype(BF)


def mm(a, b):
    return jnp.dot(a, b, preferred_element_type=F32)


def mm_nt(a, b):
    return lax.dot_general(a, b, (((1,), (1,)), ((), ())), preferred_element_type=F32)


def mm_tn(a, b):
    return lax.dot_general(a, b, (((0,), (0,)), ((), ())), preferred_element_type=F32)


def half_lanes(shape):
    return iota(shape, len(shape) - 1) < 64


def swap(v):
    return pltpu.roll(v, 64, v.ndim - 1)


def merge_low(a, b):
    return jnp.where(half_lanes(a.shape), a, swap(b))


def merge_high(a, b):
    return jnp.where(half_lanes(a.shape), swap(a), b)


def kernel(
    n_clip,
    patches,
    segment,
    dest_shard,
    dest_slot,
    w_hbm,
    out_grad,
    att_out,
    patch_out,
    weight_out,
    send,
    recv,
    back_send,
    back_recv,
    w_all,
    w_head,
    picker,
    placer_ref,
    count_inv,
    pq,
    kv,
    kvt,
    qpad,
    dopad,
    dot_ref,
    do_send,
    do_recv,
    weights,
    part_out,
    stat_max,
    stat_sum,
    fac_ref,
    gd_ref,
    att_send,
    att_recv,
    dkv_acc,
    dq_acc,
    rs_send,
    rs_recv,
    rs_send2,
    rs_recv2,
    g_send,
    g_recv,
    gnat,
    wblk,
    ws_send,
    ws_recv,
    ws_send2,
    ws_recv2,
    w15_send,
    w15_recv,
    w2_send,
    w2_recv,
    w_sem,
    a_s,
    a_r,
    b_s,
    b_r,
    p_s,
    p_r,
    k_s,
    k_r,
    do_s,
    do_r,
    at_s,
    at_r,
    rs_s,
    rs_r,
    g_s,
    g_r,
    ws_s,
    ws_r,
    w15_s,
    w15_r,
    w2_s,
    w2_r,
):
    i = lax.axis_index("seq")
    j = lax.axis_index("clip")
    x = i // 8
    y = (i // 2) % 4
    c = i % 2
    g = i % 8
    xp, xm, x2 = (x + 1) % 4, (x + 3) % 4, (x + 2) % 4
    yp, ym, y2 = (y + 1) % 4, (y + 3) % 4, (y + 2) % 4

    def seq_dev(dx, dy, dc):
        return {"seq": dx * 8 + dy * 2 + dc}

    def rcopy(src, dst, ss, rs, dev):
        return pltpu.make_async_remote_copy(
            src_ref=src, dst_ref=dst, send_sem=ss, recv_sem=rs, device_id=dev, device_id_type=MESH
        )

    barrier = pltpu.get_barrier_semaphore()

    @pl.loop(1, NSEQ)
    def _(k):
        pl.semaphore_signal(
            barrier, inc=1, device_id={"seq": (i + k) % NSEQ}, device_id_type=MESH
        )

    @pl.loop(1, n_clip)
    def _(k):
        pl.semaphore_signal(
            barrier, inc=1, device_id={"clip": (j + k) % n_clip}, device_id_type=MESH
        )

    w_copy = pltpu.make_async_copy(w_hbm, w_all, w_sem)
    w_copy.start()

    seg = segment[...]
    tgt = dest_shard[...]
    slot = dest_slot[...]
    hit = iota((192, 196), 0) == seg
    member = onehot(hit)
    counts = jnp.sum(jnp.where(hit, 1.0, 0.0), axis=1, keepdims=True)
    sums = mm(member, patches[0])
    tokens = (sums * (1.0 / jnp.maximum(counts, 1.0))).astype(BF)
    to_shard = iota((NSEQ, 192), 0) == tgt
    shard_hot = onehot(to_shard)
    earlier = onehot(iota((192, 192), 0) < iota((192, 192), 1))
    before = mm(shard_hot, earlier)
    rank = jnp.sum(jnp.where(to_shard, before, 0.0), axis=0, keepdims=True)
    position = jnp.where(tgt >= 0, tgt.astype(F32) * CAP + rank, -1.0)
    chooser = onehot(iota((NMSG, 192), 0).astype(F32) == position)
    slot_rows = jnp.where(
        iota((128, 192), 0).astype(F32) == rank, slot.astype(F32) + 1.0, 0.0
    ).astype(BF)
    slot_table = mm_nt(shard_hot, slot_rows).astype(BF)
    spread = onehot(iota((NMSG, NSEQ), 0) == iota((NMSG, NSEQ), 1) * CAP + 6)
    slot_cells = mm(spread, slot_table)
    rows = mm(chooser, tokens)
    send[:, :, 0:128] = (rows[:, 0:128] + slot_cells).reshape(NSEQ, CAP, 128).astype(BF)
    send[:, :, 128:] = rows[:, 128:].reshape(NSEQ, CAP, D - 128).astype(BF)

    pl.semaphore_wait(barrier, NSEQ - 1 + n_clip - 1)

    def token_copy(k, peer, lands):
        return rcopy(send.at[peer], recv.at[lands], a_s.at[k], a_r.at[k], {"seq": peer})

    @pl.loop(1, NSEQ)
    def _(k):
        token_copy(k, (i + k) % NSEQ, i).start()

    recv[i] = send[i]

    picker[...] = mm(chooser, member).astype(BF)
    per_patch = mm_tn(member, jnp.broadcast_to(counts, (192, 128)).astype(BF))
    count_inv[...] = 1.0 / per_patch
    for blk in range(4):
        pair = out_grad[0, :, blk * 128 : blk * 128 + 128].astype(F32)
        top, low = pair[0:32], pair[32:64]
        do_send[2 * blk] = merge_low(top, low).astype(BF)
        do_send[2 * blk + 1] = merge_high(top, low).astype(BF)
    w_copy.wait()
    lane0 = pl.multiple_of(y * 128, 128)
    w_q = w_all[:, pl.ds(lane0, 128)].astype(F32)
    w_k = w_all[:, pl.ds(pl.multiple_of(lane0 + 512, 128), 128)].astype(F32)
    w_v = w_all[:, pl.ds(pl.multiple_of(lane0 + 1024, 128), 128)].astype(F32)
    low_half = half_lanes((D, 128))
    first = c == 0
    k_low = jnp.where(first, w_k, swap(w_k))
    v_high = jnp.where(first, swap(w_v), w_v)
    q_low = jnp.where(first, w_q, swap(w_q))
    w_head[:, 0:128] = jnp.where(low_half, k_low, v_high).astype(BF)
    w_head[:, 128:256] = jnp.where(low_half, q_low, 0.0).astype(BF)

    @pl.loop(1, NSEQ)
    def _(k):
        src = (i + NSEQ - k) % NSEQ
        token_copy(k, src, src).wait_recv()

    came = recv[...].astype(F32).reshape(NMSG, D).astype(BF)
    col = iota((NMSG, NMSG), 1)
    from_row = onehot(iota((NMSG, NMSG), 0) == (col // CAP) * CAP + 6)
    slot_sq = mm_tn(came[:, 0:128], from_row)[0:8]
    slot_row = jnp.sum(
        jnp.where(iota((8, NMSG), 0) == iota((8, NMSG), 1) % CAP, slot_sq, 0.0)
        * jnp.where(iota((8, NMSG), 1) % CAP < 6, 1.0, 0.0),
        axis=0,
        keepdims=True,
    )
    placer = onehot((iota((R, NMSG), 0) + 1).astype(F32) == slot_row)
    placer_ref[...] = placer
    pq[g] = mm(placer, came).astype(BF)

    g_p, g_m, g_2 = yp * 2 + c, ym * 2 + c, y2 * 2 + c
    A, B = pl.ds(0, 32), pl.ds(32, 32)
    to_yp, to_ym, to_pal = seq_dev(x, yp, c), seq_dev(x, ym, c), seq_dev(x, y, 1 - c)

    def p_copy(n, s, half, dev):
        ref = pq.at[s] if half is None else pq.at[s, half]
        return rcopy(ref, ref, p_s.at[n], p_r.at[n], dev)

    p_copy(0, g, A, to_yp).start()
    p_copy(1, g, B, to_ym).start()
    p_copy(2, g, B, to_yp).start()
    p_copy(3, g, A, to_ym).start()
    p_copy(4, g, None, to_pal).start()
    p_copy(0, g_m, A, to_yp).wait_recv()
    p_copy(5, g_m, A, to_yp).start()
    p_copy(6, g_m, A, to_pal).start()
    p_copy(1, g_p, B, to_ym).wait_recv()
    p_copy(7, g_p, B, to_ym).start()
    p_copy(8, g_p, B, to_pal).start()
    p_copy(2, g_m, B, to_yp).wait_recv()
    p_copy(9, g_m, B, to_pal).start()
    p_copy(3, g_p, A, to_ym).wait_recv()
    p_copy(10, g_p, A, to_pal).start()
    p_copy(5, g_2, A, to_yp).wait_recv()
    p_copy(11, g_2, A, to_pal).start()
    p_copy(7, g_2, B, to_ym).wait_recv()
    p_copy(12, g_2, B, to_pal).start()
    h_p, h_m, h_2, h_g = yp * 2 + 1 - c, ym * 2 + 1 - c, y2 * 2 + 1 - c, y * 2 + 1 - c
    p_copy(4, h_g, None, to_pal).wait_recv()
    p_copy(6, h_m, A, to_pal).wait_recv()
    p_copy(8, h_p, B, to_pal).wait_recv()
    p_copy(9, h_m, B, to_pal).wait_recv()
    p_copy(10, h_p, A, to_pal).wait_recv()
    p_copy(11, h_2, A, to_pal).wait_recv()
    p_copy(12, h_2, B, to_pal).wait_recv()

    proj = mm(pq[...].reshape(QROWS, D), w_head[...]).astype(BF)
    kv[x] = proj[:, 0:128]
    qpad[...] = (proj[:, 128:256].astype(F32) * 0.125).astype(BF)

    KA, KB = pl.ds(0, 256), pl.ds(256, 256)
    to_xp, to_xm = seq_dev(xp, y, c), seq_dev(xm, y, c)

    def k_copy(n, s, half, dev):
        ref = kv.at[s, half]
        return rcopy(ref, ref, k_s.at[n], k_r.at[n], dev)

    k_copy(0, x, KA, to_xp).start()
    k_copy(1, x, KB, to_xm).start()
    k_copy(2, x, KB, to_xp).start()
    k_copy(3, x, KA, to_xm).start()

    def do_copy(k, peer, lands):
        return rcopy(
            do_send.at[peer], do_recv.at[lands], do_s.at[k], do_r.at[k], {"seq": x * 8 + peer}
        )

    @pl.loop(1, 8)
    def _(k):
        do_copy(k, (g + k) % 8, g).start()

    do_recv[g] = do_send[g]

    def forward(s, n):
        kvt[n] = kv[s].astype(F32).T.astype(BF)
        for q in range(QROWS // QC):
            qs = slice(q * QC, q * QC + QC)
            scores = mm_nt(kv[s], qpad[qs, :])
            top = jnp.max(scores, axis=0, keepdims=True)
            w = jnp.exp(scores - top)
            stat_max[n, :, qs] = top
            stat_sum[n, :, qs] = jnp.sum(w, axis=0, keepdims=True)
            weights[n, :, qs] = w
            part_out[n, :, qs] = mm(kvt[n], w.astype(BF))

    forward(x, 0)
    k_copy(0, xm, KA, to_xp).wait_recv()
    k_copy(4, xm, KA, to_xp).start()
    k_copy(1, xp, KB, to_xm).wait_recv()
    k_copy(5, xp, KB, to_xm).start()
    k_copy(2, xm, KB, to_xp).wait_recv()
    forward(xm, 1)
    k_copy(3, xp, KA, to_xm).wait_recv()
    forward(xp, 2)

    @pl.loop(1, 8)
    def _(k):
        src = (g + 8 - k) % 8
        do_copy(k, src, src).wait_recv()

    d_in = do_recv[...].astype(F32)
    high = iota((8, 32, 128), 2) >= 64
    d_rows = jnp.concatenate(
        [jnp.where(high, swap(d_in), 0.0), jnp.where(high, d_in, 0.0)], axis=1
    ).reshape(QROWS, 128)
    dopad[...] = d_rows.astype(BF)
    dot_ref[...] = d_rows.T

    k_copy(4, x2, KA, to_xp).wait_recv()
    k_copy(5, x2, KB, to_xm).wait_recv()
    forward(x2, 3)

    best = jnp.maximum(
        jnp.maximum(stat_max[0], stat_max[1]), jnp.maximum(stat_max[2], stat_max[3])
    )
    facs = [jnp.exp(stat_max[n] - best) for n in range(4)]
    total = sum(facs[n] * stat_sum[n] for n in range(4))
    att_t = sum(facs[n] * part_out[n] for n in range(4)) / total
    att_half = att_t.astype(BF).astype(F32)
    gd_ref[...] = jnp.sum(att_half[64:128] * dot_ref[64:128], axis=0, keepdims=True)
    for n in range(4):
        fac_ref[n] = facs[n] / total
    att3 = att_half.T.reshape(8, R, 128)
    att_send[...] = merge_high(att3[:, 0:32], att3[:, 32:64]).astype(BF)

    def at_copy(k, peer, lands):
        return rcopy(
            att_send.at[peer], att_recv.at[lands], at_s.at[k], at_r.at[k], {"seq": x * 8 + peer}
        )

    @pl.loop(1, 8)
    def _(k):
        at_copy(k, (g + k) % 8, g).start()

    att_recv[g] = att_send[g]

    dq_acc[...] = jnp.zeros((128, QROWS), F32)

    def backward(s, n):
        for q in range(QROWS // QC):
            qs = slice(q * QC, q * QC + QC)
            prob_grad = mm_nt(kv[s], dopad[qs, :])
            prob = weights[n, :, qs] * fac_ref[n, :, qs]
            score_grad = (prob * (prob_grad - gd_ref[:, qs])).astype(BF)
            upd = mm(score_grad, qpad[qs, :]) + mm(prob.astype(BF), dopad[qs, :])
            if q == 0:
                dkv_acc[...] = upd
            else:
                dkv_acc[...] += upd
            dq_acc[:, qs] += mm(kvt[n], score_grad)

    def rs_copy(src, dst, n, dev):
        return rcopy(src, dst, rs_s.at[n], rs_r.at[n], dev)

    backward(x2, 3)
    rs_send[0] = dkv_acc[0:256].astype(BF)
    rs_send[1] = dkv_acc[256:512].astype(BF)
    rs_copy(rs_send.at[0], rs_recv.at[0], 0, to_xp).start()
    rs_copy(rs_send.at[1], rs_recv.at[1], 1, to_xm).start()
    backward(xp, 2)
    rs_copy(rs_send.at[0], rs_recv.at[0], 0, to_xp).wait_recv()
    rs_send2[0, 0:256] = (dkv_acc[0:256] + rs_recv[0].astype(F32)).astype(BF)
    rs_send2[0, 256:512] = dkv_acc[256:512].astype(BF)
    rs_copy(rs_send2.at[0], rs_recv2.at[0], 2, to_xp).start()
    backward(xm, 1)
    rs_copy(rs_send.at[1], rs_recv.at[1], 1, to_xm).wait_recv()
    rs_send2[1, 0:256] = dkv_acc[0:256].astype(BF)
    rs_send2[1, 256:512] = (dkv_acc[256:512] + rs_recv[1].astype(F32)).astype(BF)
    rs_copy(rs_send2.at[1], rs_recv2.at[1], 3, to_xm).start()
    backward(x, 0)

    dq_rows = jnp.where(half_lanes((QROWS, 128)), dq_acc[...].T * 0.125, 0.0)
    dq3 = dq_rows.reshape(8, R, 128)
    g_send[:, 64:96] = merge_low(dq3[:, 0:32], dq3[:, 32:64]).astype(BF)
    rs_copy(rs_send2.at[0], rs_recv2.at[0], 2, to_xp).wait_recv()
    rs_copy(rs_send2.at[1], rs_recv2.at[1], 3, to_xm).wait_recv()
    dkv = (dkv_acc[...] + rs_recv2[0].astype(F32) + rs_recv2[1].astype(F32)).astype(BF)
    g_send[:, 0:64] = dkv.reshape(8, R, 128)

    def g_copy(k, peer, lands):
        return rcopy(
            g_send.at[peer], g_recv.at[lands], g_s.at[k], g_r.at[k], {"seq": x * 8 + peer}
        )

    @pl.loop(1, 8)
    def _(k):
        g_copy(k, (g + k) % 8, g).start()

    g_recv[g] = g_send[g]

    grads = jnp.concatenate([dkv, dq_rows.astype(BF)], axis=1)
    w_part = mm_tn(grads, pq[...].reshape(QROWS, D))
    for q in range(4):
        wblk[q] = w_part[0:192, q * 256 : q * 256 + 256]

    def ws_copy(src, dst, n, dev):
        return rcopy(src, dst, ws_s.at[n], ws_r.at[n], dev)

    ws_send[0] = wblk[x2, 0:96].astype(BF)
    ws_send[1] = wblk[x2, 96:192].astype(BF)
    ws_copy(ws_send.at[0], ws_recv.at[0], 0, to_xp).start()
    ws_copy(ws_send.at[1], ws_recv.at[1], 1, to_xm).start()

    @pl.loop(1, 8)
    def _(k):
        src = (g + 8 - k) % 8
        at_copy(k, src, src).wait_recv()

    for blk in range(4):
        a0 = att_recv[2 * blk].astype(F32)
        a1 = att_recv[2 * blk + 1].astype(F32)
        lanes = slice(blk * 128, blk * 128 + 128)
        att_out[0, 0:32, lanes] = merge_low(a0, a1).astype(BF)
        att_out[0, 32:64, lanes] = merge_high(a0, a1).astype(BF)

    @pl.loop(1, 8)
    def _(k):
        src = (g + 8 - k) % 8
        g_copy(k, src, src).wait_recv()

    for blk in range(4):
        r0 = g_recv[2 * blk].astype(F32)
        r1 = g_recv[2 * blk + 1].astype(F32)
        q_at, k_at, v_at = blk * 128, blk * 128 + 512, blk * 128 + 1024
        gnat[0:32, q_at : q_at + 128] = merge_low(r0[64:96], r1[64:96]).astype(BF)
        gnat[32:64, q_at : q_at + 128] = merge_high(r0[64:96], r1[64:96]).astype(BF)
        gnat[:, k_at : k_at + 128] = merge_low(r0[0:64], r1[0:64]).astype(BF)
        gnat[:, v_at : v_at + 128] = merge_high(r0[0:64], r1[0:64]).astype(BF)
    placed_grad = mm_nt(gnat[...], w_all[...]).astype(BF)
    back = mm_tn(placer_ref[...], placed_grad)
    back_send[...] = back.reshape(NSEQ, CAP, D).astype(BF)

    def back_copy(k, peer, lands):
        return rcopy(
            back_send.at[peer], back_recv.at[lands], b_s.at[k], b_r.at[k], {"seq": peer}
        )

    @pl.loop(1, NSEQ)
    def _(k):
        back_copy(k, (i + k) % NSEQ, i).start()

    back_recv[i] = back_send[i]

    ws_copy(ws_send.at[0], ws_recv.at[0], 0, to_xp).wait_recv()
    ws_send2[0, 0:96] = (wblk[xp, 0:96] + ws_recv[0].astype(F32)).astype(BF)
    ws_send2[0, 96:192] = wblk[xp, 96:192].astype(BF)
    ws_copy(ws_send2.at[0], ws_recv2.at[0], 2, to_xp).start()
    ws_copy(ws_send.at[1], ws_recv.at[1], 1, to_xm).wait_recv()
    ws_send2[1, 0:96] = wblk[xm, 0:96].astype(BF)
    ws_send2[1, 96:192] = (wblk[xm, 96:192] + ws_recv[1].astype(F32)).astype(BF)
    ws_copy(ws_send2.at[1], ws_recv2.at[1], 3, to_xm).start()
    ws_copy(ws_send2.at[0], ws_recv2.at[0], 2, to_xp).wait_recv()
    ws_copy(ws_send2.at[1], ws_recv2.at[1], 3, to_xm).wait_recv()
    w_sum = wblk[x] + ws_recv2[0].astype(F32) + ws_recv2[1].astype(F32)
    w_kv = w_sum[0:128].T.reshape(8, 32, 128)
    w_qq = jnp.concatenate([w_sum[128:192], jnp.zeros((64, 256), F32)], axis=0)
    w_qq = w_qq.T.reshape(8, 32, 128)
    w15_send[:, 0:32] = w_kv.astype(BF)
    w15_send[:, 32:48] = merge_low(w_qq[:, 0:16], w_qq[:, 16:32]).astype(BF)

    def w15_copy(k, peer, lands):
        return rcopy(
            w15_send.at[peer],
            w15_recv.at[lands],
            w15_s.at[k],
            w15_r.at[k],
            {"seq": x * 8 + peer},
        )

    @pl.loop(1, 8)
    def _(k):
        w15_copy(k, (g + k) % 8, g).start()

    w15_recv[g] = w15_send[g]

    @pl.loop(1, 8)
    def _(k):
        src = (g + 8 - k) % 8
        w15_copy(k, src, src).wait_recv()

    q_blocks, k_blocks, v_blocks = [], [], []
    for blk in range(4):
        r0 = w15_recv[2 * blk].astype(F32)
        r1 = w15_recv[2 * blk + 1].astype(F32)
        q_blocks.append(
            jnp.concatenate(
                [merge_low(r0[32:48], r1[32:48]), merge_high(r0[32:48], r1[32:48])], axis=0
            )
        )
        k_blocks.append(merge_low(r0[0:32], r1[0:32]))
        v_blocks.append(merge_high(r0[0:32], r1[0:32]))
    blocks = q_blocks + k_blocks + v_blocks
    width = 3 * INNER // n_clip
    for n in range(n_clip):
        b, off = divmod(width * n, 128)
        if off == 0:
            piece = blocks[b]
        else:
            turn = 128 - off
            piece = pltpu.roll(blocks[b], turn, 1)
            if off + width > 128:
                piece = jnp.where(
                    iota((32, 128), 1) < turn, piece, pltpu.roll(blocks[b + 1], turn, 1)
                )
        w2_send[n] = piece.astype(BF)

    def w2_copy(k, peer, lands):
        return rcopy(
            w2_send.at[peer], w2_recv.at[lands], w2_s.at[k], w2_r.at[k], {"clip": peer}
        )

    @pl.loop(1, n_clip)
    def _(k):
        w2_copy(k, (j + k) % n_clip, j).start()

    w2_recv[j] = w2_send[j]

    @pl.loop(1, NSEQ)
    def _(k):
        src = (i + NSEQ - k) % NSEQ
        back_copy(k, src, src).wait_recv()

    returned = back_recv[...].astype(F32).reshape(NMSG, D).astype(BF)
    patch_rows = mm_tn(picker[...], returned)
    patch_out[0] = (patch_rows * count_inv[:, 0:1]).astype(BF)

    @pl.loop(1, n_clip)
    def _(k):
        src = (j + n_clip - k) % n_clip
        w2_copy(k, src, src).wait_recv()

    weight_out[...] = jnp.sum(w2_recv[...].astype(F32), axis=0)[:, 0:width]

    @pl.loop(1, NSEQ)
    def _(k):
        token_copy(k, (i + k) % NSEQ, i).wait_send()
        back_copy(k, (i + k) % NSEQ, i).wait_send()

    @pl.loop(1, 8)
    def _(k):
        peer = (g + k) % 8
        do_copy(k, peer, g).wait_send()
        at_copy(k, peer, g).wait_send()
        g_copy(k, peer, g).wait_send()
        w15_copy(k, peer, g).wait_send()

    @pl.loop(1, n_clip)
    def _(k):
        w2_copy(k, (j + k) % n_clip, j).wait_send()

    for n, s, half, dev in (
        (0, g, A, to_yp),
        (1, g, B, to_ym),
        (2, g, B, to_yp),
        (3, g, A, to_ym),
        (4, g, None, to_pal),
        (5, g_m, A, to_yp),
        (6, g_m, A, to_pal),
        (7, g_p, B, to_ym),
        (8, g_p, B, to_pal),
        (9, g_m, B, to_pal),
        (10, g_p, A, to_pal),
        (11, g_2, A, to_pal),
        (12, g_2, B, to_pal),
    ):
        p_copy(n, s, half, dev).wait_send()
    for n, s, half, dev in (
        (0, x, KA, to_xp),
        (1, x, KB, to_xm),
        (2, x, KB, to_xp),
        (3, x, KA, to_xm),
        (4, xm, KA, to_xp),
        (5, xp, KB, to_xm),
    ):
        k_copy(n, s, half, dev).wait_send()
    for n, dev in ((0, to_xp), (1, to_xm)):
        rs_copy(rs_send.at[n], rs_recv.at[n], n, dev).wait_send()
        rs_copy(rs_send2.at[n], rs_recv2.at[n], n + 2, dev).wait_send()
        ws_copy(ws_send.at[n], ws_recv.at[n], n, dev).wait_send()
        ws_copy(ws_send2.at[n], ws_recv2.at[n], n + 2, dev).wait_send()


def local(patches, segment, dest_shard, dest_slot, w_qkv, out_grad):
    n_clip = lax.axis_size("clip")
    v = pltpu.VMEM
    dma = pltpu.SemaphoreType.DMA
    vmem = pl.BlockSpec(memory_space=pltpu.VMEM)
    scratch = [
        v((NSEQ, CAP, D), BF),
        v((NSEQ, CAP, D), BF),
        v((NSEQ, CAP, D), BF),
        v((NSEQ, CAP, D), BF),
        v((D, 3 * INNER), BF),
        v((D, 256), BF),
        v((NMSG, 196), BF),
        v((R, NMSG), BF),
        v((196, 128), F32),
        v((8, R, D), BF),
        v((4, QROWS, 128), BF),
        v((4, 128, QROWS), BF),
        v((QROWS, 128), BF),
        v((QROWS, 128), BF),
        v((128, QROWS), F32),
        v((8, 32, 128), BF),
        v((8, 32, 128), BF),
        v((4, QROWS, QROWS), F32),
        v((4, 128, QROWS), F32),
        v((4, 1, QROWS), F32),
        v((4, 1, QROWS), F32),
        v((4, 1, QROWS), F32),
        v((1, QROWS), F32),
        v((8, 32, 128), BF),
        v((8, 32, 128), BF),
        v((QROWS, 128), F32),
        v((128, QROWS), F32),
        v((2, 256, 128), BF),
        v((2, 256, 128), BF),
        v((2, QROWS, 128), BF),
        v((2, QROWS, 128), BF),
        v((8, 96, 128), BF),
        v((8, 96, 128), BF),
        v((R, 3 * INNER), BF),
        v((4, 192, 256), F32),
        v((2, 96, 256), BF),
        v((2, 96, 256), BF),
        v((2, 192, 256), BF),
        v((2, 192, 256), BF),
        v((8, 48, 128), BF),
        v((8, 48, 128), BF),
        v((n_clip, 32, 128), BF),
        v((n_clip, 32, 128), BF),
        dma,
        dma((NSEQ,)),
        dma((NSEQ,)),
        dma((NSEQ,)),
        dma((NSEQ,)),
        dma((13,)),
        dma((13,)),
        dma((6,)),
        dma((6,)),
        dma((8,)),
        dma((8,)),
        dma((8,)),
        dma((8,)),
        dma((4,)),
        dma((4,)),
        dma((8,)),
        dma((8,)),
        dma((4,)),
        dma((4,)),
        dma((8,)),
        dma((8,)),
        dma((n_clip,)),
        dma((n_clip,)),
    ]
    return pl.pallas_call(
        functools.partial(kernel, n_clip),
        out_shape=(
            jax.ShapeDtypeStruct((1, R, INNER), BF),
            jax.ShapeDtypeStruct((1, 196, D), BF),
            jax.ShapeDtypeStruct((32, 3 * INNER // n_clip), F32),
        ),
        in_specs=[vmem, vmem, vmem, vmem, pl.BlockSpec(memory_space=pl.ANY), vmem],
        out_specs=(vmem, vmem, vmem),
        scratch_shapes=scratch,
        compiler_params=pltpu.CompilerParams(
            collective_id=0, has_side_effects=True, vmem_limit_bytes=56 * 1024 * 1024
        ),
        name="rebalance_attention",
    )(patches, segment, dest_shard, dest_slot, w_qkv, out_grad)


def solution(mesh):
    return jax.shard_map(
        local,
        mesh=mesh,
        in_specs=(
            P("clip", "seq", None),
            P("clip", "seq"),
            P("clip", "seq"),
            P("clip", "seq"),
            P(),
            P("clip", "seq", None),
        ),
        out_specs=(P("clip", "seq", None), P("clip", "seq", None), P("seq", "clip")),
        check_vma=False,
    )
```

```python
import functools

import jax
import jax.numpy as jnp
from jax import lax
from jax.experimental import pallas as pl
from jax.experimental.pallas import tpu as pltpu
from jax.sharding import PartitionSpec as P

BF = jnp.bfloat16
F32 = jnp.float32
I32 = jnp.int32
MESH = pl.DeviceIdType.MESH

D = 1024
INNER = 512
R = 64
NSEQ = 32
CAP = 8
NMSG = NSEQ * CAP
QROWS = 512
QC = 256
TOP = 6
EXT = D + 128
HALF = D // 2


def iota(shape, dim):
    return lax.broadcasted_iota(I32, shape, dim)


def onehot(cond):
    return jnp.where(cond, 1.0, 0.0).astype(BF)


def mm(a, b):
    return jnp.dot(a, b, preferred_element_type=F32)


def mm_nt(a, b):
    return lax.dot_general(a, b, (((1,), (1,)), ((), ())), preferred_element_type=F32)


def mm_tn(a, b):
    return lax.dot_general(a, b, (((0,), (0,)), ((), ())), preferred_element_type=F32)


def half_lanes(shape):
    return iota(shape, len(shape) - 1) < 64


def swap(v):
    return pltpu.roll(v, 64, v.ndim - 1)


def merge_low(a, b):
    return jnp.where(half_lanes(a.shape), a, swap(b))


def merge_high(a, b):
    return jnp.where(half_lanes(a.shape), swap(a), b)


def kernel(
    n_clip,
    patches_hbm,
    segment_hbm,
    shard_hbm,
    slot_hbm,
    w_hbm,
    grad_hbm,
    att_hbm,
    patch_hbm,
    weight_hbm,
    patches,
    segment,
    dest_shard,
    dest_slot,
    out_grad,
    att_out,
    patch_out,
    weight_out,
    send,
    recv,
    back_send,
    back_recv,
    w_all,
    picker,
    placer_ref,
    count_inv,
    pq,
    kv,
    kvt,
    qpad,
    dopad,
    dot_ref,
    kv_send,
    qd_send,
    qd_recv,
    weights,
    part_out,
    stat_max,
    stat_sum,
    fac_ref,
    gd_ref,
    att_send,
    att_recv,
    dkv_acc,
    dq_acc,
    rs_send,
    rs_recv,
    rs_send2,
    rs_recv2,
    g_send,
    g_recv,
    gnat,
    wblk,
    ws_send,
    ws_recv,
    ws_send2,
    ws_recv2,
    w15_send,
    w15_recv,
    w2_send,
    w2_recv,
    in_sem,
    out_sem,
    a_s,
    a_r,
    b_s,
    b_r,
    p_s,
    p_r,
    k_s,
    k_r,
    kx_s,
    kx_r,
    qd_s,
    qd_r,
    at_s,
    at_r,
    rs_s,
    rs_r,
    g_s,
    g_r,
    ws_s,
    ws_r,
    w15_s,
    w15_r,
    w2_s,
    w2_r,
):
    i = lax.axis_index("seq")
    j = lax.axis_index("clip")
    x = i // 8
    y = (i // 2) % 4
    c = i % 2
    g = i % 8
    xp, xm, x2 = (x + 1) % 4, (x + 3) % 4, (x + 2) % 4
    yp, ym, y2 = (y + 1) % 4, (y + 3) % 4, (y + 2) % 4

    def seq_dev(dx, dy, dc):
        return {"seq": dx * 8 + dy * 2 + dc}

    def rcopy(src, dst, ss, rs, dev):
        return pltpu.make_async_remote_copy(
            src_ref=src, dst_ref=dst, send_sem=ss, recv_sem=rs, device_id=dev, device_id_type=MESH
        )

    loads = [
        pltpu.make_async_copy(a, b, in_sem.at[n])
        for n, (a, b) in enumerate(
            (
                (segment_hbm, segment),
                (shard_hbm, dest_shard),
                (slot_hbm, dest_slot),
                (patches_hbm.at[0], patches),
                (w_hbm, w_all),
                (grad_hbm.at[0], out_grad),
            )
        )
    ]
    for load in loads:
        load.start()

    barrier = pltpu.get_barrier_semaphore()

    @pl.loop(1, NSEQ)
    def _(k):
        pl.semaphore_signal(
            barrier, inc=1, device_id={"seq": (i + k) % NSEQ}, device_id_type=MESH
        )

    @pl.loop(1, n_clip)
    def _(k):
        pl.semaphore_signal(
            barrier, inc=1, device_id={"clip": (j + k) % n_clip}, device_id_type=MESH
        )

    for load in loads[0:4]:
        load.wait()
    seg = segment[...]
    tgt = dest_shard[...]
    slot = dest_slot[...]
    hit = iota((192, 196), 0) == seg
    member = onehot(hit)
    counts = jnp.sum(jnp.where(hit, 1.0, 0.0), axis=1, keepdims=True)
    sums = mm(member, patches[...])
    tokens = (sums * (1.0 / jnp.maximum(counts, 1.0))).astype(BF)
    to_shard = iota((NSEQ, 192), 0) == tgt
    shard_hot = onehot(to_shard)
    earlier = onehot(iota((192, 192), 0) < iota((192, 192), 1))
    before = mm(shard_hot, earlier)
    rank = jnp.sum(jnp.where(to_shard, before, 0.0), axis=0, keepdims=True)
    position = jnp.where(tgt >= 0, tgt.astype(F32) * CAP + rank, -1.0)
    chooser = onehot(iota((NMSG, 192), 0).astype(F32) == position)
    same = onehot(iota((192, 192), 0) == iota((192, 192), 1))
    slot_cells = jnp.broadcast_to(slot.astype(F32) + 1.0, (128, 192)).astype(BF)
    slot_column = mm_nt(same, slot_cells).astype(BF)
    rows = mm(chooser, jnp.concatenate([tokens, slot_column], axis=1))
    send[...] = rows.reshape(NSEQ, CAP, EXT).astype(BF)

    pl.semaphore_wait(barrier, NSEQ - 1 + n_clip - 1)

    def token_copy(k, peer, lands):
        return rcopy(
            send.at[peer, pl.ds(0, TOP)],
            recv.at[lands, pl.ds(0, TOP)],
            a_s.at[k],
            a_r.at[k],
            {"seq": peer},
        )

    @pl.loop(1, NSEQ)
    def _(k):
        token_copy(k, (i + k) % NSEQ, i).start()

    recv[i] = send[i]

    picker[...] = mm(chooser, member).astype(BF)
    per_patch = mm_tn(member, jnp.broadcast_to(counts, (192, 128)).astype(BF))
    count_inv[...] = 1.0 / per_patch
    loads[5].wait()
    for blk in range(4):
        pair = out_grad[:, blk * 128 : blk * 128 + 128].astype(F32)
        top, low = pair[0:32], pair[32:64]
        qd_send[2 * blk, 32:64] = merge_low(top, low).astype(BF)
        qd_send[2 * blk + 1, 32:64] = merge_high(top, low).astype(BF)
    loads[4].wait()

    @pl.loop(1, NSEQ)
    def _(k):
        src = (i + NSEQ - k) % NSEQ
        token_copy(k, src, src).wait_recv()

    full = iota((NSEQ, CAP, EXT), 1) < TOP
    came = jnp.where(full, recv[...].astype(F32), 0.0).reshape(NMSG, EXT).astype(BF)
    one_lane = onehot(iota((8, 128), 1) == 0)
    slot_row = mm_nt(one_lane, came[:, D:])[0:1]
    placer = onehot((iota((R, NMSG), 0) + 1).astype(F32) == slot_row)
    placer_ref[...] = placer
    placed = mm(placer, came[:, 0:D]).astype(BF)
    pq[g] = placed

    def kx_copy(k, peer, lands):
        return rcopy(
            kv_send.at[peer],
            kv.at[x, pl.ds(pl.multiple_of(lands * R, R), R)],
            kx_s.at[k],
            kx_r.at[k],
            {"seq": x * 8 + peer},
        )

    def qd_copy(k, peer, lands):
        return rcopy(
            qd_send.at[peer], qd_recv.at[lands], qd_s.at[k], qd_r.at[k], {"seq": x * 8 + peer}
        )

    def half_up(v):
        return v.astype(BF).astype(F32)

    proj = half_up(mm(placed, w_all[:, INNER:]))
    for blk in range(4):
        k_blk = proj[:, blk * 128 : blk * 128 + 128]
        v_blk = proj[:, INNER + blk * 128 : INNER + blk * 128 + 128]
        kv_send[2 * blk] = merge_low(k_blk, v_blk).astype(BF)
        kv_send[2 * blk + 1] = merge_high(k_blk, v_blk).astype(BF)

    @pl.loop(1, 8)
    def _(k):
        kx_copy(k, (g + k) % 8, g).start()

    kv[x, pl.ds(pl.multiple_of(g * R, R), R)] = kv_send[g]
    proj_q = half_up(mm(placed, w_all[:, 0:INNER])) * 0.125
    for blk in range(4):
        q_blk = proj_q[:, blk * 128 : blk * 128 + 128]
        qd_send[2 * blk, 0:32] = merge_low(q_blk[0:32], q_blk[32:64]).astype(BF)
        qd_send[2 * blk + 1, 0:32] = merge_high(q_blk[0:32], q_blk[32:64]).astype(BF)

    @pl.loop(1, 8)
    def _(k):
        qd_copy(k, (g + k) % 8, g).start()

    qd_recv[g] = qd_send[g]

    g_p, g_m, g_2 = yp * 2 + c, ym * 2 + c, y2 * 2 + c
    A, B = pl.ds(0, 32), pl.ds(32, 32)
    to_yp, to_ym, to_pal = seq_dev(x, yp, c), seq_dev(x, ym, c), seq_dev(x, y, 1 - c)

    def p_copy(n, s, half, dev):
        ref = pq.at[s] if half is None else pq.at[s, half]
        return rcopy(ref, ref, p_s.at[n], p_r.at[n], dev)

    h_p, h_m, h_2, h_g = yp * 2 + 1 - c, ym * 2 + 1 - c, y2 * 2 + 1 - c, y * 2 + 1 - c

    def gather_first():
        p_copy(0, g, A, to_yp).start()
        p_copy(1, g, B, to_ym).start()
        p_copy(2, g, B, to_yp).start()
        p_copy(3, g, A, to_ym).start()
        p_copy(4, g, None, to_pal).start()

    def gather_second():
        p_copy(0, g_m, A, to_yp).wait_recv()
        p_copy(5, g_m, A, to_yp).start()
        p_copy(6, g_m, A, to_pal).start()
        p_copy(1, g_p, B, to_ym).wait_recv()
        p_copy(7, g_p, B, to_ym).start()
        p_copy(8, g_p, B, to_pal).start()
        p_copy(2, g_m, B, to_yp).wait_recv()
        p_copy(9, g_m, B, to_pal).start()
        p_copy(3, g_p, A, to_ym).wait_recv()
        p_copy(10, g_p, A, to_pal).start()

    def gather_third():
        p_copy(5, g_2, A, to_yp).wait_recv()
        p_copy(11, g_2, A, to_pal).start()
        p_copy(7, g_2, B, to_ym).wait_recv()
        p_copy(12, g_2, B, to_pal).start()

    def gather_last():
        p_copy(4, h_g, None, to_pal).wait_recv()
        p_copy(6, h_m, A, to_pal).wait_recv()
        p_copy(8, h_p, B, to_pal).wait_recv()
        p_copy(9, h_m, B, to_pal).wait_recv()
        p_copy(10, h_p, A, to_pal).wait_recv()
        p_copy(11, h_2, A, to_pal).wait_recv()
        p_copy(12, h_2, B, to_pal).wait_recv()

    @pl.loop(1, 8)
    def _(k):
        src = (g + 8 - k) % 8
        kx_copy(k, src, src).wait_recv()

    KA, KB = pl.ds(0, 256), pl.ds(256, 256)
    to_xp, to_xm = seq_dev(xp, y, c), seq_dev(xm, y, c)

    def k_copy(n, s, half, dev):
        ref = kv.at[s, half]
        return rcopy(ref, ref, k_s.at[n], k_r.at[n], dev)

    k_copy(0, x, KA, to_xp).start()
    k_copy(1, x, KB, to_xm).start()
    k_copy(2, x, KB, to_xp).start()
    k_copy(3, x, KA, to_xm).start()

    @pl.loop(1, 8)
    def _(k):
        src = (g + 8 - k) % 8
        qd_copy(k, src, src).wait_recv()

    gather_first()
    qd_in = qd_recv[...].astype(F32)
    q_in, d_in = qd_in[:, 0:32], qd_in[:, 32:64]
    low = half_lanes((8, 32, 128))
    q_rows = jnp.concatenate([jnp.where(low, q_in, 0.0), jnp.where(low, swap(q_in), 0.0)], axis=1)
    qpad[...] = q_rows.reshape(QROWS, 128).astype(BF)

    def forward(s, n):
        kvt[n] = kv[s].astype(F32).T.astype(BF)
        for q in range(QROWS // QC):
            qs = slice(q * QC, q * QC + QC)
            scores = mm_nt(kv[s], qpad[qs, :])
            top = jnp.max(scores, axis=0, keepdims=True)
            w = jnp.exp(scores - top)
            stat_max[n, :, qs] = top
            stat_sum[n, :, qs] = jnp.sum(w, axis=0, keepdims=True)
            weights[n, :, qs] = w
            part_out[n, :, qs] = mm(kvt[n], w.astype(BF))

    forward(x, 0)
    d_rows = jnp.concatenate(
        [jnp.where(low, 0.0, swap(d_in)), jnp.where(low, 0.0, d_in)], axis=1
    ).reshape(QROWS, 128)
    dopad[...] = d_rows.astype(BF)
    dot_ref[...] = d_rows.T

    k_copy(0, xm, KA, to_xp).wait_recv()
    k_copy(4, xm, KA, to_xp).start()
    k_copy(1, xp, KB, to_xm).wait_recv()
    k_copy(5, xp, KB, to_xm).start()
    k_copy(2, xm, KB, to_xp).wait_recv()
    forward(xm, 1)
    k_copy(3, xp, KA, to_xm).wait_recv()
    forward(xp, 2)

    k_copy(4, x2, KA, to_xp).wait_recv()
    k_copy(5, x2, KB, to_xm).wait_recv()
    forward(x2, 3)

    best = jnp.maximum(
        jnp.maximum(stat_max[0], stat_max[1]), jnp.maximum(stat_max[2], stat_max[3])
    )
    facs = [jnp.exp(stat_max[n] - best) for n in range(4)]
    total = sum(facs[n] * stat_sum[n] for n in range(4))
    att_t = sum(facs[n] * part_out[n] for n in range(4)) / total
    att_half = att_t.astype(BF).astype(F32)
    gd_ref[...] = jnp.sum(att_half[64:128] * dot_ref[64:128], axis=0, keepdims=True)
    for n in range(4):
        fac_ref[n] = facs[n] / total
    att3 = att_half.T.reshape(8, R, 128)
    att_send[...] = merge_high(att3[:, 0:32], att3[:, 32:64]).astype(BF)

    def at_copy(k, peer, lands):
        return rcopy(
            att_send.at[peer], att_recv.at[lands], at_s.at[k], at_r.at[k], {"seq": x * 8 + peer}
        )

    @pl.loop(1, 8)
    def _(k):
        at_copy(k, (g + k) % 8, g).start()

    att_recv[g] = att_send[g]

    gather_second()
    dq_acc[...] = jnp.zeros((128, QROWS), F32)

    def backward(s, n):
        for q in range(QROWS // QC):
            qs = slice(q * QC, q * QC + QC)
            prob_grad = mm_nt(kv[s], dopad[qs, :])
            prob = weights[n, :, qs] * fac_ref[n, :, qs]
            score_grad = (prob * (prob_grad - gd_ref[:, qs])).astype(BF)
            upd = mm(score_grad, qpad[qs, :]) + mm(prob.astype(BF), dopad[qs, :])
            if q == 0:
                dkv_acc[...] = upd
            else:
                dkv_acc[...] += upd
            dq_acc[:, qs] += mm(kvt[n], score_grad)

    def rs_copy(src, dst, n, dev):
        return rcopy(src, dst, rs_s.at[n], rs_r.at[n], dev)

    backward(x2, 3)
    rs_send[0] = dkv_acc[0:256].astype(BF)
    rs_send[1] = dkv_acc[256:512].astype(BF)
    rs_copy(rs_send.at[0], rs_recv.at[0], 0, to_xp).start()
    rs_copy(rs_send.at[1], rs_recv.at[1], 1, to_xm).start()
    backward(xp, 2)
    rs_copy(rs_send.at[0], rs_recv.at[0], 0, to_xp).wait_recv()
    rs_send2[0, 0:256] = (dkv_acc[0:256] + rs_recv[0].astype(F32)).astype(BF)
    rs_send2[0, 256:512] = dkv_acc[256:512].astype(BF)
    rs_copy(rs_send2.at[0], rs_recv2.at[0], 2, to_xp).start()
    backward(xm, 1)
    rs_copy(rs_send.at[1], rs_recv.at[1], 1, to_xm).wait_recv()
    rs_send2[1, 0:256] = dkv_acc[0:256].astype(BF)
    rs_send2[1, 256:512] = (dkv_acc[256:512] + rs_recv[1].astype(F32)).astype(BF)
    rs_copy(rs_send2.at[1], rs_recv2.at[1], 3, to_xm).start()
    backward(x, 0)

    gather_third()
    dq_rows = jnp.where(half_lanes((QROWS, 128)), dq_acc[...].T * 0.125, 0.0)
    dq3 = dq_rows.reshape(8, R, 128)
    g_send[:, 64:96] = merge_low(dq3[:, 0:32], dq3[:, 32:64]).astype(BF)
    rs_copy(rs_send2.at[0], rs_recv2.at[0], 2, to_xp).wait_recv()
    rs_copy(rs_send2.at[1], rs_recv2.at[1], 3, to_xm).wait_recv()
    dkv = (dkv_acc[...] + rs_recv2[0].astype(F32) + rs_recv2[1].astype(F32)).astype(BF)
    g_send[:, 0:64] = dkv.reshape(8, R, 128)

    def g_copy(k, peer, lands):
        return rcopy(
            g_send.at[peer], g_recv.at[lands], g_s.at[k], g_r.at[k], {"seq": x * 8 + peer}
        )

    @pl.loop(1, 8)
    def _(k):
        g_copy(k, (g + k) % 8, g).start()

    g_recv[g] = g_send[g]

    gather_last()
    grads = jnp.concatenate([dkv, dq_rows.astype(BF)], axis=1)
    w_part = mm_tn(grads, pq[...].reshape(QROWS, D))
    for q in range(4):
        wblk[q] = w_part[0:192, q * 256 : q * 256 + 256]

    def ws_copy(src, dst, n, dev):
        return rcopy(src, dst, ws_s.at[n], ws_r.at[n], dev)

    ws_send[0] = wblk[x2, 0:96].astype(BF)
    ws_send[1] = wblk[x2, 96:192].astype(BF)
    ws_copy(ws_send.at[0], ws_recv.at[0], 0, to_xp).start()
    ws_copy(ws_send.at[1], ws_recv.at[1], 1, to_xm).start()

    @pl.loop(1, 8)
    def _(k):
        src = (g + 8 - k) % 8
        at_copy(k, src, src).wait_recv()

    stores = [
        pltpu.make_async_copy(a, b, out_sem.at[n])
        for n, (a, b) in enumerate(
            ((att_out, att_hbm.at[0]), (patch_out, patch_hbm.at[0]), (weight_out, weight_hbm))
        )
    ]
    for blk in range(4):
        a0 = att_recv[2 * blk].astype(F32)
        a1 = att_recv[2 * blk + 1].astype(F32)
        lanes = slice(blk * 128, blk * 128 + 128)
        att_out[0:32, lanes] = merge_low(a0, a1).astype(BF)
        att_out[32:64, lanes] = merge_high(a0, a1).astype(BF)
    stores[0].start()

    ws_copy(ws_send.at[0], ws_recv.at[0], 0, to_xp).wait_recv()
    ws_send2[0, 0:96] = (wblk[xp, 0:96] + ws_recv[0].astype(F32)).astype(BF)
    ws_send2[0, 96:192] = wblk[xp, 96:192].astype(BF)
    ws_copy(ws_send2.at[0], ws_recv2.at[0], 2, to_xp).start()
    ws_copy(ws_send.at[1], ws_recv.at[1], 1, to_xm).wait_recv()
    ws_send2[1, 0:96] = wblk[xm, 0:96].astype(BF)
    ws_send2[1, 96:192] = (wblk[xm, 96:192] + ws_recv[1].astype(F32)).astype(BF)
    ws_copy(ws_send2.at[1], ws_recv2.at[1], 3, to_xm).start()

    @pl.loop(1, 8)
    def _(k):
        src = (g + 8 - k) % 8
        g_copy(k, src, src).wait_recv()

    for blk in range(4):
        r0 = g_recv[2 * blk].astype(F32)
        r1 = g_recv[2 * blk + 1].astype(F32)
        q_at, k_at, v_at = blk * 128, blk * 128 + 512, blk * 128 + 1024
        gnat[0:32, q_at : q_at + 128] = merge_low(r0[64:96], r1[64:96]).astype(BF)
        gnat[32:64, q_at : q_at + 128] = merge_high(r0[64:96], r1[64:96]).astype(BF)
        gnat[:, k_at : k_at + 128] = merge_low(r0[0:64], r1[0:64]).astype(BF)
        gnat[:, v_at : v_at + 128] = merge_high(r0[0:64], r1[0:64]).astype(BF)
    def back_copy(h, k, peer, lands):
        return rcopy(
            back_send.at[h, peer, pl.ds(0, TOP)],
            back_recv.at[h, lands, pl.ds(0, TOP)],
            b_s.at[h, k],
            b_r.at[h, k],
            {"seq": peer},
        )

    def send_back(h):
        grad = mm_nt(gnat[...], w_all[h * HALF : h * HALF + HALF, :]).astype(BF)
        back = mm_tn(placer_ref[...], grad)
        back_send[h] = back.reshape(NSEQ, CAP, HALF).astype(BF)

        @pl.loop(1, NSEQ)
        def _(k):
            back_copy(h, k, (i + k) % NSEQ, i).start()

        back_recv[h, i] = back_send[h, i]

    send_back(0)

    ws_copy(ws_send2.at[0], ws_recv2.at[0], 2, to_xp).wait_recv()
    ws_copy(ws_send2.at[1], ws_recv2.at[1], 3, to_xm).wait_recv()
    w_sum = wblk[x] + ws_recv2[0].astype(F32) + ws_recv2[1].astype(F32)
    w_kv = w_sum[0:128].T.reshape(8, 32, 128)
    w_qq = jnp.concatenate([w_sum[128:192], jnp.zeros((64, 256), F32)], axis=0)
    w_qq = w_qq.T.reshape(8, 32, 128)
    w15_send[:, 0:32] = w_kv.astype(BF)
    w15_send[:, 32:48] = merge_low(w_qq[:, 0:16], w_qq[:, 16:32]).astype(BF)

    def w15_copy(k, peer, lands):
        return rcopy(
            w15_send.at[peer],
            w15_recv.at[lands],
            w15_s.at[k],
            w15_r.at[k],
            {"seq": x * 8 + peer},
        )

    @pl.loop(1, 8)
    def _(k):
        w15_copy(k, (g + k) % 8, g).start()

    w15_recv[g] = w15_send[g]

    send_back(1)

    @pl.loop(1, 8)
    def _(k):
        src = (g + 8 - k) % 8
        w15_copy(k, src, src).wait_recv()

    q_blocks, k_blocks, v_blocks = [], [], []
    for blk in range(4):
        r0 = w15_recv[2 * blk].astype(F32)
        r1 = w15_recv[2 * blk + 1].astype(F32)
        q_blocks.append(
            jnp.concatenate(
                [merge_low(r0[32:48], r1[32:48]), merge_high(r0[32:48], r1[32:48])], axis=0
            )
        )
        k_blocks.append(merge_low(r0[0:32], r1[0:32]))
        v_blocks.append(merge_high(r0[0:32], r1[0:32]))
    blocks = q_blocks + k_blocks + v_blocks
    width = 3 * INNER // n_clip
    for n in range(n_clip):
        b, off = divmod(width * n, 128)
        if off == 0:
            piece = blocks[b]
        else:
            turn = 128 - off
            piece = pltpu.roll(blocks[b], turn, 1)
            if off + width > 128:
                piece = jnp.where(
                    iota((32, 128), 1) < turn, piece, pltpu.roll(blocks[b + 1], turn, 1)
                )
        w2_send[n] = piece.astype(BF)

    def w2_copy(k, peer, lands):
        return rcopy(
            w2_send.at[peer], w2_recv.at[lands], w2_s.at[k], w2_r.at[k], {"clip": peer}
        )

    @pl.loop(1, n_clip)
    def _(k):
        w2_copy(k, (j + k) % n_clip, j).start()

    w2_recv[j] = w2_send[j]

    some = iota((NSEQ, CAP, HALF), 1) < TOP
    for h in range(2):

        @pl.loop(1, NSEQ)
        def _(k):
            src = (i + NSEQ - k) % NSEQ
            back_copy(h, k, src, src).wait_recv()

        returned = jnp.where(some, back_recv[h].astype(F32), 0.0).reshape(NMSG, HALF)
        patch_rows = mm_tn(picker[...], returned.astype(BF))
        patch_out[:, h * HALF : h * HALF + HALF] = (patch_rows * count_inv[:, 0:1]).astype(BF)

    stores[1].start()

    @pl.loop(1, n_clip)
    def _(k):
        src = (j + n_clip - k) % n_clip
        w2_copy(k, src, src).wait_recv()

    weight_out[...] = jnp.sum(w2_recv[...].astype(F32), axis=0)[:, 0:width]
    stores[2].start()

    @pl.loop(1, NSEQ)
    def _(k):
        token_copy(k, (i + k) % NSEQ, i).wait_send()
        back_copy(0, k, (i + k) % NSEQ, i).wait_send()
        back_copy(1, k, (i + k) % NSEQ, i).wait_send()

    @pl.loop(1, 8)
    def _(k):
        peer = (g + k) % 8
        kx_copy(k, peer, g).wait_send()
        qd_copy(k, peer, g).wait_send()
        at_copy(k, peer, g).wait_send()
        g_copy(k, peer, g).wait_send()
        w15_copy(k, peer, g).wait_send()

    @pl.loop(1, n_clip)
    def _(k):
        w2_copy(k, (j + k) % n_clip, j).wait_send()

    for n, s, half, dev in (
        (0, g, A, to_yp),
        (1, g, B, to_ym),
        (2, g, B, to_yp),
        (3, g, A, to_ym),
        (4, g, None, to_pal),
        (5, g_m, A, to_yp),
        (6, g_m, A, to_pal),
        (7, g_p, B, to_ym),
        (8, g_p, B, to_pal),
        (9, g_m, B, to_pal),
        (10, g_p, A, to_pal),
        (11, g_2, A, to_pal),
        (12, g_2, B, to_pal),
    ):
        p_copy(n, s, half, dev).wait_send()
    for n, s, half, dev in (
        (0, x, KA, to_xp),
        (1, x, KB, to_xm),
        (2, x, KB, to_xp),
        (3, x, KA, to_xm),
        (4, xm, KA, to_xp),
        (5, xp, KB, to_xm),
    ):
        k_copy(n, s, half, dev).wait_send()
    for n, dev in ((0, to_xp), (1, to_xm)):
        rs_copy(rs_send.at[n], rs_recv.at[n], n, dev).wait_send()
        rs_copy(rs_send2.at[n], rs_recv2.at[n], n + 2, dev).wait_send()
        ws_copy(ws_send.at[n], ws_recv.at[n], n, dev).wait_send()
        ws_copy(ws_send2.at[n], ws_recv2.at[n], n + 2, dev).wait_send()
    for store in stores:
        store.wait()


def hand_over(att, patch, weight, att_out, patch_out, weight_out, *scratch):
    bufs, sems = scratch[0:3], scratch[3]
    trios = tuple(zip((att, patch, weight), bufs, (att_out, patch_out, weight_out)))
    come = [pltpu.make_async_copy(a, b, sems.at[n]) for n, (a, b, _) in enumerate(trios)]
    leave = [pltpu.make_async_copy(b, o, sems.at[3 + n]) for n, (_, b, o) in enumerate(trios)]
    for move in come:
        move.start()
    for n in range(3):
        come[n].wait()
        leave[n].start()
    for move in leave:
        move.wait()


def local(patches, segment, dest_shard, dest_slot, w_qkv, out_grad):
    n_clip = lax.axis_size("clip")
    v = pltpu.VMEM
    dma = pltpu.SemaphoreType.DMA
    scratch = [
        v((196, D), BF),
        v((1, 196), I32),
        v((1, 192), I32),
        v((1, 192), I32),
        v((R, INNER), BF),
        v((R, INNER), BF),
        v((196, D), BF),
        v((32, 3 * INNER // n_clip), F32),
        v((NSEQ, CAP, EXT), BF),
        v((NSEQ, CAP, EXT), BF),
        v((2, NSEQ, CAP, HALF), BF),
        v((2, NSEQ, CAP, HALF), BF),
        v((D, 3 * INNER), BF),
        v((NMSG, 196), BF),
        v((R, NMSG), BF),
        v((196, 128), F32),
        v((8, R, D), BF),
        v((4, QROWS, 128), BF),
        v((4, 128, QROWS), BF),
        v((QROWS, 128), BF),
        v((QROWS, 128), BF),
        v((128, QROWS), F32),
        v((8, R, 128), BF),
        v((8, R, 128), BF),
        v((8, R, 128), BF),
        v((4, QROWS, QROWS), F32),
        v((4, 128, QROWS), F32),
        v((4, 1, QROWS), F32),
        v((4, 1, QROWS), F32),
        v((4, 1, QROWS), F32),
        v((1, QROWS), F32),
        v((8, 32, 128), BF),
        v((8, 32, 128), BF),
        v((QROWS, 128), F32),
        v((128, QROWS), F32),
        v((2, 256, 128), BF),
        v((2, 256, 128), BF),
        v((2, QROWS, 128), BF),
        v((2, QROWS, 128), BF),
        v((8, 96, 128), BF),
        v((8, 96, 128), BF),
        v((R, 3 * INNER), BF),
        v((4, 192, 256), F32),
        v((2, 96, 256), BF),
        v((2, 96, 256), BF),
        v((2, 192, 256), BF),
        v((2, 192, 256), BF),
        v((8, 48, 128), BF),
        v((8, 48, 128), BF),
        v((n_clip, 32, 128), BF),
        v((n_clip, 32, 128), BF),
        dma((6,)),
        dma((3,)),
        dma((NSEQ,)),
        dma((NSEQ,)),
        dma((2, NSEQ)),
        dma((2, NSEQ)),
        dma((13,)),
        dma((13,)),
        dma((6,)),
        dma((6,)),
        dma((8,)),
        dma((8,)),
        dma((8,)),
        dma((8,)),
        dma((8,)),
        dma((8,)),
        dma((4,)),
        dma((4,)),
        dma((8,)),
        dma((8,)),
        dma((4,)),
        dma((4,)),
        dma((8,)),
        dma((8,)),
        dma((n_clip,)),
        dma((n_clip,)),
    ]
    anywhere = pl.BlockSpec(memory_space=pl.ANY)
    shapes = (
        jax.ShapeDtypeStruct((1, R, INNER), BF),
        jax.ShapeDtypeStruct((1, 196, D), BF),
        jax.ShapeDtypeStruct((32, 3 * INNER // n_clip), F32),
    )
    results = pl.pallas_call(
        functools.partial(kernel, n_clip),
        out_shape=shapes,
        in_specs=[anywhere] * 6,
        out_specs=(anywhere,) * 3,
        scratch_shapes=scratch,
        compiler_params=pltpu.CompilerParams(
            collective_id=0, has_side_effects=True, vmem_limit_bytes=67_043_328
        ),
        name="rebalance_attention",
    )(patches, segment, dest_shard, dest_slot, w_qkv, out_grad)
    return pl.pallas_call(
        hand_over,
        out_shape=shapes,
        in_specs=[anywhere] * 3,
        out_specs=(anywhere,) * 3,
        scratch_shapes=[v(t.shape, t.dtype) for t in shapes] + [dma((6,))],
        name="hand_over",
    )(*results)


def solution(mesh):
    return jax.shard_map(
        local,
        mesh=mesh,
        in_specs=(
            P("clip", "seq", None),
            P("clip", "seq"),
            P("clip", "seq"),
            P("clip", "seq"),
            P(),
            P("clip", "seq", None),
        ),
        out_specs=(P("clip", "seq", None), P("clip", "seq", None), P("seq", "clip")),
        check_vma=False,
    )
```

```python
import functools

import jax
import jax.numpy as jnp
from jax import lax
from jax.experimental import pallas as pl
from jax.experimental.pallas import tpu as pltpu
from jax.sharding import PartitionSpec as P

BF = jnp.bfloat16
F32 = jnp.float32
I32 = jnp.int32
MESH = pl.DeviceIdType.MESH

D = 1024
INNER = 512
R = 64
NSEQ = 32
CAP = 8
NMSG = NSEQ * CAP
QROWS = 512
QC = 256
TOP = 6
EXT = D + 128
HALF = D // 2


def iota(shape, dim):
    return lax.broadcasted_iota(I32, shape, dim)


def onehot(cond):
    return jnp.where(cond, 1.0, 0.0).astype(BF)


def mm(a, b):
    return jnp.dot(a, b, preferred_element_type=F32)


def mm_nt(a, b):
    return lax.dot_general(a, b, (((1,), (1,)), ((), ())), preferred_element_type=F32)


def mm_tn(a, b):
    return lax.dot_general(a, b, (((0,), (0,)), ((), ())), preferred_element_type=F32)


def half_lanes(shape):
    return iota(shape, len(shape) - 1) < 64


def swap(v):
    return pltpu.roll(v, 64, v.ndim - 1)


def merge_low(a, b):
    return jnp.where(half_lanes(a.shape), a, swap(b))


def merge_high(a, b):
    return jnp.where(half_lanes(a.shape), swap(a), b)


def kernel(
    n_clip,
    patches_hbm,
    segment_hbm,
    shard_hbm,
    slot_hbm,
    w_hbm,
    grad_hbm,
    att_hbm,
    patch_hbm,
    weight_hbm,
    patches,
    segment,
    dest_shard,
    dest_slot,
    out_grad,
    att_out,
    patch_out,
    weight_out,
    send,
    recv,
    back_send,
    back_recv,
    w_all,
    picker,
    placer_ref,
    count_inv,
    pq,
    kv,
    kvt,
    qpad,
    dopad,
    dot_ref,
    kv_send,
    q_send,
    q_recv,
    do_send,
    do_recv,
    weights,
    part_out,
    stat_max,
    stat_sum,
    fac_ref,
    gd_ref,
    att_send,
    att_recv,
    dkv_acc,
    dq_acc,
    rs_send,
    rs_recv,
    g_send,
    g_recv,
    gnat,
    wblk,
    ws_send,
    ws_recv,
    w15_send,
    w15_recv,
    w2_send,
    w2_recv,
    in_sem,
    out_sem,
    a_s,
    a_r,
    b_s,
    b_r,
    p_s,
    p_r,
    k_s,
    k_r,
    kx_s,
    kx_r,
    q_s,
    q_r,
    do_s,
    do_r,
    at_s,
    at_r,
    rs_s,
    rs_r,
    g_s,
    g_r,
    ws_s,
    ws_r,
    w15_s,
    w15_r,
    w2_s,
    w2_r,
):
    i = lax.axis_index("seq")
    j = lax.axis_index("clip")
    x = i // 8
    y = (i // 2) % 4
    c = i % 2
    g = i % 8
    xp, xm, x2 = (x + 1) % 4, (x + 3) % 4, (x + 2) % 4
    yp, ym, y2 = (y + 1) % 4, (y + 3) % 4, (y + 2) % 4

    def seq_dev(dx, dy, dc):
        return {"seq": dx * 8 + dy * 2 + dc}

    def rcopy(src, dst, ss, rs, dev):
        return pltpu.make_async_remote_copy(
            src_ref=src, dst_ref=dst, send_sem=ss, recv_sem=rs, device_id=dev, device_id_type=MESH
        )

    loads = [
        pltpu.make_async_copy(a, b, in_sem.at[n])
        for n, (a, b) in enumerate(
            (
                (segment_hbm, segment),
                (shard_hbm, dest_shard),
                (slot_hbm, dest_slot),
                (patches_hbm.at[0], patches),
                (w_hbm, w_all),
                (grad_hbm.at[0], out_grad),
            )
        )
    ]
    for load in loads:
        load.start()

    to_pal = seq_dev(x, y, 1 - c)

    def seven(src, dst, ss, rs):
        return rcopy(src.at[pl.ds(0, 7)], dst.at[pl.ds(0, 7)], ss, rs, to_pal)

    barrier = pltpu.get_barrier_semaphore()

    @pl.loop(1, NSEQ)
    def _(k):
        pl.semaphore_signal(
            barrier, inc=1, device_id={"seq": (i + k) % NSEQ}, device_id_type=MESH
        )

    @pl.loop(1, n_clip)
    def _(k):
        pl.semaphore_signal(
            barrier, inc=1, device_id={"clip": (j + k) % n_clip}, device_id_type=MESH
        )

    for load in loads[0:4]:
        load.wait()
    seg = segment[...]
    tgt = dest_shard[...]
    slot = dest_slot[...]
    hit = iota((192, 196), 0) == seg
    member = onehot(hit)
    counts = jnp.sum(jnp.where(hit, 1.0, 0.0), axis=1, keepdims=True)
    sums = mm(member, patches[...])
    tokens = (sums * (1.0 / jnp.maximum(counts, 1.0))).astype(BF)
    to_shard = iota((NSEQ, 192), 0) == tgt
    shard_hot = onehot(to_shard)
    earlier = onehot(iota((192, 192), 0) < iota((192, 192), 1))
    before = mm(shard_hot, earlier)
    rank = jnp.sum(jnp.where(to_shard, before, 0.0), axis=0, keepdims=True)
    position = jnp.where(tgt >= 0, tgt.astype(F32) * CAP + rank, -1.0)
    chooser = onehot(iota((NMSG, 192), 0).astype(F32) == position)
    same = onehot(iota((192, 192), 0) == iota((192, 192), 1))
    slot_cells = jnp.broadcast_to(slot.astype(F32) + 1.0, (128, 192)).astype(BF)
    slot_column = mm_nt(same, slot_cells).astype(BF)
    rows = mm(chooser, jnp.concatenate([tokens, slot_column], axis=1))
    send[...] = rows.reshape(NSEQ, CAP, EXT).astype(BF)

    pl.semaphore_wait(barrier, NSEQ - 1 + n_clip - 1)

    def token_copy(peer, lands):
        return rcopy(
            send.at[peer, pl.ds(0, TOP)],
            recv.at[lands, pl.ds(0, TOP)],
            a_s,
            a_r,
            {"seq": peer},
        )

    @pl.loop(1, NSEQ)
    def _(k):
        token_copy((i + k) % NSEQ, i).start()

    recv[i] = send[i]

    picker[...] = mm(chooser, member).astype(BF)
    per_patch = mm_tn(member, jnp.broadcast_to(counts, (192, 128)).astype(BF))
    count_inv[...] = 1.0 / per_patch
    loads[5].wait()
    for blk in range(4):
        pair = out_grad[:, blk * 128 : blk * 128 + 128].astype(F32)
        top, low = pair[0:32], pair[32:64]
        do_send[2 * blk] = merge_low(top, low).astype(BF)
        do_send[2 * blk + 1] = merge_high(top, low).astype(BF)
    loads[4].wait()

    def token_all():
        part = (pl.ds(0, NSEQ - 1), pl.ds(0, TOP))
        return rcopy(send.at[part], recv.at[part], a_s, a_r, to_pal)

    token_all().wait_recv()

    full = iota((NSEQ, CAP, EXT), 1) < TOP
    came = jnp.where(full, recv[...].astype(F32), 0.0).reshape(NMSG, EXT).astype(BF)
    one_lane = onehot(iota((8, 128), 1) == 0)
    slot_row = mm_nt(one_lane, came[:, D:])[0:1]
    placer = onehot((iota((R, NMSG), 0) + 1).astype(F32) == slot_row)
    placer_ref[...] = placer
    placed = mm(placer, came[:, 0:D]).astype(BF)
    pq[g] = placed

    def kx_copy(peer, lands):
        return rcopy(
            kv_send.at[peer],
            kv.at[x, pl.ds(pl.multiple_of(lands * R, R), R)],
            kx_s,
            kx_r,
            {"seq": x * 8 + peer},
        )

    def q_copy(peer, lands):
        return rcopy(q_send.at[peer], q_recv.at[lands], q_s, q_r, {"seq": x * 8 + peer})

    def do_copy(peer, lands):
        return rcopy(do_send.at[peer], do_recv.at[lands], do_s, do_r, {"seq": x * 8 + peer})

    def half_up(v):
        return v.astype(BF).astype(F32)

    proj = half_up(mm(placed, w_all[:, INNER:]))
    for blk in range(4):
        k_blk = proj[:, blk * 128 : blk * 128 + 128]
        v_blk = proj[:, INNER + blk * 128 : INNER + blk * 128 + 128]
        kv_send[2 * blk] = merge_low(k_blk, v_blk).astype(BF)
        kv_send[2 * blk + 1] = merge_high(k_blk, v_blk).astype(BF)

    @pl.loop(1, 8)
    def _(k):
        kx_copy((g + k) % 8, g).start()

    kv[x, pl.ds(pl.multiple_of(g * R, R), R)] = kv_send[g]
    proj_q = half_up(mm(placed, w_all[:, 0:INNER])) * 0.125
    for blk in range(4):
        q_blk = proj_q[:, blk * 128 : blk * 128 + 128]
        q_send[2 * blk] = merge_low(q_blk[0:32], q_blk[32:64]).astype(BF)
        q_send[2 * blk + 1] = merge_high(q_blk[0:32], q_blk[32:64]).astype(BF)

    @pl.loop(1, 8)
    def _(k):
        q_copy((g + k) % 8, g).start()

    @pl.loop(1, 8)
    def _(k):
        do_copy((g + k) % 8, g).start()

    q_recv[g] = q_send[g]
    do_recv[g] = do_send[g]

    g_p, g_m, g_2 = yp * 2 + c, ym * 2 + c, y2 * 2 + c
    A, B = pl.ds(0, 32), pl.ds(32, 32)
    to_yp, to_ym = seq_dev(x, yp, c), seq_dev(x, ym, c)

    def p_copy(n, s, half, dev):
        ref = pq.at[s] if half is None else pq.at[s, half]
        return rcopy(ref, ref, p_s, p_r.at[n], dev)

    h_p, h_m, h_2, h_g = yp * 2 + 1 - c, ym * 2 + 1 - c, y2 * 2 + 1 - c, y * 2 + 1 - c

    def gather_first():
        p_copy(0, g, A, to_yp).start()
        p_copy(1, g, B, to_ym).start()
        p_copy(2, g, B, to_yp).start()
        p_copy(3, g, A, to_ym).start()
        p_copy(4, g, None, to_pal).start()

    def gather_second():
        p_copy(0, g_m, A, to_yp).wait_recv()
        p_copy(5, g_m, A, to_yp).start()
        p_copy(6, g_m, A, to_pal).start()
        p_copy(1, g_p, B, to_ym).wait_recv()
        p_copy(7, g_p, B, to_ym).start()
        p_copy(8, g_p, B, to_pal).start()
        p_copy(2, g_m, B, to_yp).wait_recv()
        p_copy(9, g_m, B, to_pal).start()
        p_copy(3, g_p, A, to_ym).wait_recv()
        p_copy(10, g_p, A, to_pal).start()

    def gather_third():
        p_copy(5, g_2, A, to_yp).wait_recv()
        p_copy(11, g_2, A, to_pal).start()
        p_copy(7, g_2, B, to_ym).wait_recv()
        p_copy(12, g_2, B, to_pal).start()

    def gather_last():
        p_copy(4, h_g, None, to_pal).wait_recv()
        p_copy(6, h_m, A, to_pal).wait_recv()
        p_copy(8, h_p, B, to_pal).wait_recv()
        p_copy(9, h_m, B, to_pal).wait_recv()
        p_copy(10, h_p, A, to_pal).wait_recv()
        p_copy(11, h_2, A, to_pal).wait_recv()
        p_copy(12, h_2, B, to_pal).wait_recv()

    def kx_all():
        part = pl.ds(0, 7 * R)
        return rcopy(kv.at[x, part], kv.at[x, part], kx_s, kx_r, to_pal)

    kx_all().wait_recv()
    KA, KB = pl.ds(0, 256), pl.ds(256, 256)
    to_xp, to_xm = seq_dev(xp, y, c), seq_dev(xm, y, c)

    def k_copy(n, s, half, dev):
        ref = kv.at[s, half]
        return rcopy(ref, ref, k_s, k_r.at[n], dev)

    k_copy(0, x, KA, to_xp).start()
    k_copy(1, x, KB, to_xm).start()
    k_copy(2, x, KB, to_xp).start()
    k_copy(3, x, KA, to_xm).start()

    seven(q_send, q_recv, q_s, q_r).wait_recv()
    gather_first()
    q_in = q_recv[...].astype(F32)
    low = half_lanes((8, 32, 128))
    q_rows = jnp.concatenate([jnp.where(low, q_in, 0.0), jnp.where(low, swap(q_in), 0.0)], axis=1)
    qpad[...] = q_rows.reshape(QROWS, 128).astype(BF)

    def forward(s, n):
        kvt[n] = kv[s].astype(F32).T.astype(BF)
        for q in range(QROWS // QC):
            qs = slice(q * QC, q * QC + QC)
            scores = mm_nt(kv[s], qpad[qs, :])
            top = jnp.max(scores, axis=0, keepdims=True)
            w = jnp.exp(scores - top)
            stat_max[n, :, qs] = top
            stat_sum[n, :, qs] = jnp.sum(w, axis=0, keepdims=True)
            weights[n, :, qs] = w
            part_out[n, :, qs] = mm(kvt[n], w.astype(BF))

    forward(x, 0)
    seven(do_send, do_recv, do_s, do_r).wait_recv()
    d_in = do_recv[...].astype(F32)
    d_rows = jnp.concatenate(
        [jnp.where(low, 0.0, swap(d_in)), jnp.where(low, 0.0, d_in)], axis=1
    ).reshape(QROWS, 128)
    dopad[...] = d_rows.astype(BF)
    dot_ref[...] = d_rows.T

    k_copy(0, xm, KA, to_xp).wait_recv()
    k_copy(4, xm, KA, to_xp).start()
    k_copy(1, xp, KB, to_xm).wait_recv()
    k_copy(5, xp, KB, to_xm).start()
    k_copy(2, xm, KB, to_xp).wait_recv()
    forward(xm, 1)
    k_copy(3, xp, KA, to_xm).wait_recv()
    forward(xp, 2)

    k_copy(4, x2, KA, to_xp).wait_recv()
    k_copy(5, x2, KB, to_xm).wait_recv()
    forward(x2, 3)

    best = jnp.maximum(
        jnp.maximum(stat_max[0], stat_max[1]), jnp.maximum(stat_max[2], stat_max[3])
    )
    facs = [jnp.exp(stat_max[n] - best) for n in range(4)]
    total = sum(facs[n] * stat_sum[n] for n in range(4))
    att_t = sum(facs[n] * part_out[n] for n in range(4)) / total
    att_half = att_t.astype(BF).astype(F32)
    gd_ref[...] = jnp.sum(att_half[64:128] * dot_ref[64:128], axis=0, keepdims=True)
    for n in range(4):
        fac_ref[n] = facs[n] / total
    att3 = att_half.T.reshape(8, R, 128)
    att_send[...] = merge_high(att3[:, 0:32], att3[:, 32:64]).astype(BF)

    def at_copy(peer, lands):
        return rcopy(att_send.at[peer], att_recv.at[lands], at_s, at_r, {"seq": x * 8 + peer})

    @pl.loop(1, 8)
    def _(k):
        at_copy((g + k) % 8, g).start()

    att_recv[g] = att_send[g]

    gather_second()
    dq_acc[...] = jnp.zeros((128, QROWS), F32)

    def backward(s, n):
        for q in range(QROWS // QC):
            qs = slice(q * QC, q * QC + QC)
            prob_grad = mm_nt(kv[s], dopad[qs, :])
            prob = weights[n, :, qs] * fac_ref[n, :, qs]
            score_grad = (prob * (prob_grad - gd_ref[:, qs])).astype(BF)
            upd = mm(score_grad, qpad[qs, :]) + mm(prob.astype(BF), dopad[qs, :])
            if q == 0:
                dkv_acc[n] = upd
            else:
                dkv_acc[n] += upd
            dq_acc[:, qs] += mm(kvt[n], score_grad)

    def ring_sum(sends, recvs, ss, rs, part, rows):
        half = rows // 2

        def copy(n, dev):
            return rcopy(sends.at[n], recvs.at[n], ss, rs.at[n], dev)

        def put(n, value, dev):
            sends[n] = value.astype(BF)
            copy(n, dev).start()

        def first():
            put(0, part(x2, 3, slice(0, half)), to_xp)
            put(1, part(x2, 3, slice(half, rows)), to_xm)

        def second():
            put(2, part(xp, 2, slice(half, rows)), to_xp)

        def third():
            put(3, part(xm, 1, slice(0, half)), to_xm)

        def fourth():
            copy(0, to_xp).wait_recv()
            put(4, part(xp, 2, slice(0, half)) + recvs[0].astype(F32), to_xp)
            copy(1, to_xm).wait_recv()
            put(5, part(xm, 1, slice(half, rows)) + recvs[1].astype(F32), to_xm)

        def fifth():
            for n, dev in ((2, to_xp), (3, to_xm), (4, to_xp), (5, to_xm)):
                copy(n, dev).wait_recv()
            up = recvs[4].astype(F32) + recvs[3].astype(F32)
            down = recvs[2].astype(F32) + recvs[5].astype(F32)
            return part(x, 0, slice(0, rows)) + jnp.concatenate([up, down], axis=0)

        def sent():
            rcopy(sends, recvs, ss, rs.at[0], to_xp).wait_send()

        return first, second, third, fourth, fifth, sent

    rs = ring_sum(rs_send, rs_recv, rs_s, rs_r, lambda s, n, part: dkv_acc[n, part], QROWS)
    backward(x2, 3)
    rs[0]()
    backward(xp, 2)
    rs[1]()
    backward(xm, 1)
    rs[2]()
    backward(x, 0)
    rs[3]()
    gather_third()
    dq_rows = jnp.where(half_lanes((QROWS, 128)), dq_acc[...].T * 0.125, 0.0)
    dq3 = dq_rows.reshape(8, R, 128)
    g_send[:, 64:96] = merge_low(dq3[:, 0:32], dq3[:, 32:64]).astype(BF)
    dkv = rs[4]().astype(BF)
    g_send[:, 0:64] = dkv.reshape(8, R, 128)

    def g_copy(peer, lands):
        return rcopy(g_send.at[peer], g_recv.at[lands], g_s, g_r, {"seq": x * 8 + peer})

    @pl.loop(1, 8)
    def _(k):
        g_copy((g + k) % 8, g).start()

    g_recv[g] = g_send[g]

    gather_last()
    grads = jnp.concatenate([dkv, dq_rows.astype(BF)], axis=1)
    w_part = mm_tn(grads, pq[...].reshape(QROWS, D))
    for q in range(4):
        wblk[q] = w_part[0:192, q * 256 : q * 256 + 256]

    ws = ring_sum(ws_send, ws_recv, ws_s, ws_r, lambda s, n, part: wblk[s, part], 192)
    for step in ws[0:3]:
        step()

    seven(att_send, att_recv, at_s, at_r).wait_recv()
    stores = [
        pltpu.make_async_copy(a, b, out_sem.at[n])
        for n, (a, b) in enumerate(
            ((att_out, att_hbm.at[0]), (patch_out, patch_hbm.at[0]), (weight_out, weight_hbm))
        )
    ]
    for blk in range(4):
        a0 = att_recv[2 * blk].astype(F32)
        a1 = att_recv[2 * blk + 1].astype(F32)
        lanes = slice(blk * 128, blk * 128 + 128)
        att_out[0:32, lanes] = merge_low(a0, a1).astype(BF)
        att_out[32:64, lanes] = merge_high(a0, a1).astype(BF)
    stores[0].start()

    ws[3]()

    seven(g_send, g_recv, g_s, g_r).wait_recv()
    for blk in range(4):
        r0 = g_recv[2 * blk].astype(F32)
        r1 = g_recv[2 * blk + 1].astype(F32)
        q_at, k_at, v_at = blk * 128, blk * 128 + 512, blk * 128 + 1024
        gnat[0:32, q_at : q_at + 128] = merge_low(r0[64:96], r1[64:96]).astype(BF)
        gnat[32:64, q_at : q_at + 128] = merge_high(r0[64:96], r1[64:96]).astype(BF)
        gnat[:, k_at : k_at + 128] = merge_low(r0[0:64], r1[0:64]).astype(BF)
        gnat[:, v_at : v_at + 128] = merge_high(r0[0:64], r1[0:64]).astype(BF)
    def back_copy(h, peer, lands):
        return rcopy(
            back_send.at[h, peer, pl.ds(0, TOP)],
            back_recv.at[h, lands, pl.ds(0, TOP)],
            b_s,
            b_r.at[h],
            {"seq": peer},
        )

    def send_back(h):
        grad = mm_nt(gnat[...], w_all[h * HALF : h * HALF + HALF, :]).astype(BF)
        back = mm_tn(placer_ref[...], grad)
        back_send[h] = back.reshape(NSEQ, CAP, HALF).astype(BF)

        @pl.loop(1, NSEQ)
        def _(k):
            back_copy(h, (i + k) % NSEQ, i).start()

        back_recv[h, i] = back_send[h, i]

    w_sum = ws[4]()
    w_kv = w_sum[0:128].T.reshape(8, 32, 128)
    w_qq = jnp.concatenate([w_sum[128:192], jnp.zeros((64, 256), F32)], axis=0)
    w_qq = w_qq.T.reshape(8, 32, 128)
    w15_send[:, 0:32] = w_kv.astype(BF)
    w15_send[:, 32:48] = merge_low(w_qq[:, 0:16], w_qq[:, 16:32]).astype(BF)

    def w15_copy(peer, lands):
        return rcopy(
            w15_send.at[peer], w15_recv.at[lands], w15_s, w15_r, {"seq": x * 8 + peer}
        )

    @pl.loop(1, 8)
    def _(k):
        w15_copy((g + k) % 8, g).start()

    w15_recv[g] = w15_send[g]

    send_back(0)
    send_back(1)

    seven(w15_send, w15_recv, w15_s, w15_r).wait_recv()
    q_blocks, k_blocks, v_blocks = [], [], []
    for blk in range(4):
        r0 = w15_recv[2 * blk].astype(F32)
        r1 = w15_recv[2 * blk + 1].astype(F32)
        q_blocks.append(
            jnp.concatenate(
                [merge_low(r0[32:48], r1[32:48]), merge_high(r0[32:48], r1[32:48])], axis=0
            )
        )
        k_blocks.append(merge_low(r0[0:32], r1[0:32]))
        v_blocks.append(merge_high(r0[0:32], r1[0:32]))
    blocks = q_blocks + k_blocks + v_blocks
    width = 3 * INNER // n_clip
    for n in range(n_clip):
        b, off = divmod(width * n, 128)
        if off == 0:
            piece = blocks[b]
        else:
            turn = 128 - off
            piece = pltpu.roll(blocks[b], turn, 1)
            if off + width > 128:
                piece = jnp.where(
                    iota((32, 128), 1) < turn, piece, pltpu.roll(blocks[b + 1], turn, 1)
                )
        w2_send[n] = piece.astype(BF)

    def w2_copy(peer, lands):
        return rcopy(w2_send.at[peer], w2_recv.at[lands], w2_s, w2_r, {"clip": peer})

    def w2_all():
        part = pl.ds(0, n_clip - 1)
        return rcopy(w2_send.at[part], w2_recv.at[part], w2_s, w2_r, to_pal)

    @pl.loop(1, n_clip)
    def _(k):
        w2_copy((j + k) % n_clip, j).start()

    w2_recv[j] = w2_send[j]

    some = iota((NSEQ, CAP, HALF), 1) < TOP
    for h in range(2):
        part = (pl.ds(0, NSEQ - 1), pl.ds(0, TOP))
        rcopy(back_send.at[h].at[part], back_recv.at[h].at[part], b_s, b_r.at[h], to_pal).wait_recv()
        returned = jnp.where(some, back_recv[h].astype(F32), 0.0).reshape(NMSG, HALF)
        patch_rows = mm_tn(picker[...], returned.astype(BF))
        patch_out[:, h * HALF : h * HALF + HALF] = (patch_rows * count_inv[:, 0:1]).astype(BF)

    stores[1].start()

    w2_all().wait_recv()
    weight_out[...] = jnp.sum(w2_recv[...].astype(F32), axis=0)[:, 0:width]
    stores[2].start()

    token_all().wait_send()
    part = (pl.ds(0, 2), pl.ds(0, NSEQ - 1), pl.ds(0, TOP))
    rcopy(back_send.at[part], back_recv.at[part], b_s, b_r.at[0], to_pal).wait_send()
    kx_all().wait_send()
    seven(q_send, q_recv, q_s, q_r).wait_send()
    seven(do_send, do_recv, do_s, do_r).wait_send()
    seven(att_send, att_recv, at_s, at_r).wait_send()
    seven(g_send, g_recv, g_s, g_r).wait_send()
    seven(w15_send, w15_recv, w15_s, w15_r).wait_send()
    w2_all().wait_send()
    seven(pq, pq, p_s, p_r.at[0]).wait_send()
    rcopy(kv.at[pl.ds(0, 3)], kv.at[pl.ds(0, 3)], k_s, k_r.at[0], to_xp).wait_send()
    rs[5]()
    ws[5]()
    for store in stores:
        store.wait()


def hand_over(att, patch, weight, att_out, patch_out, weight_out, *scratch):
    bufs, sems = scratch[0:3], scratch[3]
    trios = tuple(zip((att, patch, weight), bufs, (att_out, patch_out, weight_out)))
    come = [pltpu.make_async_copy(a, b, sems.at[n]) for n, (a, b, _) in enumerate(trios)]
    leave = [pltpu.make_async_copy(b, o, sems.at[3 + n]) for n, (_, b, o) in enumerate(trios)]
    for move in come:
        move.start()
    for n in range(3):
        come[n].wait()
        leave[n].start()
    for move in leave:
        move.wait()


def local(patches, segment, dest_shard, dest_slot, w_qkv, out_grad):
    n_clip = lax.axis_size("clip")
    v = pltpu.VMEM
    dma = pltpu.SemaphoreType.DMA
    scratch = [
        v((196, D), BF),
        v((1, 196), I32),
        v((1, 192), I32),
        v((1, 192), I32),
        v((R, INNER), BF),
        v((R, INNER), BF),
        v((196, D), BF),
        v((32, 3 * INNER // n_clip), F32),
        v((NSEQ, CAP, EXT), BF),
        v((NSEQ, CAP, EXT), BF),
        v((2, NSEQ, CAP, HALF), BF),
        v((2, NSEQ, CAP, HALF), BF),
        v((D, 3 * INNER), BF),
        v((NMSG, 196), BF),
        v((R, NMSG), BF),
        v((196, 128), F32),
        v((8, R, D), BF),
        v((4, QROWS, 128), BF),
        v((4, 128, QROWS), BF),
        v((QROWS, 128), BF),
        v((QROWS, 128), BF),
        v((128, QROWS), F32),
        v((8, R, 128), BF),
        v((8, 32, 128), BF),
        v((8, 32, 128), BF),
        v((8, 32, 128), BF),
        v((8, 32, 128), BF),
        v((4, QROWS, QROWS), F32),
        v((4, 128, QROWS), F32),
        v((4, 1, QROWS), F32),
        v((4, 1, QROWS), F32),
        v((4, 1, QROWS), F32),
        v((1, QROWS), F32),
        v((8, 32, 128), BF),
        v((8, 32, 128), BF),
        v((4, QROWS, 128), F32),
        v((128, QROWS), F32),
        v((6, 256, 128), BF),
        v((6, 256, 128), BF),
        v((8, 96, 128), BF),
        v((8, 96, 128), BF),
        v((R, 3 * INNER), BF),
        v((4, 192, 256), F32),
        v((6, 96, 256), BF),
        v((6, 96, 256), BF),
        v((8, 48, 128), BF),
        v((8, 48, 128), BF),
        v((n_clip, 32, 128), BF),
        v((n_clip, 32, 128), BF),
        dma((6,)),
        dma((3,)),
        dma,
        dma,
        dma,
        dma((2,)),
        dma,
        dma((13,)),
        dma,
        dma((6,)),
        dma,
        dma,
        dma,
        dma,
        dma,
        dma,
        dma,
        dma,
        dma,
        dma((6,)),
        dma,
        dma,
        dma,
        dma((6,)),
        dma,
        dma,
        dma,
        dma,
    ]
    anywhere = pl.BlockSpec(memory_space=pl.ANY)
    shapes = (
        jax.ShapeDtypeStruct((1, R, INNER), BF),
        jax.ShapeDtypeStruct((1, 196, D), BF),
        jax.ShapeDtypeStruct((32, 3 * INNER // n_clip), F32),
    )
    results = pl.pallas_call(
        functools.partial(kernel, n_clip),
        out_shape=shapes,
        in_specs=[anywhere] * 6,
        out_specs=(anywhere,) * 3,
        scratch_shapes=scratch,
        compiler_params=pltpu.CompilerParams(
            collective_id=0, has_side_effects=True, vmem_limit_bytes=67_043_328
        ),
        name="rebalance_attention",
    )(patches, segment, dest_shard, dest_slot, w_qkv, out_grad)
    return pl.pallas_call(
        hand_over,
        out_shape=shapes,
        in_specs=[anywhere] * 3,
        out_specs=(anywhere,) * 3,
        scratch_shapes=[v(t.shape, t.dtype) for t in shapes] + [dma((6,))],
        name="hand_over",
    )(*results)


def solution(mesh):
    return jax.shard_map(
        local,
        mesh=mesh,
        in_specs=(
            P("clip", "seq", None),
            P("clip", "seq"),
            P("clip", "seq"),
            P("clip", "seq"),
            P(),
            P("clip", "seq", None),
        ),
        out_specs=(P("clip", "seq", None), P("clip", "seq", None), P("seq", "clip")),
        check_vma=False,
    )
```

```python
import functools

import jax
import jax.numpy as jnp
from jax import lax
from jax.experimental import pallas as pl
from jax.experimental.pallas import tpu as pltpu
from jax.sharding import PartitionSpec as P

BF = jnp.bfloat16
F32 = jnp.float32
I32 = jnp.int32
MESH = pl.DeviceIdType.MESH

D = 1024
INNER = 512
R = 64
NSEQ = 32
CAP = 8
NMSG = NSEQ * CAP
QROWS = 512
QC = 256
TOP = 6
PARTS = ((0, 512), (512, 384), (896, 128))


def iota(shape, dim):
    return lax.broadcasted_iota(I32, shape, dim)


def onehot(cond):
    return jnp.where(cond, 1.0, 0.0).astype(BF)


def mm(a, b):
    return jnp.dot(a, b, preferred_element_type=F32)


def mm_nt(a, b):
    return lax.dot_general(a, b, (((1,), (1,)), ((), ())), preferred_element_type=F32)


def mm_tn(a, b):
    return lax.dot_general(a, b, (((0,), (0,)), ((), ())), preferred_element_type=F32)


def half_lanes(shape):
    return iota(shape, len(shape) - 1) < 64


def swap(v):
    return pltpu.roll(v, 64, v.ndim - 1)


def merge_low(a, b):
    return jnp.where(half_lanes(a.shape), a, swap(b))


def merge_high(a, b):
    return jnp.where(half_lanes(a.shape), swap(a), b)


def kernel(
    n_clip,
    patches_hbm,
    segment_hbm,
    shard_hbm,
    slot_hbm,
    w_hbm,
    grad_hbm,
    att_hbm,
    patch_hbm,
    weight_hbm,
    patches,
    segment,
    dest_shard,
    dest_slot,
    out_grad,
    att_out,
    patch_out,
    weight_out,
    send,
    recv,
    back_send_0,
    back_send_1,
    back_send_2,
    back_recv_0,
    back_recv_1,
    back_recv_2,
    w_all,
    picker,
    placer_ref,
    count_inv,
    pq,
    kv,
    kvt,
    qpad,
    dopad,
    dot_ref,
    kv_send,
    q_send,
    q_recv,
    do_send,
    do_recv,
    weights,
    part_out,
    stat_max,
    stat_sum,
    fac_ref,
    gd_ref,
    att_send,
    att_recv,
    dkv_acc,
    dq_acc,
    rs_send,
    rs_recv,
    g_send,
    g_recv,
    gq_send,
    gq_recv,
    gnat,
    pg_acc,
    wblk,
    ws_send,
    ws_recv,
    w15_send,
    w15_recv,
    w2_send,
    w2_recv,
    in_sem,
    out_sem,
    a_s,
    a_r,
    sl_s,
    sl_r,
    b_s,
    b_r,
    p_s,
    p_r,
    k_s,
    k_r,
    kx_s,
    kx_r,
    q_s,
    q_r,
    do_s,
    do_r,
    at_s,
    at_r,
    rs_s,
    rs_r,
    g_s,
    g_r,
    gq_s,
    gq_r,
    ws_s,
    ws_r,
    w15_s,
    w15_r,
    w2_s,
    w2_r,
):
    back_send = (back_send_0, back_send_1, back_send_2)
    back_recv = (back_recv_0, back_recv_1, back_recv_2)
    i = lax.axis_index("seq")
    j = lax.axis_index("clip")
    x = i // 8
    y = (i // 2) % 4
    c = i % 2
    g = i % 8
    xp, xm, x2 = (x + 1) % 4, (x + 3) % 4, (x + 2) % 4
    yp, ym, y2 = (y + 1) % 4, (y + 3) % 4, (y + 2) % 4

    def seq_dev(dx, dy, dc):
        return {"seq": dx * 8 + dy * 2 + dc}

    def rcopy(src, dst, ss, rs, dev):
        return pltpu.make_async_remote_copy(
            src_ref=src, dst_ref=dst, send_sem=ss, recv_sem=rs, device_id=dev, device_id_type=MESH
        )

    loads = [
        pltpu.make_async_copy(a, b, in_sem.at[n])
        for n, (a, b) in enumerate(
            (
                (segment_hbm, segment),
                (shard_hbm, dest_shard),
                (slot_hbm, dest_slot),
                (patches_hbm.at[0], patches),
                (w_hbm, w_all),
                (grad_hbm.at[0], out_grad),
            )
        )
    ]
    for load in loads:
        load.start()

    to_pal = seq_dev(x, y, 1 - c)

    def seven(src, dst, ss, rs):
        return rcopy(src.at[pl.ds(0, 7)], dst.at[pl.ds(0, 7)], ss, rs, to_pal)

    barrier = pltpu.get_barrier_semaphore()

    for k in range(1, NSEQ):
        pl.semaphore_signal(
            barrier, inc=1, device_id={"seq": lax.rem(i + k, NSEQ)}, device_id_type=MESH
        )
    for k in range(1, n_clip):
        pl.semaphore_signal(
            barrier, inc=1, device_id={"clip": lax.rem(j + k, n_clip)}, device_id_type=MESH
        )

    for load in loads[0:3]:
        load.wait()
    seg = segment[...]
    tgt = dest_shard[...]
    slot = dest_slot[...]
    hit = iota((192, 196), 0) == seg
    member = onehot(hit)
    counts = jnp.sum(jnp.where(hit, 1.0, 0.0), axis=1, keepdims=True)
    to_shard = iota((NSEQ, 192), 0) == tgt
    shard_hot = onehot(to_shard)
    earlier = onehot(iota((192, 192), 0) < iota((192, 192), 1))
    before = mm(shard_hot, earlier)
    rank = jnp.sum(jnp.where(to_shard, before, 0.0), axis=0, keepdims=True)
    position = jnp.where(tgt >= 0, tgt.astype(F32) * CAP + rank, -1.0)
    chooser = onehot(iota((NMSG, 192), 0).astype(F32) == position)
    slot_rows = jnp.where(
        iota((128, 192), 0).astype(F32) == rank, slot.astype(F32) + 1.0, 0.0
    ).astype(BF)
    slot_table = mm_nt(shard_hot, slot_rows).astype(BF)
    spread = onehot(iota((NMSG, NSEQ), 0) == iota((NMSG, NSEQ), 1) * CAP + TOP)
    slot_cells = mm(spread, slot_table)
    loads[3].wait()
    sums = mm(member, patches[...])
    tokens = (sums * (1.0 / jnp.maximum(counts, 1.0))).astype(BF)
    rows = mm(chooser, tokens)
    send[:, :, 0:128] = (rows[:, 0:128] + slot_cells).reshape(NSEQ, CAP, 128).astype(BF)
    send[:, :, 128:] = rows[:, 128:].reshape(NSEQ, CAP, D - 128).astype(BF)

    pl.semaphore_wait(barrier, NSEQ - 1 + n_clip - 1)

    def slot_copy(peer, lands):
        part = (pl.ds(TOP, 2), pl.ds(0, 128))
        return rcopy(
            send.at[(peer, *part)], recv.at[(lands, *part)], sl_s, sl_r, {"seq": peer}
        )

    def slot_all():
        part = (pl.ds(0, NSEQ - 1), pl.ds(TOP, 2), pl.ds(0, 128))
        return rcopy(send.at[part], recv.at[part], sl_s, sl_r, to_pal)

    def token_copy(peer, lands):
        return rcopy(
            send.at[peer, pl.ds(0, TOP)],
            recv.at[lands, pl.ds(0, TOP)],
            a_s,
            a_r,
            {"seq": peer},
        )

    @pl.loop(1, NSEQ)
    def _(k):
        slot_copy((i + k) % NSEQ, i).start()
        token_copy((i + k) % NSEQ, i).start()

    recv[i] = send[i]

    picker[...] = mm(chooser, member).astype(BF)
    per_patch = mm_tn(member, jnp.broadcast_to(counts, (192, 128)).astype(BF))
    count_inv[...] = 1.0 / per_patch
    loads[5].wait()
    for blk in range(4):
        pair = out_grad[:, blk * 128 : blk * 128 + 128].astype(F32)
        top, low = pair[0:32], pair[32:64]
        do_send[2 * blk] = merge_low(top, low).astype(BF)
        do_send[2 * blk + 1] = merge_high(top, low).astype(BF)
    loads[4].wait()

    def token_all():
        part = (pl.ds(0, NSEQ - 1), pl.ds(0, TOP))
        return rcopy(send.at[part], recv.at[part], a_s, a_r, to_pal)

    slot_all().wait_recv()
    token_all().wait_recv()

    full = iota((NSEQ, CAP, D), 1) < TOP
    came = jnp.where(full, recv[...].astype(F32), 0.0).reshape(NMSG, D).astype(BF)
    cells = recv[:, :, 0:128].astype(F32).reshape(NMSG, 128).astype(BF)
    col = iota((NMSG, NMSG), 1)
    from_row = onehot(iota((NMSG, NMSG), 0) == (col // CAP) * CAP + TOP)
    slot_sq = mm_tn(cells, from_row)[0:8]
    rank_of = iota((8, NMSG), 1) % CAP
    wanted = (iota((8, NMSG), 0) == rank_of) & (rank_of < TOP)
    slot_row = jnp.sum(jnp.where(wanted, slot_sq, 0.0), axis=0, keepdims=True)
    placer = onehot((iota((R, NMSG), 0) + 1).astype(F32) == slot_row)
    placer_ref[...] = placer
    placed = mm(placer, came).astype(BF)
    pq[g] = placed

    def kx_copy(peer, lands):
        return rcopy(
            kv_send.at[peer],
            kv.at[x, pl.ds(pl.multiple_of(lands * R, R), R)],
            kx_s,
            kx_r,
            {"seq": x * 8 + peer},
        )

    def q_copy(peer, lands):
        return rcopy(q_send.at[peer], q_recv.at[lands], q_s, q_r, {"seq": x * 8 + peer})

    def do_copy(peer, lands):
        return rcopy(do_send.at[peer], do_recv.at[lands], do_s, do_r, {"seq": x * 8 + peer})

    def half_up(v):
        return v.astype(BF).astype(F32)

    proj = half_up(mm(placed, w_all[:, INNER:]))
    for blk in range(4):
        k_blk = proj[:, blk * 128 : blk * 128 + 128]
        v_blk = proj[:, INNER + blk * 128 : INNER + blk * 128 + 128]
        kv_send[2 * blk] = merge_low(k_blk, v_blk).astype(BF)
        kv_send[2 * blk + 1] = merge_high(k_blk, v_blk).astype(BF)

    @pl.loop(1, 8)
    def _(k):
        kx_copy((g + k) % 8, g).start()

    kv[x, pl.ds(pl.multiple_of(g * R, R), R)] = kv_send[g]
    proj_q = half_up(mm(placed, w_all[:, 0:INNER])) * 0.125
    for blk in range(4):
        q_blk = proj_q[:, blk * 128 : blk * 128 + 128]
        q_send[2 * blk] = merge_low(q_blk[0:32], q_blk[32:64]).astype(BF)
        q_send[2 * blk + 1] = merge_high(q_blk[0:32], q_blk[32:64]).astype(BF)

    @pl.loop(1, 8)
    def _(k):
        q_copy((g + k) % 8, g).start()

    @pl.loop(1, 8)
    def _(k):
        do_copy((g + k) % 8, g).start()

    q_recv[g] = q_send[g]
    do_recv[g] = do_send[g]

    g_p, g_m, g_2 = yp * 2 + c, ym * 2 + c, y2 * 2 + c
    A, B = pl.ds(0, 32), pl.ds(32, 32)
    to_yp, to_ym = seq_dev(x, yp, c), seq_dev(x, ym, c)

    def p_copy(n, s, half, dev):
        ref = pq.at[s] if half is None else pq.at[s, half]
        return rcopy(ref, ref, p_s, p_r.at[n], dev)

    h_p, h_m, h_2, h_g = yp * 2 + 1 - c, ym * 2 + 1 - c, y2 * 2 + 1 - c, y * 2 + 1 - c

    def gather_first():
        p_copy(0, g, A, to_yp).start()
        p_copy(1, g, B, to_ym).start()
        p_copy(2, g, B, to_yp).start()
        p_copy(3, g, A, to_ym).start()
        p_copy(4, g, None, to_pal).start()

    def gather_second():
        p_copy(0, g_m, A, to_yp).wait_recv()
        p_copy(5, g_m, A, to_yp).start()
        p_copy(6, g_m, A, to_pal).start()
        p_copy(1, g_p, B, to_ym).wait_recv()
        p_copy(7, g_p, B, to_ym).start()
        p_copy(8, g_p, B, to_pal).start()
        p_copy(2, g_m, B, to_yp).wait_recv()
        p_copy(9, g_m, B, to_pal).start()
        p_copy(3, g_p, A, to_ym).wait_recv()
        p_copy(10, g_p, A, to_pal).start()

    def gather_third():
        p_copy(5, g_2, A, to_yp).wait_recv()
        p_copy(11, g_2, A, to_pal).start()
        p_copy(7, g_2, B, to_ym).wait_recv()
        p_copy(12, g_2, B, to_pal).start()

    def gather_last():
        p_copy(4, h_g, None, to_pal).wait_recv()
        p_copy(6, h_m, A, to_pal).wait_recv()
        p_copy(8, h_p, B, to_pal).wait_recv()
        p_copy(9, h_m, B, to_pal).wait_recv()
        p_copy(10, h_p, A, to_pal).wait_recv()
        p_copy(11, h_2, A, to_pal).wait_recv()
        p_copy(12, h_2, B, to_pal).wait_recv()

    def kx_all():
        part = pl.ds(0, 7 * R)
        return rcopy(kv.at[x, part], kv.at[x, part], kx_s, kx_r, to_pal)

    kx_all().wait_recv()
    KA, KB = pl.ds(0, 256), pl.ds(256, 256)
    to_xp, to_xm = seq_dev(xp, y, c), seq_dev(xm, y, c)

    def k_copy(n, s, half, dev):
        ref = kv.at[s, half]
        return rcopy(ref, ref, k_s, k_r.at[n], dev)

    k_copy(0, x, KA, to_xp).start()
    k_copy(1, x, KB, to_xm).start()
    k_copy(2, x, KB, to_xp).start()
    k_copy(3, x, KA, to_xm).start()

    seven(q_send, q_recv, q_s, q_r).wait_recv()
    gather_first()
    q_in = q_recv[...].astype(F32)
    low = half_lanes((8, 32, 128))
    q_rows = jnp.concatenate([jnp.where(low, q_in, 0.0), jnp.where(low, swap(q_in), 0.0)], axis=1)
    qpad[...] = q_rows.reshape(QROWS, 128).astype(BF)

    def forward(s, n):
        kvt[n] = kv[s].astype(F32).T.astype(BF)
        for q in range(QROWS // QC):
            qs = slice(q * QC, q * QC + QC)
            scores = mm_nt(kv[s], qpad[qs, :])
            top = jnp.max(scores, axis=0, keepdims=True)
            w = jnp.exp(scores - top)
            stat_max[n, :, qs] = top
            stat_sum[n, :, qs] = jnp.sum(w, axis=0, keepdims=True)
            weights[n, :, qs] = w
            part_out[n, :, qs] = mm(kvt[n], w.astype(BF))

    forward(x, 0)
    seven(do_send, do_recv, do_s, do_r).wait_recv()
    d_in = do_recv[...].astype(F32)
    d_rows = jnp.concatenate(
        [jnp.where(low, 0.0, swap(d_in)), jnp.where(low, 0.0, d_in)], axis=1
    ).reshape(QROWS, 128)
    dopad[...] = d_rows.astype(BF)
    dot_ref[...] = d_rows.T

    k_copy(0, xm, KA, to_xp).wait_recv()
    k_copy(4, xm, KA, to_xp).start()
    k_copy(1, xp, KB, to_xm).wait_recv()
    k_copy(5, xp, KB, to_xm).start()
    k_copy(2, xm, KB, to_xp).wait_recv()
    forward(xm, 1)
    k_copy(3, xp, KA, to_xm).wait_recv()
    forward(xp, 2)

    k_copy(4, x2, KA, to_xp).wait_recv()
    k_copy(5, x2, KB, to_xm).wait_recv()
    forward(x2, 3)

    best = jnp.maximum(
        jnp.maximum(stat_max[0], stat_max[1]), jnp.maximum(stat_max[2], stat_max[3])
    )
    facs = [jnp.exp(stat_max[n] - best) for n in range(4)]
    total = sum(facs[n] * stat_sum[n] for n in range(4))
    att_t = sum(facs[n] * part_out[n] for n in range(4)) / total
    att_half = att_t.astype(BF).astype(F32)
    gd_ref[...] = jnp.sum(att_half[64:128] * dot_ref[64:128], axis=0, keepdims=True)
    for n in range(4):
        fac_ref[n] = facs[n] / total
    att3 = att_half.T.reshape(8, R, 128)
    att_send[...] = merge_high(att3[:, 0:32], att3[:, 32:64]).astype(BF)

    def at_copy(peer, lands):
        return rcopy(att_send.at[peer], att_recv.at[lands], at_s, at_r, {"seq": x * 8 + peer})

    @pl.loop(1, 8)
    def _(k):
        at_copy((g + k) % 8, g).start()

    att_recv[g] = att_send[g]

    dq_acc[...] = jnp.zeros((128, QROWS), F32)

    def backward(s, n):
        for q in range(QROWS // QC):
            qs = slice(q * QC, q * QC + QC)
            prob_grad = mm_nt(kv[s], dopad[qs, :])
            prob = weights[n, :, qs] * fac_ref[n, :, qs]
            score_grad = (prob * (prob_grad - gd_ref[:, qs])).astype(BF)
            upd = mm(score_grad, qpad[qs, :]) + mm(prob.astype(BF), dopad[qs, :])
            if q == 0:
                dkv_acc[n] = upd
            else:
                dkv_acc[n] += upd
            dq_acc[:, qs] += mm(kvt[n], score_grad)

    def ring_sum(sends, recvs, ss, rs, part, rows):
        half = rows // 2

        def copy(n, dev):
            return rcopy(sends.at[n], recvs.at[n], ss, rs.at[n], dev)

        def put(n, value, dev):
            sends[n] = value.astype(BF)
            copy(n, dev).start()

        def first():
            put(0, part(x2, 3, slice(0, half)), to_xp)
            put(1, part(x2, 3, slice(half, rows)), to_xm)

        def second():
            put(2, part(xp, 2, slice(half, rows)), to_xp)

        def third():
            put(3, part(xm, 1, slice(0, half)), to_xm)

        def fourth():
            copy(0, to_xp).wait_recv()
            put(4, part(xp, 2, slice(0, half)) + recvs[0].astype(F32), to_xp)
            copy(1, to_xm).wait_recv()
            put(5, part(xm, 1, slice(half, rows)) + recvs[1].astype(F32), to_xm)

        def fifth():
            for n, dev in ((2, to_xp), (3, to_xm), (4, to_xp), (5, to_xm)):
                copy(n, dev).wait_recv()
            up = recvs[4].astype(F32) + recvs[3].astype(F32)
            down = recvs[2].astype(F32) + recvs[5].astype(F32)
            return part(x, 0, slice(0, rows)) + jnp.concatenate([up, down], axis=0)

        def sent():
            rcopy(sends, recvs, ss, rs.at[0], to_xp).wait_send()

        return first, second, third, fourth, fifth, sent

    rs = ring_sum(rs_send, rs_recv, rs_s, rs_r, lambda s, n, part: dkv_acc[n, part], QROWS)
    backward(x2, 3)
    rs[0]()
    gather_second()
    backward(xp, 2)
    rs[1]()
    backward(xm, 1)
    rs[2]()
    backward(x, 0)
    rs[3]()
    dq_rows = jnp.where(half_lanes((QROWS, 128)), dq_acc[...].T * 0.125, 0.0)
    dq3 = dq_rows.reshape(8, R, 128)
    gq_send[...] = merge_low(dq3[:, 0:32], dq3[:, 32:64]).astype(BF)

    def gq_copy(peer, lands):
        return rcopy(gq_send.at[peer], gq_recv.at[lands], gq_s, gq_r, {"seq": x * 8 + peer})

    def g_copy(peer, lands):
        return rcopy(g_send.at[peer], g_recv.at[lands], g_s, g_r, {"seq": x * 8 + peer})

    @pl.loop(1, 8)
    def _(k):
        gq_copy((g + k) % 8, g).start()

    gq_recv[g] = gq_send[g]
    gather_third()
    dkv = rs[4]().astype(BF)
    g_send[...] = dkv.reshape(8, R, 128)

    @pl.loop(1, 8)
    def _(k):
        g_copy((g + k) % 8, g).start()

    g_recv[g] = g_send[g]

    gather_last()
    grads = jnp.concatenate([dkv, dq_rows.astype(BF)], axis=1)
    w_part = mm_tn(grads, pq[...].reshape(QROWS, D))
    for q in range(4):
        wblk[q] = w_part[0:192, q * 256 : q * 256 + 256]

    ws = ring_sum(ws_send, ws_recv, ws_s, ws_r, lambda s, n, part: wblk[s, part], 192)
    for step in ws[0:3]:
        step()

    seven(att_send, att_recv, at_s, at_r).wait_recv()
    stores = [
        pltpu.make_async_copy(a, b, out_sem.at[n])
        for n, (a, b) in enumerate(
            ((att_out, att_hbm.at[0]), (patch_out, patch_hbm.at[0]), (weight_out, weight_hbm))
        )
    ]
    for blk in range(4):
        a0 = att_recv[2 * blk].astype(F32)
        a1 = att_recv[2 * blk + 1].astype(F32)
        lanes = slice(blk * 128, blk * 128 + 128)
        att_out[0:32, lanes] = merge_low(a0, a1).astype(BF)
        att_out[32:64, lanes] = merge_high(a0, a1).astype(BF)
    stores[0].start()

    ws[3]()

    def lane_block(n):
        return slice(n * 128, n * 128 + 128)

    seven(gq_send, gq_recv, gq_s, gq_r).wait_recv()
    for blk in range(4):
        r0 = gq_recv[2 * blk].astype(F32)
        r1 = gq_recv[2 * blk + 1].astype(F32)
        gnat[0:32, lane_block(blk)] = merge_low(r0, r1).astype(BF)
        gnat[32:64, lane_block(blk)] = merge_high(r0, r1).astype(BF)
    pg_acc[...] = mm_nt(gnat[:, 0:INNER], w_all[:, 0:INNER])
    seven(g_send, g_recv, g_s, g_r).wait_recv()
    for blk in range(4):
        r0 = g_recv[2 * blk].astype(F32)
        r1 = g_recv[2 * blk + 1].astype(F32)
        gnat[:, lane_block(blk + 4)] = merge_low(r0, r1).astype(BF)
        gnat[:, lane_block(blk + 8)] = merge_high(r0, r1).astype(BF)

    def back_copy(h, peer, lands):
        return rcopy(
            back_send[h].at[peer, pl.ds(0, TOP)],
            back_recv[h].at[lands, pl.ds(0, TOP)],
            b_s.at[h],
            b_r.at[h],
            {"seq": peer},
        )

    def back_all(h):
        part = (pl.ds(0, NSEQ - 1), pl.ds(0, TOP))
        return rcopy(
            back_send[h].at[part], back_recv[h].at[part], b_s.at[h], b_r.at[h], to_pal
        )

    def make_back(h):
        start, size = PARTS[h]
        cols = slice(start, start + size)
        grad = pg_acc[:, cols] + mm_nt(gnat[:, INNER:], w_all[cols, INNER:])
        back = mm_tn(placer_ref[...], grad.astype(BF))
        back_send[h][...] = back.reshape(NSEQ, CAP, size).astype(BF)

    def send_back(h):
        @pl.loop(1, NSEQ)
        def _(k):
            back_copy(h, (i + k) % NSEQ, i).start()

        back_recv[h][i] = back_send[h][i]

    make_back(0)

    w_sum = ws[4]()
    w_kv = w_sum[0:128].T.reshape(8, 32, 128)
    w_qq = jnp.concatenate([w_sum[128:192], jnp.zeros((64, 256), F32)], axis=0)
    w_qq = w_qq.T.reshape(8, 32, 128)
    w15_send[:, 0:32] = w_kv.astype(BF)
    w15_send[:, 32:48] = merge_low(w_qq[:, 0:16], w_qq[:, 16:32]).astype(BF)

    def w15_copy(peer, lands):
        return rcopy(
            w15_send.at[peer], w15_recv.at[lands], w15_s, w15_r, {"seq": x * 8 + peer}
        )

    @pl.loop(1, 8)
    def _(k):
        w15_copy((g + k) % 8, g).start()

    w15_recv[g] = w15_send[g]

    send_back(0)
    make_back(1)
    send_back(1)
    make_back(2)

    seven(w15_send, w15_recv, w15_s, w15_r).wait_recv()
    q_blocks, k_blocks, v_blocks = [], [], []
    for blk in range(4):
        r0 = w15_recv[2 * blk].astype(F32)
        r1 = w15_recv[2 * blk + 1].astype(F32)
        q_blocks.append(
            jnp.concatenate(
                [merge_low(r0[32:48], r1[32:48]), merge_high(r0[32:48], r1[32:48])], axis=0
            )
        )
        k_blocks.append(merge_low(r0[0:32], r1[0:32]))
        v_blocks.append(merge_high(r0[0:32], r1[0:32]))
    blocks = q_blocks + k_blocks + v_blocks
    width = 3 * INNER // n_clip
    for n in range(n_clip):
        b, off = divmod(width * n, 128)
        if off == 0:
            piece = blocks[b]
        else:
            turn = 128 - off
            piece = pltpu.roll(blocks[b], turn, 1)
            if off + width > 128:
                piece = jnp.where(
                    iota((32, 128), 1) < turn, piece, pltpu.roll(blocks[b + 1], turn, 1)
                )
        tail = piece[24:32]
        last = jnp.concatenate(
            [pltpu.roll(tail, 96, 1), pltpu.roll(tail, 64, 1), pltpu.roll(tail, 32, 1)], axis=0
        )
        w2_send[n] = jnp.where(iota((24, 128), 1) < width, piece[0:24], last).astype(BF)

    def w2_copy(peer, lands):
        return rcopy(w2_send.at[peer], w2_recv.at[lands], w2_s, w2_r, {"clip": peer})

    def w2_all():
        part = pl.ds(0, n_clip - 1)
        return rcopy(w2_send.at[part], w2_recv.at[part], w2_s, w2_r, to_pal)

    @pl.loop(1, n_clip)
    def _(k):
        w2_copy((j + k) % n_clip, j).start()

    w2_recv[j] = w2_send[j]
    send_back(2)

    for h, (start, size) in enumerate(PARTS):
        back_all(h).wait_recv()
        some = iota((NSEQ, CAP, size), 1) < TOP
        returned = jnp.where(some, back_recv[h][...].astype(F32), 0.0).reshape(NMSG, size)
        patch_rows = mm_tn(picker[...], returned.astype(BF))
        patch_out[:, start : start + size] = (patch_rows * count_inv[:, 0:1]).astype(BF)

    stores[1].start()

    w2_all().wait_recv()
    w_rows = jnp.sum(w2_recv[...].astype(F32), axis=0)
    weight_out[0:24] = w_rows[:, 0:width]
    lane = iota((8, 128), 1)
    tail = jnp.where(
        lane < 32,
        pltpu.roll(w_rows[0:8], 32, 1),
        jnp.where(lane < 64, pltpu.roll(w_rows[8:16], 64, 1), pltpu.roll(w_rows[16:24], 96, 1)),
    )
    weight_out[24:32] = tail[:, 0:width]
    stores[2].start()

    slot_all().wait_send()
    token_all().wait_send()
    for h in range(len(PARTS)):
        back_all(h).wait_send()
    kx_all().wait_send()
    seven(q_send, q_recv, q_s, q_r).wait_send()
    seven(do_send, do_recv, do_s, do_r).wait_send()
    seven(att_send, att_recv, at_s, at_r).wait_send()
    seven(g_send, g_recv, g_s, g_r).wait_send()
    seven(gq_send, gq_recv, gq_s, gq_r).wait_send()
    seven(w15_send, w15_recv, w15_s, w15_r).wait_send()
    w2_all().wait_send()
    seven(pq, pq, p_s, p_r.at[0]).wait_send()
    rcopy(kv.at[pl.ds(0, 3)], kv.at[pl.ds(0, 3)], k_s, k_r.at[0], to_xp).wait_send()
    rs[5]()
    ws[5]()
    for store in stores:
        store.wait()


def hand_over(att, patch, weight, att_out, patch_out, weight_out, sems):
    pairs = ((patch, patch_out), (att, att_out), (weight, weight_out))
    moves = [pltpu.make_async_copy(a, b, sems.at[n]) for n, (a, b) in enumerate(pairs)]
    for move in moves:
        move.start()
    for move in moves:
        move.wait()


def local(patches, segment, dest_shard, dest_slot, w_qkv, out_grad):
    n_clip = lax.axis_size("clip")
    v = pltpu.VMEM
    dma = pltpu.SemaphoreType.DMA
    scratch = [
        v((196, D), BF),
        v((1, 196), I32),
        v((1, 192), I32),
        v((1, 192), I32),
        v((R, INNER), BF),
        v((R, INNER), BF),
        v((196, D), BF),
        v((32, 3 * INNER // n_clip), F32),
        v((NSEQ, CAP, D), BF),
        v((NSEQ, CAP, D), BF),
        *[v((NSEQ, CAP, size), BF) for _, size in PARTS],
        *[v((NSEQ, CAP, size), BF) for _, size in PARTS],
        v((D, 3 * INNER), BF),
        v((NMSG, 196), BF),
        v((R, NMSG), BF),
        v((196, 128), F32),
        v((8, R, D), BF),
        v((4, QROWS, 128), BF),
        v((4, 128, QROWS), BF),
        v((QROWS, 128), BF),
        v((QROWS, 128), BF),
        v((128, QROWS), F32),
        v((8, R, 128), BF),
        v((8, 32, 128), BF),
        v((8, 32, 128), BF),
        v((8, 32, 128), BF),
        v((8, 32, 128), BF),
        v((4, QROWS, QROWS), F32),
        v((4, 128, QROWS), F32),
        v((4, 1, QROWS), F32),
        v((4, 1, QROWS), F32),
        v((4, 1, QROWS), F32),
        v((1, QROWS), F32),
        v((8, 32, 128), BF),
        v((8, 32, 128), BF),
        v((4, QROWS, 128), F32),
        v((128, QROWS), F32),
        v((6, 256, 128), BF),
        v((6, 256, 128), BF),
        v((8, R, 128), BF),
        v((8, R, 128), BF),
        v((8, 32, 128), BF),
        v((8, 32, 128), BF),
        v((R, 3 * INNER), BF),
        v((R, D), F32),
        v((4, 192, 256), F32),
        v((6, 96, 256), BF),
        v((6, 96, 256), BF),
        v((8, 48, 128), BF),
        v((8, 48, 128), BF),
        v((n_clip, 24, 128), BF),
        v((n_clip, 24, 128), BF),
        dma((6,)),
        dma((3,)),
        dma,
        dma,
        dma,
        dma,
        dma((3,)),
        dma((3,)),
        dma,
        dma((13,)),
        dma,
        dma((6,)),
        dma,
        dma,
        dma,
        dma,
        dma,
        dma,
        dma,
        dma,
        dma,
        dma((6,)),
        dma,
        dma,
        dma,
        dma,
        dma,
        dma((6,)),
        dma,
        dma,
        dma,
        dma,
    ]
    anywhere = pl.BlockSpec(memory_space=pl.ANY)
    shapes = (
        jax.ShapeDtypeStruct((1, R, INNER), BF),
        jax.ShapeDtypeStruct((1, 196, D), BF),
        jax.ShapeDtypeStruct((32, 3 * INNER // n_clip), F32),
    )
    operands = (patches, segment, dest_shard, dest_slot, w_qkv, out_grad)
    results = pl.pallas_call(
        functools.partial(kernel, n_clip),
        out_shape=shapes,
        in_specs=[anywhere] * 6,
        out_specs=(anywhere,) * 3,
        scratch_shapes=scratch,
        compiler_params=pltpu.CompilerParams(
            collective_id=0, has_side_effects=True, vmem_limit_bytes=40 * 1024 * 1024
        ),
        name="rebalance_attention",
    )(*[pltpu.with_memory_space_constraint(a, pltpu.HBM) for a in operands])
    return pl.pallas_call(
        hand_over,
        out_shape=shapes,
        in_specs=[anywhere] * 3,
        out_specs=(anywhere,) * 3,
        scratch_shapes=[dma((3,))],
        compiler_params=pltpu.CompilerParams(vmem_limit_bytes=2 * 1024 * 1024),
        name="hand_over",
    )(*results)


def solution(mesh):
    return jax.shard_map(
        local,
        mesh=mesh,
        in_specs=(
            P("clip", "seq", None),
            P("clip", "seq"),
            P("clip", "seq"),
            P("clip", "seq"),
            P(),
            P("clip", "seq", None),
        ),
        out_specs=(P("clip", "seq", None), P("clip", "seq", None), P("seq", "clip")),
        check_vma=False,
    )
```

```python
import functools

import jax
import jax.numpy as jnp
from jax import lax
from jax.experimental import pallas as pl
from jax.experimental.pallas import tpu as pltpu
from jax.sharding import PartitionSpec as P

BF = jnp.bfloat16
F32 = jnp.float32
I32 = jnp.int32
MESH = pl.DeviceIdType.MESH

D = 1024
INNER = 512
R = 64
NSEQ = 32
CAP = 8
NMSG = NSEQ * CAP
QROWS = 512
QC = 256
TOP = 6
PARTS = ((0, 256), (256, 512), (768, 256))
HOPS_X = (0, 1, 2, 1)
HOPS_Y = (0, 2, 4, 2)
FAR_FIRST = sorted(
    ((a, b, d) for a in range(4) for b in range(4) for d in range(2) if a or b or d),
    key=lambda t: -(HOPS_X[t[0]] + HOPS_Y[t[1]]),
)


def iota(shape, dim):
    return lax.broadcasted_iota(I32, shape, dim)


def onehot(cond):
    return jnp.where(cond, 1.0, 0.0).astype(BF)


def mm(a, b):
    return jnp.dot(a, b, preferred_element_type=F32)


def mm_nt(a, b):
    return lax.dot_general(a, b, (((1,), (1,)), ((), ())), preferred_element_type=F32)


def mm_tn(a, b):
    return lax.dot_general(a, b, (((0,), (0,)), ((), ())), preferred_element_type=F32)


def half_lanes(shape):
    return iota(shape, len(shape) - 1) < 64


def swap(v):
    return pltpu.roll(v, 64, v.ndim - 1)


def merge_low(a, b):
    return jnp.where(half_lanes(a.shape), a, swap(b))


def merge_high(a, b):
    return jnp.where(half_lanes(a.shape), swap(a), b)


def kernel(
    n_clip,
    patches_hbm,
    segment_hbm,
    shard_hbm,
    slot_hbm,
    w_hbm,
    grad_hbm,
    att_hbm,
    patch_hbm,
    weight_hbm,
    patches,
    segment,
    dest_shard,
    dest_slot,
    out_grad,
    att_out,
    patch_out,
    weight_out,
    send,
    recv,
    back_send_0,
    back_send_1,
    back_send_2,
    back_recv_0,
    back_recv_1,
    back_recv_2,
    w_all,
    picker,
    placer_ref,
    count_inv,
    pq,
    kv,
    kvt,
    qpad,
    dopad,
    dot_ref,
    kv_send,
    q_send,
    q_recv,
    do_send,
    do_recv,
    weights,
    part_out,
    stat_max,
    stat_sum,
    fac_ref,
    gd_ref,
    att_send,
    att_recv,
    dkv_acc,
    dq_acc,
    rs_send,
    rs_recv,
    g_send,
    g_recv,
    gq_send,
    gq_recv,
    gnat,
    pg_acc,
    wblk,
    ws_send,
    ws_recv,
    w15_send,
    w15_recv,
    w2_send,
    w2_recv,
    in_sem,
    out_sem,
    a_s,
    a_r,
    sl_s,
    sl_r,
    b_s,
    b_r,
    p_s,
    p_r,
    k_s,
    k_r,
    kx_s,
    kx_r,
    q_s,
    q_r,
    do_s,
    do_r,
    at_s,
    at_r,
    rs_s,
    rs_r,
    g_s,
    g_r,
    gq_s,
    gq_r,
    ws_s,
    ws_r,
    w15_s,
    w15_r,
    w2_s,
    w2_r,
):
    back_send = (back_send_0, back_send_1, back_send_2)
    back_recv = (back_recv_0, back_recv_1, back_recv_2)
    i = lax.axis_index("seq")
    j = lax.axis_index("clip")
    x = i // 8
    y = (i // 2) % 4
    c = i % 2
    g = i % 8
    xp, xm, x2 = (x + 1) % 4, (x + 3) % 4, (x + 2) % 4
    yp, ym, y2 = (y + 1) % 4, (y + 3) % 4, (y + 2) % 4

    def seq_dev(dx, dy, dc):
        return {"seq": dx * 8 + dy * 2 + dc}

    xs = (x, xp, x2, xm)
    ys = (y, yp, y2, ym)
    cs = (c, 1 - c)
    clip_peers = [xs[a] * 8 + ys[b] * 2 + cs[d] for a, b, d in FAR_FIRST]
    group_peers = [ys[b] * 2 + cs[d] for a, b, d in FAR_FIRST if a == 0]

    def rcopy(src, dst, ss, rs, dev):
        return pltpu.make_async_remote_copy(
            src_ref=src, dst_ref=dst, send_sem=ss, recv_sem=rs, device_id=dev, device_id_type=MESH
        )

    loads = [
        pltpu.make_async_copy(a, b, in_sem.at[n])
        for n, (a, b) in enumerate(
            (
                (segment_hbm, segment),
                (shard_hbm, dest_shard),
                (slot_hbm, dest_slot),
                (patches_hbm.at[0], patches),
                (w_hbm, w_all),
                (grad_hbm.at[0], out_grad),
            )
        )
    ]
    for load in loads:
        load.start()

    to_pal = seq_dev(x, y, 1 - c)
    h_g = y * 2 + 1 - c

    def seven(src, dst, ss, rs):
        return rcopy(src.at[pl.ds(0, 7)], dst.at[pl.ds(0, 7)], ss, rs, to_pal)

    barrier = pltpu.get_barrier_semaphore()

    for peer in clip_peers:
        pl.semaphore_signal(barrier, inc=1, device_id={"seq": peer}, device_id_type=MESH)
    for k in range(1, n_clip):
        pl.semaphore_signal(
            barrier, inc=1, device_id={"clip": lax.rem(j + k, n_clip)}, device_id_type=MESH
        )

    for load in loads[0:3]:
        load.wait()
    seg = segment[...]
    tgt = dest_shard[...]
    slot = dest_slot[...]
    hit = iota((192, 196), 0) == seg
    member = onehot(hit)
    counts = jnp.sum(jnp.where(hit, 1.0, 0.0), axis=1, keepdims=True)
    to_shard = iota((NSEQ, 192), 0) == tgt
    shard_hot = onehot(to_shard)
    earlier = onehot(iota((192, 192), 0) < iota((192, 192), 1))
    before = mm(shard_hot, earlier)
    rank = jnp.sum(jnp.where(to_shard, before, 0.0), axis=0, keepdims=True)
    position = jnp.where(tgt >= 0, tgt.astype(F32) * CAP + rank, -1.0)
    chooser = onehot(iota((NMSG, 192), 0).astype(F32) == position)
    slot_rows = jnp.where(
        iota((128, 192), 0).astype(F32) == rank, slot.astype(F32) + 1.0, 0.0
    ).astype(BF)
    slot_table = mm_nt(shard_hot, slot_rows).astype(BF)
    spread = onehot(iota((NMSG, NSEQ), 0) == iota((NMSG, NSEQ), 1) * CAP + TOP)
    slot_cells = mm(spread, slot_table)
    loads[3].wait()
    sums = mm(member, patches[...])
    tokens = (sums * (1.0 / jnp.maximum(counts, 1.0))).astype(BF)
    rows = mm(chooser, tokens)
    send[:, :, 0:128] = (rows[:, 0:128] + slot_cells).reshape(NSEQ, CAP, 128).astype(BF)
    send[:, :, 128:] = rows[:, 128:].reshape(NSEQ, CAP, D - 128).astype(BF)

    pl.semaphore_wait(barrier, NSEQ - 1 + n_clip - 1)

    def slot_copy(peer, lands):
        part = (pl.ds(TOP, 2), pl.ds(0, 128))
        return rcopy(
            send.at[(peer, *part)], recv.at[(lands, *part)], sl_s, sl_r, {"seq": peer}
        )

    def slot_all():
        part = (pl.ds(0, NSEQ - 1), pl.ds(TOP, 2), pl.ds(0, 128))
        return rcopy(send.at[part], recv.at[part], sl_s, sl_r, to_pal)

    def token_copy(peer, lands):
        return rcopy(
            send.at[peer, pl.ds(0, TOP)],
            recv.at[lands, pl.ds(0, TOP)],
            a_s,
            a_r,
            {"seq": peer},
        )

    for peer in clip_peers:
        slot_copy(peer, i).start()
        token_copy(peer, i).start()

    recv[i] = send[i]

    picker[...] = mm(chooser, member).astype(BF)
    per_patch = mm_tn(member, jnp.broadcast_to(counts, (192, 128)).astype(BF))
    count_inv[...] = 1.0 / per_patch
    loads[5].wait()
    for blk in range(4):
        pair = out_grad[:, blk * 128 : blk * 128 + 128].astype(F32)
        top, low = pair[0:32], pair[32:64]
        do_send[2 * blk] = merge_low(top, low).astype(BF)
        do_send[2 * blk + 1] = merge_high(top, low).astype(BF)
    loads[4].wait()

    def token_all():
        part = (pl.ds(0, NSEQ - 1), pl.ds(0, TOP))
        return rcopy(send.at[part], recv.at[part], a_s, a_r, to_pal)

    slot_all().wait_recv()
    token_all().wait_recv()

    full = iota((NSEQ, CAP, D), 1) < TOP
    came = jnp.where(full, recv[...].astype(F32), 0.0).reshape(NMSG, D).astype(BF)
    cells = recv[:, :, 0:128].astype(F32).reshape(NMSG, 128).astype(BF)
    col = iota((NMSG, NMSG), 1)
    from_row = onehot(iota((NMSG, NMSG), 0) == (col // CAP) * CAP + TOP)
    slot_sq = mm_tn(cells, from_row)[0:8]
    rank_of = iota((8, NMSG), 1) % CAP
    wanted = (iota((8, NMSG), 0) == rank_of) & (rank_of < TOP)
    slot_row = jnp.sum(jnp.where(wanted, slot_sq, 0.0), axis=0, keepdims=True)
    placer = onehot((iota((R, NMSG), 0) + 1).astype(F32) == slot_row)
    placer_ref[...] = placer
    placed = mm(placer, came).astype(BF)
    pq[g] = placed

    def kx_copy(peer, lands):
        return rcopy(
            kv_send.at[peer],
            kv.at[x, pl.ds(pl.multiple_of(lands * R, R), R)],
            kx_s,
            kx_r,
            {"seq": x * 8 + peer},
        )

    def q_copy(peer, lands):
        return rcopy(q_send.at[peer], q_recv.at[lands], q_s, q_r, {"seq": x * 8 + peer})

    def do_copy(peer, lands):
        return rcopy(do_send.at[peer], do_recv.at[lands], do_s, do_r, {"seq": x * 8 + peer})

    def half_up(v):
        return v.astype(BF).astype(F32)

    def w_cols(at, pair):
        return w_all[:, pl.ds(pl.multiple_of(at + pair * 128, 128), 128)]

    for pair in (y2, yp, ym, y):
        w_pair = jnp.concatenate([w_cols(INNER, pair), w_cols(2 * INNER, pair)], axis=1)
        proj = half_up(mm(placed, w_pair))
        k_blk, v_blk = proj[:, 0:128], proj[:, 128:256]
        kv_send[2 * pair] = merge_low(k_blk, v_blk).astype(BF)
        kv_send[2 * pair + 1] = merge_high(k_blk, v_blk).astype(BF)
        if pair is y:
            kx_copy(h_g, g).start()
        else:
            kx_copy(2 * pair + c, g).start()
            kx_copy(2 * pair + 1 - c, g).start()
    kv[x, pl.ds(pl.multiple_of(g * R, R), R)] = kv_send[g]
    proj_q = half_up(mm(placed, w_all[:, 0:INNER])) * 0.125
    for blk in range(4):
        q_blk = proj_q[:, blk * 128 : blk * 128 + 128]
        q_send[2 * blk] = merge_low(q_blk[0:32], q_blk[32:64]).astype(BF)
        q_send[2 * blk + 1] = merge_high(q_blk[0:32], q_blk[32:64]).astype(BF)
    for peer in group_peers:
        q_copy(peer, g).start()
    for peer in group_peers:
        do_copy(peer, g).start()
    q_recv[g] = q_send[g]
    do_recv[g] = do_send[g]

    g_p, g_m, g_2 = yp * 2 + c, ym * 2 + c, y2 * 2 + c
    A, B = pl.ds(0, 32), pl.ds(32, 32)
    to_yp, to_ym = seq_dev(x, yp, c), seq_dev(x, ym, c)

    def p_copy(n, s, half, dev):
        ref = pq.at[s] if half is None else pq.at[s, half]
        return rcopy(ref, ref, p_s, p_r.at[n], dev)

    h_p, h_m, h_2 = yp * 2 + 1 - c, ym * 2 + 1 - c, y2 * 2 + 1 - c

    def gather_first():
        p_copy(0, g, A, to_yp).start()
        p_copy(1, g, B, to_ym).start()
        p_copy(2, g, B, to_yp).start()
        p_copy(3, g, A, to_ym).start()
        p_copy(4, g, None, to_pal).start()

    def gather_second():
        p_copy(0, g_m, A, to_yp).wait_recv()
        p_copy(5, g_m, A, to_yp).start()
        p_copy(6, g_m, A, to_pal).start()
        p_copy(1, g_p, B, to_ym).wait_recv()
        p_copy(7, g_p, B, to_ym).start()
        p_copy(8, g_p, B, to_pal).start()
        p_copy(2, g_m, B, to_yp).wait_recv()
        p_copy(9, g_m, B, to_pal).start()
        p_copy(3, g_p, A, to_ym).wait_recv()
        p_copy(10, g_p, A, to_pal).start()

    def gather_third():
        p_copy(5, g_2, A, to_yp).wait_recv()
        p_copy(11, g_2, A, to_pal).start()
        p_copy(7, g_2, B, to_ym).wait_recv()
        p_copy(12, g_2, B, to_pal).start()

    def gather_last():
        p_copy(4, h_g, None, to_pal).wait_recv()
        p_copy(6, h_m, A, to_pal).wait_recv()
        p_copy(8, h_p, B, to_pal).wait_recv()
        p_copy(9, h_m, B, to_pal).wait_recv()
        p_copy(10, h_p, A, to_pal).wait_recv()
        p_copy(11, h_2, A, to_pal).wait_recv()
        p_copy(12, h_2, B, to_pal).wait_recv()

    def kx_all():
        part = pl.ds(0, 7 * R)
        return rcopy(kv.at[x, part], kv.at[x, part], kx_s, kx_r, to_pal)

    kx_all().wait_recv()
    KA, KB = pl.ds(0, 256), pl.ds(256, 256)
    to_xp, to_xm = seq_dev(xp, y, c), seq_dev(xm, y, c)

    def k_copy(n, s, half, dev):
        ref = kv.at[s, half]
        return rcopy(ref, ref, k_s, k_r.at[n], dev)

    k_copy(0, x, KA, to_xp).start()
    k_copy(1, x, KB, to_xm).start()
    k_copy(2, x, KB, to_xp).start()
    k_copy(3, x, KA, to_xm).start()

    seven(q_send, q_recv, q_s, q_r).wait_recv()
    gather_first()
    q_in = q_recv[...].astype(F32)
    low = half_lanes((8, 32, 128))
    q_rows = jnp.concatenate([jnp.where(low, q_in, 0.0), jnp.where(low, swap(q_in), 0.0)], axis=1)
    qpad[...] = q_rows.reshape(QROWS, 128).astype(BF)

    def forward(s, n):
        kvt[n] = kv[s].astype(F32).T.astype(BF)
        for q in range(QROWS // QC):
            qs = slice(q * QC, q * QC + QC)
            scores = mm_nt(kv[s], qpad[qs, :])
            top = jnp.max(scores, axis=0, keepdims=True)
            w = jnp.exp(scores - top)
            stat_max[n, :, qs] = top
            stat_sum[n, :, qs] = jnp.sum(w, axis=0, keepdims=True)
            weights[n, :, qs] = w
            part_out[n, :, qs] = mm(kvt[n], w.astype(BF))

    forward(x, 0)
    seven(do_send, do_recv, do_s, do_r).wait_recv()
    d_in = do_recv[...].astype(F32)
    d_rows = jnp.concatenate(
        [jnp.where(low, 0.0, swap(d_in)), jnp.where(low, 0.0, d_in)], axis=1
    ).reshape(QROWS, 128)
    dopad[...] = d_rows.astype(BF)
    dot_ref[...] = d_rows.T

    k_copy(0, xm, KA, to_xp).wait_recv()
    k_copy(4, xm, KA, to_xp).start()
    k_copy(1, xp, KB, to_xm).wait_recv()
    k_copy(5, xp, KB, to_xm).start()
    k_copy(2, xm, KB, to_xp).wait_recv()
    forward(xm, 1)
    k_copy(3, xp, KA, to_xm).wait_recv()
    forward(xp, 2)

    k_copy(4, x2, KA, to_xp).wait_recv()
    k_copy(5, x2, KB, to_xm).wait_recv()
    forward(x2, 3)

    best = jnp.maximum(
        jnp.maximum(stat_max[0], stat_max[1]), jnp.maximum(stat_max[2], stat_max[3])
    )
    facs = [jnp.exp(stat_max[n] - best) for n in range(4)]
    total = sum(facs[n] * stat_sum[n] for n in range(4))
    att_t = sum(facs[n] * part_out[n] for n in range(4)) / total
    att_half = att_t.astype(BF).astype(F32)
    gd_ref[...] = jnp.sum(att_half[64:128] * dot_ref[64:128], axis=0, keepdims=True)
    for n in range(4):
        fac_ref[n] = facs[n] / total
    att3 = att_half.T.reshape(8, R, 128)
    att_send[...] = merge_high(att3[:, 0:32], att3[:, 32:64]).astype(BF)

    def at_copy(peer, lands):
        return rcopy(att_send.at[peer], att_recv.at[lands], at_s, at_r, {"seq": x * 8 + peer})

    for peer in group_peers:
        at_copy(peer, g).start()

    att_recv[g] = att_send[g]

    dq_acc[...] = jnp.zeros((128, QROWS), F32)

    def backward(s, n):
        for q in range(QROWS // QC):
            qs = slice(q * QC, q * QC + QC)
            prob_grad = mm_nt(kv[s], dopad[qs, :])
            prob = weights[n, :, qs] * fac_ref[n, :, qs]
            score_grad = (prob * (prob_grad - gd_ref[:, qs])).astype(BF)
            upd = mm(score_grad, qpad[qs, :]) + mm(prob.astype(BF), dopad[qs, :])
            if q == 0:
                dkv_acc[n] = upd
            else:
                dkv_acc[n] += upd
            dq_acc[:, qs] += mm(kvt[n], score_grad)

    def ring_sum(sends, recvs, ss, rs, part, rows):
        half = rows // 2

        def copy(n, dev):
            return rcopy(sends.at[n], recvs.at[n], ss, rs.at[n], dev)

        def put(n, value, dev):
            sends[n] = value.astype(BF)
            copy(n, dev).start()

        def first():
            put(0, part(x2, 3, slice(0, half)), to_xp)
            put(1, part(x2, 3, slice(half, rows)), to_xm)

        def second():
            put(2, part(xp, 2, slice(half, rows)), to_xp)

        def third():
            put(3, part(xm, 1, slice(0, half)), to_xm)

        def fourth():
            copy(0, to_xp).wait_recv()
            put(4, part(xp, 2, slice(0, half)) + recvs[0].astype(F32), to_xp)
            copy(1, to_xm).wait_recv()
            put(5, part(xm, 1, slice(half, rows)) + recvs[1].astype(F32), to_xm)

        def fifth():
            for n, dev in ((2, to_xp), (3, to_xm), (4, to_xp), (5, to_xm)):
                copy(n, dev).wait_recv()
            up = recvs[4].astype(F32) + recvs[3].astype(F32)
            down = recvs[2].astype(F32) + recvs[5].astype(F32)
            return part(x, 0, slice(0, rows)) + jnp.concatenate([up, down], axis=0)

        def sent():
            rcopy(sends, recvs, ss, rs.at[0], to_xp).wait_send()

        return first, second, third, fourth, fifth, sent

    rs = ring_sum(rs_send, rs_recv, rs_s, rs_r, lambda s, n, part: dkv_acc[n, part], QROWS)
    backward(x2, 3)
    rs[0]()
    gather_second()
    backward(xp, 2)
    rs[1]()
    backward(xm, 1)
    rs[2]()
    backward(x, 0)
    rs[3]()
    dq_rows = jnp.where(half_lanes((QROWS, 128)), dq_acc[...].T * 0.125, 0.0)
    dq3 = dq_rows.reshape(8, R, 128)
    gq_send[...] = merge_low(dq3[:, 0:32], dq3[:, 32:64]).astype(BF)

    def gq_copy(peer, lands):
        return rcopy(gq_send.at[peer], gq_recv.at[lands], gq_s, gq_r, {"seq": x * 8 + peer})

    def g_copy(peer, lands):
        return rcopy(g_send.at[peer], g_recv.at[lands], g_s, g_r, {"seq": x * 8 + peer})

    for peer in group_peers:
        gq_copy(peer, g).start()

    gq_recv[g] = gq_send[g]
    gather_third()
    dkv = rs[4]().astype(BF)
    g_send[...] = dkv.reshape(8, R, 128)

    for peer in group_peers:
        g_copy(peer, g).start()

    g_recv[g] = g_send[g]

    gather_last()
    grads = jnp.concatenate([dkv, dq_rows.astype(BF)], axis=1)
    w_part = mm_tn(grads, pq[...].reshape(QROWS, D))
    for q in range(4):
        wblk[q] = w_part[0:192, q * 256 : q * 256 + 256]

    ws = ring_sum(ws_send, ws_recv, ws_s, ws_r, lambda s, n, part: wblk[s, part], 192)
    for step in ws[0:3]:
        step()

    seven(att_send, att_recv, at_s, at_r).wait_recv()
    stores = [
        pltpu.make_async_copy(a, b, out_sem.at[n])
        for n, (a, b) in enumerate(
            ((att_out, att_hbm.at[0]), (patch_out, patch_hbm.at[0]), (weight_out, weight_hbm))
        )
    ]
    for blk in range(4):
        a0 = att_recv[2 * blk].astype(F32)
        a1 = att_recv[2 * blk + 1].astype(F32)
        lanes = slice(blk * 128, blk * 128 + 128)
        att_out[0:32, lanes] = merge_low(a0, a1).astype(BF)
        att_out[32:64, lanes] = merge_high(a0, a1).astype(BF)
    stores[0].start()

    ws[3]()

    def lane_block(n):
        return slice(n * 128, n * 128 + 128)

    seven(gq_send, gq_recv, gq_s, gq_r).wait_recv()
    for blk in range(4):
        r0 = gq_recv[2 * blk].astype(F32)
        r1 = gq_recv[2 * blk + 1].astype(F32)
        gnat[0:32, lane_block(blk)] = merge_low(r0, r1).astype(BF)
        gnat[32:64, lane_block(blk)] = merge_high(r0, r1).astype(BF)
    pg_acc[...] = mm_nt(gnat[:, 0:INNER], w_all[:, 0:INNER])
    seven(g_send, g_recv, g_s, g_r).wait_recv()
    for blk in range(4):
        r0 = g_recv[2 * blk].astype(F32)
        r1 = g_recv[2 * blk + 1].astype(F32)
        gnat[:, lane_block(blk + 4)] = merge_low(r0, r1).astype(BF)
        gnat[:, lane_block(blk + 8)] = merge_high(r0, r1).astype(BF)

    def back_copy(h, peer, lands):
        return rcopy(
            back_send[h].at[peer, pl.ds(0, TOP)],
            back_recv[h].at[lands, pl.ds(0, TOP)],
            b_s.at[h],
            b_r.at[h],
            {"seq": peer},
        )

    def back_all(h):
        part = (pl.ds(0, NSEQ - 1), pl.ds(0, TOP))
        return rcopy(
            back_send[h].at[part], back_recv[h].at[part], b_s.at[h], b_r.at[h], to_pal
        )

    def make_back(h):
        start, size = PARTS[h]
        cols = slice(start, start + size)
        grad = pg_acc[:, cols] + mm_nt(gnat[:, INNER:], w_all[cols, INNER:])
        back = mm_tn(placer_ref[...], grad.astype(BF))
        back_send[h][...] = back.reshape(NSEQ, CAP, size).astype(BF)

    def send_back(h):
        for peer in clip_peers:
            back_copy(h, peer, i).start()

        back_recv[h][i] = back_send[h][i]

    make_back(0)
    send_back(0)

    w_sum = ws[4]()
    w_kv = w_sum[0:128].T.reshape(8, 32, 128)
    w_qq = jnp.concatenate([w_sum[128:192], jnp.zeros((64, 256), F32)], axis=0)
    w_qq = w_qq.T.reshape(8, 32, 128)
    w15_send[:, 0:32] = w_kv.astype(BF)
    w15_send[:, 32:48] = merge_low(w_qq[:, 0:16], w_qq[:, 16:32]).astype(BF)

    def w15_copy(peer, lands):
        return rcopy(
            w15_send.at[peer], w15_recv.at[lands], w15_s, w15_r, {"seq": x * 8 + peer}
        )

    for peer in group_peers:
        w15_copy(peer, g).start()

    w15_recv[g] = w15_send[g]

    make_back(1)
    send_back(1)
    make_back(2)

    seven(w15_send, w15_recv, w15_s, w15_r).wait_recv()
    q_blocks, k_blocks, v_blocks = [], [], []
    for blk in range(4):
        r0 = w15_recv[2 * blk].astype(F32)
        r1 = w15_recv[2 * blk + 1].astype(F32)
        q_blocks.append(
            jnp.concatenate(
                [merge_low(r0[32:48], r1[32:48]), merge_high(r0[32:48], r1[32:48])], axis=0
            )
        )
        k_blocks.append(merge_low(r0[0:32], r1[0:32]))
        v_blocks.append(merge_high(r0[0:32], r1[0:32]))
    blocks = q_blocks + k_blocks + v_blocks
    width = 3 * INNER // n_clip
    for n in range(n_clip):
        b, off = divmod(width * n, 128)
        if off == 0:
            piece = blocks[b]
        else:
            turn = 128 - off
            piece = pltpu.roll(blocks[b], turn, 1)
            if off + width > 128:
                piece = jnp.where(
                    iota((32, 128), 1) < turn, piece, pltpu.roll(blocks[b + 1], turn, 1)
                )
        tail = piece[24:32]
        last = jnp.concatenate(
            [pltpu.roll(tail, 96, 1), pltpu.roll(tail, 64, 1), pltpu.roll(tail, 32, 1)], axis=0
        )
        w2_send[n] = jnp.where(iota((24, 128), 1) < width, piece[0:24], last).astype(BF)

    def w2_copy(peer, lands):
        return rcopy(w2_send.at[peer], w2_recv.at[lands], w2_s, w2_r, {"clip": peer})

    def w2_all():
        part = pl.ds(0, n_clip - 1)
        return rcopy(w2_send.at[part], w2_recv.at[part], w2_s, w2_r, to_pal)

    @pl.loop(1, n_clip)
    def _(k):
        w2_copy((j + k) % n_clip, j).start()

    w2_recv[j] = w2_send[j]
    send_back(2)

    for h, (start, size) in enumerate(PARTS):
        back_all(h).wait_recv()
        some = iota((NSEQ, CAP, size), 1) < TOP
        returned = jnp.where(some, back_recv[h][...].astype(F32), 0.0).reshape(NMSG, size)
        patch_rows = mm_tn(picker[...], returned.astype(BF))
        patch_out[:, start : start + size] = (patch_rows * count_inv[:, 0:1]).astype(BF)

    stores[1].start()

    w2_all().wait_recv()
    w_rows = jnp.sum(w2_recv[...].astype(F32), axis=0)
    weight_out[0:24] = w_rows[:, 0:width]
    lane = iota((8, 128), 1)
    tail = jnp.where(
        lane < 32,
        pltpu.roll(w_rows[0:8], 32, 1),
        jnp.where(lane < 64, pltpu.roll(w_rows[8:16], 64, 1), pltpu.roll(w_rows[16:24], 96, 1)),
    )
    weight_out[24:32] = tail[:, 0:width]
    stores[2].start()

    slot_all().wait_send()
    token_all().wait_send()
    for h in range(len(PARTS)):
        back_all(h).wait_send()
    kx_all().wait_send()
    seven(q_send, q_recv, q_s, q_r).wait_send()
    seven(do_send, do_recv, do_s, do_r).wait_send()
    seven(att_send, att_recv, at_s, at_r).wait_send()
    seven(g_send, g_recv, g_s, g_r).wait_send()
    seven(gq_send, gq_recv, gq_s, gq_r).wait_send()
    seven(w15_send, w15_recv, w15_s, w15_r).wait_send()
    w2_all().wait_send()
    seven(pq, pq, p_s, p_r.at[0]).wait_send()
    rcopy(kv.at[pl.ds(0, 3)], kv.at[pl.ds(0, 3)], k_s, k_r.at[0], to_xp).wait_send()
    rs[5]()
    ws[5]()
    for store in stores:
        store.wait()


def hand_over(att, patch, weight, att_out, patch_out, weight_out, sems):
    pairs = ((patch, patch_out), (att, att_out), (weight, weight_out))
    moves = [pltpu.make_async_copy(a, b, sems.at[n]) for n, (a, b) in enumerate(pairs)]
    for move in moves:
        move.start()
    for move in moves:
        move.wait()


def local(patches, segment, dest_shard, dest_slot, w_qkv, out_grad):
    n_clip = lax.axis_size("clip")
    v = pltpu.VMEM
    dma = pltpu.SemaphoreType.DMA
    scratch = [
        v((196, D), BF),
        v((1, 196), I32),
        v((1, 192), I32),
        v((1, 192), I32),
        v((R, INNER), BF),
        v((R, INNER), BF),
        v((196, D), BF),
        v((32, 3 * INNER // n_clip), F32),
        v((NSEQ, CAP, D), BF),
        v((NSEQ, CAP, D), BF),
        *[v((NSEQ, CAP, size), BF) for _, size in PARTS],
        *[v((NSEQ, CAP, size), BF) for _, size in PARTS],
        v((D, 3 * INNER), BF),
        v((NMSG, 196), BF),
        v((R, NMSG), BF),
        v((196, 128), F32),
        v((8, R, D), BF),
        v((4, QROWS, 128), BF),
        v((4, 128, QROWS), BF),
        v((QROWS, 128), BF),
        v((QROWS, 128), BF),
        v((128, QROWS), F32),
        v((8, R, 128), BF),
        v((8, 32, 128), BF),
        v((8, 32, 128), BF),
        v((8, 32, 128), BF),
        v((8, 32, 128), BF),
        v((4, QROWS, QROWS), F32),
        v((4, 128, QROWS), F32),
        v((4, 1, QROWS), F32),
        v((4, 1, QROWS), F32),
        v((4, 1, QROWS), F32),
        v((1, QROWS), F32),
        v((8, 32, 128), BF),
        v((8, 32, 128), BF),
        v((4, QROWS, 128), F32),
        v((128, QROWS), F32),
        v((6, 256, 128), BF),
        v((6, 256, 128), BF),
        v((8, R, 128), BF),
        v((8, R, 128), BF),
        v((8, 32, 128), BF),
        v((8, 32, 128), BF),
        v((R, 3 * INNER), BF),
        v((R, D), F32),
        v((4, 192, 256), F32),
        v((6, 96, 256), BF),
        v((6, 96, 256), BF),
        v((8, 48, 128), BF),
        v((8, 48, 128), BF),
        v((n_clip, 24, 128), BF),
        v((n_clip, 24, 128), BF),
        dma((6,)),
        dma((3,)),
        dma,
        dma,
        dma,
        dma,
        dma((3,)),
        dma((3,)),
        dma,
        dma((13,)),
        dma,
        dma((6,)),
        dma,
        dma,
        dma,
        dma,
        dma,
        dma,
        dma,
        dma,
        dma,
        dma((6,)),
        dma,
        dma,
        dma,
        dma,
        dma,
        dma((6,)),
        dma,
        dma,
        dma,
        dma,
    ]
    anywhere = pl.BlockSpec(memory_space=pl.ANY)
    shapes = (
        jax.ShapeDtypeStruct((1, R, INNER), BF),
        jax.ShapeDtypeStruct((1, 196, D), BF),
        jax.ShapeDtypeStruct((32, 3 * INNER // n_clip), F32),
    )
    operands = (patches, segment, dest_shard, dest_slot, w_qkv, out_grad)
    results = pl.pallas_call(
        functools.partial(kernel, n_clip),
        out_shape=shapes,
        in_specs=[anywhere] * 6,
        out_specs=(anywhere,) * 3,
        scratch_shapes=scratch,
        compiler_params=pltpu.CompilerParams(
            collective_id=0, has_side_effects=True, vmem_limit_bytes=40 * 1024 * 1024
        ),
        name="rebalance_attention",
    )(*[pltpu.with_memory_space_constraint(a, pltpu.HBM) for a in operands])
    return pl.pallas_call(
        hand_over,
        out_shape=shapes,
        in_specs=[anywhere] * 3,
        out_specs=(anywhere,) * 3,
        scratch_shapes=[dma((3,))],
        compiler_params=pltpu.CompilerParams(vmem_limit_bytes=2 * 1024 * 1024),
        name="hand_over",
    )(*results)


def solution(mesh):
    return jax.shard_map(
        local,
        mesh=mesh,
        in_specs=(
            P("clip", "seq", None),
            P("clip", "seq"),
            P("clip", "seq"),
            P("clip", "seq"),
            P(),
            P("clip", "seq", None),
        ),
        out_specs=(P("clip", "seq", None), P("clip", "seq", None), P("seq", "clip")),
        check_vma=False,
    )
```

```python
import functools

import jax
import jax.numpy as jnp
from jax import lax
from jax.experimental import pallas as pl
from jax.experimental.pallas import tpu as pltpu
from jax.sharding import PartitionSpec as P

BF = jnp.bfloat16
F32 = jnp.float32
I32 = jnp.int32
MESH = pl.DeviceIdType.MESH

D = 1024
INNER = 512
R = 64
NSEQ = 32
CAP = 8
NMSG = NSEQ * CAP
QROWS = 512
QC = 256
TOP = 6
PARTS = ((0, 256), (256, 640), (896, 128))
HOPS_X = (0, 1, 2, 1)
HOPS_Y = (0, 2, 4, 2)
FAR_FIRST = sorted(
    ((a, b, d) for a in range(4) for b in range(4) for d in range(2) if a or b or d),
    key=lambda t: -(HOPS_X[t[0]] + HOPS_Y[t[1]]),
)


def iota(shape, dim):
    return lax.broadcasted_iota(I32, shape, dim)


def onehot(cond):
    return jnp.where(cond, 1.0, 0.0).astype(BF)


def mm(a, b):
    return jnp.dot(a, b, preferred_element_type=F32)


def mm_nt(a, b):
    return lax.dot_general(a, b, (((1,), (1,)), ((), ())), preferred_element_type=F32)


def mm_tn(a, b):
    return lax.dot_general(a, b, (((0,), (0,)), ((), ())), preferred_element_type=F32)


def half_lanes(shape):
    return iota(shape, len(shape) - 1) < 64


def swap(v):
    return pltpu.roll(v, 64, v.ndim - 1)


def merge_low(a, b):
    return jnp.where(half_lanes(a.shape), a, swap(b))


def merge_high(a, b):
    return jnp.where(half_lanes(a.shape), swap(a), b)


def kernel(
    n_clip,
    patches_hbm,
    segment_hbm,
    shard_hbm,
    slot_hbm,
    w_hbm,
    grad_hbm,
    att_hbm,
    patch_hbm,
    weight_hbm,
    patches,
    segment,
    dest_shard,
    dest_slot,
    out_grad,
    att_out,
    patch_out,
    weight_out,
    send,
    recv,
    back_send_0,
    back_send_1,
    back_send_2,
    back_recv_0,
    back_recv_1,
    back_recv_2,
    w_all,
    picker,
    placer_ref,
    count_inv,
    pq,
    kv,
    kvt,
    qpad,
    dopad,
    dot_ref,
    kv_send,
    q_send,
    q_recv,
    do_send,
    do_recv,
    weights,
    part_out,
    stat_max,
    stat_sum,
    fac_ref,
    gd_ref,
    att_send,
    att_recv,
    dkv_acc,
    dq_acc,
    rs_send,
    rs_recv,
    g_send,
    g_recv,
    gq_send,
    gq_recv,
    gnat,
    pg_acc,
    wblk,
    ws_send,
    ws_recv,
    w15_send,
    w15_recv,
    w2_send,
    w2_recv,
    in_sem,
    out_sem,
    a_s,
    a_r,
    sl_s,
    sl_r,
    b_s,
    b_r,
    p_s,
    p_r,
    k_s,
    k_r,
    kx_s,
    kx_r,
    q_s,
    q_r,
    do_s,
    do_r,
    at_s,
    at_r,
    rs_s,
    rs_r,
    g_s,
    g_r,
    gq_s,
    gq_r,
    ws_s,
    ws_r,
    w15_s,
    w15_r,
    w2_s,
    w2_r,
):
    back_send = (back_send_0, back_send_1, back_send_2)
    back_recv = (back_recv_0, back_recv_1, back_recv_2)
    i = lax.axis_index("seq")
    j = lax.axis_index("clip")
    x = i // 8
    y = (i // 2) % 4
    c = i % 2
    g = i % 8
    xp, xm, x2 = (x + 1) % 4, (x + 3) % 4, (x + 2) % 4
    yp, ym, y2 = (y + 1) % 4, (y + 3) % 4, (y + 2) % 4

    def seq_dev(dx, dy, dc):
        return {"seq": dx * 8 + dy * 2 + dc}

    xs = (x, xp, x2, xm)
    ys = (y, yp, y2, ym)
    cs = (c, 1 - c)
    clip_peers = [xs[a] * 8 + ys[b] * 2 + cs[d] for a, b, d in FAR_FIRST]
    group_peers = [ys[b] * 2 + cs[d] for a, b, d in FAR_FIRST if a == 0]

    def rcopy(src, dst, ss, rs, dev):
        return pltpu.make_async_remote_copy(
            src_ref=src, dst_ref=dst, send_sem=ss, recv_sem=rs, device_id=dev, device_id_type=MESH
        )

    loads = [
        pltpu.make_async_copy(a, b, in_sem.at[n])
        for n, (a, b) in enumerate(
            (
                (segment_hbm, segment),
                (shard_hbm, dest_shard),
                (slot_hbm, dest_slot),
                (patches_hbm.at[0], patches),
                (w_hbm, w_all),
                (grad_hbm.at[0], out_grad),
            )
        )
    ]
    for load in loads:
        load.start()

    to_pal = seq_dev(x, y, 1 - c)
    h_g = y * 2 + 1 - c

    def seven(src, dst, ss, rs):
        return rcopy(src.at[pl.ds(0, 7)], dst.at[pl.ds(0, 7)], ss, rs, to_pal)

    barrier = pltpu.get_barrier_semaphore()

    for peer in clip_peers:
        pl.semaphore_signal(barrier, inc=1, device_id={"seq": peer}, device_id_type=MESH)
    for k in range(1, n_clip):
        pl.semaphore_signal(
            barrier, inc=1, device_id={"clip": lax.rem(j + k, n_clip)}, device_id_type=MESH
        )

    for load in loads[0:3]:
        load.wait()
    seg = segment[...]
    tgt = dest_shard[...]
    slot = dest_slot[...]
    hit = iota((192, 196), 0) == seg
    member = onehot(hit)
    counts = jnp.sum(jnp.where(hit, 1.0, 0.0), axis=1, keepdims=True)
    to_shard = iota((NSEQ, 192), 0) == tgt
    shard_hot = onehot(to_shard)
    earlier = onehot(iota((192, 192), 0) < iota((192, 192), 1))
    before = mm(shard_hot, earlier)
    rank = jnp.sum(jnp.where(to_shard, before, 0.0), axis=0, keepdims=True)
    position = jnp.where(tgt >= 0, tgt.astype(F32) * CAP + rank, -1.0)
    chooser = onehot(iota((NMSG, 192), 0).astype(F32) == position)
    slot_rows = jnp.where(
        iota((128, 192), 0).astype(F32) == rank, slot.astype(F32) + 1.0, 0.0
    ).astype(BF)
    slot_table = mm_nt(shard_hot, slot_rows).astype(BF)
    spread = onehot(iota((NMSG, NSEQ), 0) == iota((NMSG, NSEQ), 1) * CAP + TOP)
    slot_cells = mm(spread, slot_table)
    loads[3].wait()
    sums = mm(member, patches[...])
    tokens = (sums * (1.0 / jnp.maximum(counts, 1.0))).astype(BF)
    rows = mm(chooser, tokens)
    send[:, :, 0:128] = (rows[:, 0:128] + slot_cells).reshape(NSEQ, CAP, 128).astype(BF)
    send[:, :, 128:] = rows[:, 128:].reshape(NSEQ, CAP, D - 128).astype(BF)

    pl.semaphore_wait(barrier, NSEQ - 1 + n_clip - 1)

    def slot_copy(peer, lands):
        part = (pl.ds(TOP, 2), pl.ds(0, 128))
        return rcopy(
            send.at[(peer, *part)], recv.at[(lands, *part)], sl_s, sl_r, {"seq": peer}
        )

    def slot_all():
        part = (pl.ds(0, NSEQ - 1), pl.ds(TOP, 2), pl.ds(0, 128))
        return rcopy(send.at[part], recv.at[part], sl_s, sl_r, to_pal)

    def token_copy(peer, lands):
        return rcopy(
            send.at[peer, pl.ds(0, TOP)],
            recv.at[lands, pl.ds(0, TOP)],
            a_s,
            a_r,
            {"seq": peer},
        )

    for peer in clip_peers:
        slot_copy(peer, i).start()
        token_copy(peer, i).start()

    recv[i] = send[i]

    picker[...] = mm(chooser, member).astype(BF)
    per_patch = mm_tn(member, jnp.broadcast_to(counts, (192, 128)).astype(BF))
    count_inv[...] = 1.0 / per_patch
    loads[5].wait()
    for blk in range(4):
        pair = out_grad[:, blk * 128 : blk * 128 + 128].astype(F32)
        top, low = pair[0:32], pair[32:64]
        do_send[2 * blk] = merge_low(top, low).astype(BF)
        do_send[2 * blk + 1] = merge_high(top, low).astype(BF)
    loads[4].wait()

    def token_all():
        part = (pl.ds(0, NSEQ - 1), pl.ds(0, TOP))
        return rcopy(send.at[part], recv.at[part], a_s, a_r, to_pal)

    slot_all().wait_recv()
    token_all().wait_recv()

    full = iota((NSEQ, CAP, D), 1) < TOP
    came = jnp.where(full, recv[...].astype(F32), 0.0).reshape(NMSG, D).astype(BF)
    cells = recv[:, :, 0:128].astype(F32).reshape(NMSG, 128).astype(BF)
    col = iota((NMSG, NMSG), 1)
    from_row = onehot(iota((NMSG, NMSG), 0) == (col // CAP) * CAP + TOP)
    slot_sq = mm_tn(cells, from_row)[0:8]
    rank_of = iota((8, NMSG), 1) % CAP
    wanted = (iota((8, NMSG), 0) == rank_of) & (rank_of < TOP)
    slot_row = jnp.sum(jnp.where(wanted, slot_sq, 0.0), axis=0, keepdims=True)
    placer = onehot((iota((R, NMSG), 0) + 1).astype(F32) == slot_row)
    placer_ref[...] = placer
    placed = mm(placer, came).astype(BF)
    pq[g] = placed

    def kx_copy(peer, lands):
        return rcopy(
            kv_send.at[peer],
            kv.at[x, pl.ds(pl.multiple_of(lands * R, R), R)],
            kx_s,
            kx_r,
            {"seq": x * 8 + peer},
        )

    def q_copy(peer, lands):
        return rcopy(q_send.at[peer], q_recv.at[lands], q_s, q_r, {"seq": x * 8 + peer})

    def do_copy(peer, lands):
        return rcopy(do_send.at[peer], do_recv.at[lands], do_s, do_r, {"seq": x * 8 + peer})

    def half_up(v):
        return v.astype(BF).astype(F32)

    def w_cols(at, pair):
        return w_all[:, pl.ds(pl.multiple_of(at + pair * 128, 128), 128)]

    for pair in (y2, yp, ym, y):
        w_pair = jnp.concatenate([w_cols(INNER, pair), w_cols(2 * INNER, pair)], axis=1)
        proj = half_up(mm(placed, w_pair))
        k_blk, v_blk = proj[:, 0:128], proj[:, 128:256]
        kv_send[2 * pair] = merge_low(k_blk, v_blk).astype(BF)
        kv_send[2 * pair + 1] = merge_high(k_blk, v_blk).astype(BF)
        if pair is y:
            kx_copy(h_g, g).start()
        else:
            kx_copy(2 * pair + c, g).start()
            kx_copy(2 * pair + 1 - c, g).start()
    kv[x, pl.ds(pl.multiple_of(g * R, R), R)] = kv_send[g]
    proj_q = half_up(mm(placed, w_all[:, 0:INNER])) * 0.125
    for blk in range(4):
        q_blk = proj_q[:, blk * 128 : blk * 128 + 128]
        q_send[2 * blk] = merge_low(q_blk[0:32], q_blk[32:64]).astype(BF)
        q_send[2 * blk + 1] = merge_high(q_blk[0:32], q_blk[32:64]).astype(BF)
    for peer in group_peers:
        q_copy(peer, g).start()
    for peer in group_peers:
        do_copy(peer, g).start()
    q_recv[g] = q_send[g]
    do_recv[g] = do_send[g]

    g_p, g_m, g_2 = yp * 2 + c, ym * 2 + c, y2 * 2 + c
    A, B = pl.ds(0, 32), pl.ds(32, 32)
    to_yp, to_ym = seq_dev(x, yp, c), seq_dev(x, ym, c)

    def p_copy(n, s, half, dev):
        ref = pq.at[s] if half is None else pq.at[s, half]
        return rcopy(ref, ref, p_s, p_r.at[n], dev)

    h_p, h_m, h_2 = yp * 2 + 1 - c, ym * 2 + 1 - c, y2 * 2 + 1 - c

    def gather_first():
        p_copy(0, g, A, to_yp).start()
        p_copy(1, g, B, to_ym).start()
        p_copy(2, g, B, to_yp).start()
        p_copy(3, g, A, to_ym).start()
        p_copy(4, g, None, to_pal).start()

    def gather_second():
        p_copy(0, g_m, A, to_yp).wait_recv()
        p_copy(5, g_m, A, to_yp).start()
        p_copy(6, g_m, A, to_pal).start()
        p_copy(1, g_p, B, to_ym).wait_recv()
        p_copy(7, g_p, B, to_ym).start()
        p_copy(8, g_p, B, to_pal).start()
        p_copy(2, g_m, B, to_yp).wait_recv()
        p_copy(9, g_m, B, to_pal).start()
        p_copy(3, g_p, A, to_ym).wait_recv()
        p_copy(10, g_p, A, to_pal).start()

    def gather_third():
        p_copy(5, g_2, A, to_yp).wait_recv()
        p_copy(11, g_2, A, to_pal).start()
        p_copy(7, g_2, B, to_ym).wait_recv()
        p_copy(12, g_2, B, to_pal).start()

    def gather_last():
        p_copy(4, h_g, None, to_pal).wait_recv()
        p_copy(6, h_m, A, to_pal).wait_recv()
        p_copy(8, h_p, B, to_pal).wait_recv()
        p_copy(9, h_m, B, to_pal).wait_recv()
        p_copy(10, h_p, A, to_pal).wait_recv()
        p_copy(11, h_2, A, to_pal).wait_recv()
        p_copy(12, h_2, B, to_pal).wait_recv()

    def kx_all():
        part = pl.ds(0, 7 * R)
        return rcopy(kv.at[x, part], kv.at[x, part], kx_s, kx_r, to_pal)

    kx_all().wait_recv()
    KA, KB = pl.ds(0, 256), pl.ds(256, 256)
    to_xp, to_xm = seq_dev(xp, y, c), seq_dev(xm, y, c)

    def k_copy(n, s, half, dev):
        ref = kv.at[s, half]
        return rcopy(ref, ref, k_s, k_r.at[n], dev)

    k_copy(0, x, KA, to_xp).start()
    k_copy(1, x, KB, to_xm).start()
    k_copy(2, x, KB, to_xp).start()
    k_copy(3, x, KA, to_xm).start()

    seven(q_send, q_recv, q_s, q_r).wait_recv()
    gather_first()
    q_in = q_recv[...].astype(F32)
    low = half_lanes((8, 32, 128))
    q_rows = jnp.concatenate([jnp.where(low, q_in, 0.0), jnp.where(low, swap(q_in), 0.0)], axis=1)
    qpad[...] = q_rows.reshape(QROWS, 128).astype(BF)

    def forward(s, n):
        kvt[n] = kv[s].astype(F32).T.astype(BF)
        for q in range(QROWS // QC):
            qs = slice(q * QC, q * QC + QC)
            scores = mm_nt(kv[s], qpad[qs, :])
            top = jnp.max(scores, axis=0, keepdims=True)
            w = jnp.exp(scores - top)
            stat_max[n, :, qs] = top
            stat_sum[n, :, qs] = jnp.sum(w, axis=0, keepdims=True)
            weights[n, :, qs] = w
            part_out[n, :, qs] = mm(kvt[n], w.astype(BF))

    forward(x, 0)
    seven(do_send, do_recv, do_s, do_r).wait_recv()
    d_in = do_recv[...].astype(F32)
    d_rows = jnp.concatenate(
        [jnp.where(low, 0.0, swap(d_in)), jnp.where(low, 0.0, d_in)], axis=1
    ).reshape(QROWS, 128)
    dopad[...] = d_rows.astype(BF)
    dot_ref[...] = d_rows.T

    k_copy(0, xm, KA, to_xp).wait_recv()
    k_copy(4, xm, KA, to_xp).start()
    k_copy(1, xp, KB, to_xm).wait_recv()
    k_copy(5, xp, KB, to_xm).start()
    k_copy(2, xm, KB, to_xp).wait_recv()
    forward(xm, 1)
    k_copy(3, xp, KA, to_xm).wait_recv()
    forward(xp, 2)

    k_copy(4, x2, KA, to_xp).wait_recv()
    k_copy(5, x2, KB, to_xm).wait_recv()
    forward(x2, 3)

    best = jnp.maximum(
        jnp.maximum(stat_max[0], stat_max[1]), jnp.maximum(stat_max[2], stat_max[3])
    )
    facs = [jnp.exp(stat_max[n] - best) for n in range(4)]
    total = sum(facs[n] * stat_sum[n] for n in range(4))
    att_t = sum(facs[n] * part_out[n] for n in range(4)) / total
    att_half = att_t.astype(BF).astype(F32)
    gd_ref[...] = jnp.sum(att_half[64:128] * dot_ref[64:128], axis=0, keepdims=True)
    for n in range(4):
        fac_ref[n] = facs[n] / total
    att3 = att_half.T.reshape(8, R, 128)
    att_send[...] = merge_high(att3[:, 0:32], att3[:, 32:64]).astype(BF)

    def at_copy(peer, lands):
        return rcopy(att_send.at[peer], att_recv.at[lands], at_s, at_r, {"seq": x * 8 + peer})

    for peer in group_peers:
        at_copy(peer, g).start()

    att_recv[g] = att_send[g]

    dq_acc[...] = jnp.zeros((128, QROWS), F32)

    def backward(s, n):
        for q in range(QROWS // QC):
            qs = slice(q * QC, q * QC + QC)
            prob_grad = mm_nt(kv[s], dopad[qs, :])
            prob = weights[n, :, qs] * fac_ref[n, :, qs]
            score_grad = (prob * (prob_grad - gd_ref[:, qs])).astype(BF)
            upd = mm(score_grad, qpad[qs, :]) + mm(prob.astype(BF), dopad[qs, :])
            if q == 0:
                dkv_acc[n] = upd
            else:
                dkv_acc[n] += upd
            dq_acc[:, qs] += mm(kvt[n], score_grad)

    def ring_sum(sends, recvs, ss, rs, part, rows):
        half = rows // 2

        def copy(n, dev):
            return rcopy(sends.at[n], recvs.at[n], ss, rs.at[n], dev)

        def put(n, value, dev):
            sends[n] = value.astype(BF)
            copy(n, dev).start()

        def first():
            put(0, part(x2, 3, slice(0, half)), to_xp)
            put(1, part(x2, 3, slice(half, rows)), to_xm)

        def second():
            put(2, part(xp, 2, slice(half, rows)), to_xp)

        def third():
            put(3, part(xm, 1, slice(0, half)), to_xm)

        def fourth():
            copy(0, to_xp).wait_recv()
            put(4, part(xp, 2, slice(0, half)) + recvs[0].astype(F32), to_xp)
            copy(1, to_xm).wait_recv()
            put(5, part(xm, 1, slice(half, rows)) + recvs[1].astype(F32), to_xm)

        def fifth():
            for n, dev in ((2, to_xp), (3, to_xm), (4, to_xp), (5, to_xm)):
                copy(n, dev).wait_recv()
            up = recvs[4].astype(F32) + recvs[3].astype(F32)
            down = recvs[2].astype(F32) + recvs[5].astype(F32)
            return part(x, 0, slice(0, rows)) + jnp.concatenate([up, down], axis=0)

        def sent():
            rcopy(sends, recvs, ss, rs.at[0], to_xp).wait_send()

        return first, second, third, fourth, fifth, sent

    rs = ring_sum(rs_send, rs_recv, rs_s, rs_r, lambda s, n, part: dkv_acc[n, part], QROWS)
    backward(x2, 3)
    rs[0]()
    gather_second()
    backward(xp, 2)
    rs[1]()
    backward(xm, 1)
    rs[2]()
    backward(x, 0)
    rs[3]()
    dq_rows = jnp.where(half_lanes((QROWS, 128)), dq_acc[...].T * 0.125, 0.0)
    dq3 = dq_rows.reshape(8, R, 128)
    gq_send[...] = merge_low(dq3[:, 0:32], dq3[:, 32:64]).astype(BF)

    def gq_copy(peer, lands):
        return rcopy(gq_send.at[peer], gq_recv.at[lands], gq_s, gq_r, {"seq": x * 8 + peer})

    def g_copy(peer, lands):
        return rcopy(g_send.at[peer], g_recv.at[lands], g_s, g_r, {"seq": x * 8 + peer})

    for peer in group_peers:
        gq_copy(peer, g).start()

    gq_recv[g] = gq_send[g]
    gather_third()
    dkv = rs[4]().astype(BF)
    g_send[...] = dkv.reshape(8, R, 128)

    for peer in group_peers:
        g_copy(peer, g).start()

    g_recv[g] = g_send[g]

    gather_last()
    grads = jnp.concatenate([dkv, dq_rows.astype(BF)], axis=1)
    w_part = mm_tn(grads, pq[...].reshape(QROWS, D))
    for q in range(4):
        wblk[q] = w_part[0:192, q * 256 : q * 256 + 256]

    ws = ring_sum(ws_send, ws_recv, ws_s, ws_r, lambda s, n, part: wblk[s, part], 192)
    for step in ws[0:3]:
        step()

    seven(att_send, att_recv, at_s, at_r).wait_recv()
    stores = [
        pltpu.make_async_copy(a, b, out_sem.at[n])
        for n, (a, b) in enumerate(
            ((att_out, att_hbm.at[0]), (patch_out, patch_hbm.at[0]), (weight_out, weight_hbm))
        )
    ]
    for blk in range(4):
        a0 = att_recv[2 * blk].astype(F32)
        a1 = att_recv[2 * blk + 1].astype(F32)
        lanes = slice(blk * 128, blk * 128 + 128)
        att_out[0:32, lanes] = merge_low(a0, a1).astype(BF)
        att_out[32:64, lanes] = merge_high(a0, a1).astype(BF)
    stores[0].start()

    def lane_block(n):
        return slice(n * 128, n * 128 + 128)

    seven(gq_send, gq_recv, gq_s, gq_r).wait_recv()
    for blk in range(4):
        r0 = gq_recv[2 * blk].astype(F32)
        r1 = gq_recv[2 * blk + 1].astype(F32)
        gnat[0:32, lane_block(blk)] = merge_low(r0, r1).astype(BF)
        gnat[32:64, lane_block(blk)] = merge_high(r0, r1).astype(BF)
    pg_acc[...] = mm_nt(gnat[:, 0:INNER], w_all[:, 0:INNER])

    ws[3]()

    seven(g_send, g_recv, g_s, g_r).wait_recv()
    for blk in range(4):
        r0 = g_recv[2 * blk].astype(F32)
        r1 = g_recv[2 * blk + 1].astype(F32)
        gnat[:, lane_block(blk + 4)] = merge_low(r0, r1).astype(BF)
        gnat[:, lane_block(blk + 8)] = merge_high(r0, r1).astype(BF)

    def back_copy(h, peer, lands):
        return rcopy(
            back_send[h].at[peer, pl.ds(0, TOP)],
            back_recv[h].at[lands, pl.ds(0, TOP)],
            b_s.at[h],
            b_r.at[h],
            {"seq": peer},
        )

    def back_all(h):
        part = (pl.ds(0, NSEQ - 1), pl.ds(0, TOP))
        return rcopy(
            back_send[h].at[part], back_recv[h].at[part], b_s.at[h], b_r.at[h], to_pal
        )

    def make_back(h):
        start, size = PARTS[h]
        cols = slice(start, start + size)
        grad = pg_acc[:, cols] + mm_nt(gnat[:, INNER:], w_all[cols, INNER:])
        back = mm_tn(placer_ref[...], grad.astype(BF))
        back_send[h][...] = back.reshape(NSEQ, CAP, size).astype(BF)

    def send_back(h):
        for peer in clip_peers:
            back_copy(h, peer, i).start()

        back_recv[h][i] = back_send[h][i]

    make_back(0)
    send_back(0)

    w_sum = ws[4]()
    w_kv = w_sum[0:128].T.reshape(8, 32, 128)
    w_qq = jnp.concatenate([w_sum[128:192], jnp.zeros((64, 256), F32)], axis=0)
    w_qq = w_qq.T.reshape(8, 32, 128)
    w15_send[:, 0:32] = w_kv.astype(BF)
    w15_send[:, 32:48] = merge_low(w_qq[:, 0:16], w_qq[:, 16:32]).astype(BF)

    def w15_copy(peer, lands):
        return rcopy(
            w15_send.at[peer], w15_recv.at[lands], w15_s, w15_r, {"seq": x * 8 + peer}
        )

    for peer in group_peers:
        w15_copy(peer, g).start()

    w15_recv[g] = w15_send[g]

    make_back(1)
    send_back(1)
    make_back(2)

    seven(w15_send, w15_recv, w15_s, w15_r).wait_recv()
    q_blocks, k_blocks, v_blocks = [], [], []
    for blk in range(4):
        r0 = w15_recv[2 * blk].astype(F32)
        r1 = w15_recv[2 * blk + 1].astype(F32)
        q_blocks.append(
            jnp.concatenate(
                [merge_low(r0[32:48], r1[32:48]), merge_high(r0[32:48], r1[32:48])], axis=0
            )
        )
        k_blocks.append(merge_low(r0[0:32], r1[0:32]))
        v_blocks.append(merge_high(r0[0:32], r1[0:32]))
    blocks = q_blocks + k_blocks + v_blocks
    width = 3 * INNER // n_clip
    for n in range(n_clip):
        b, off = divmod(width * n, 128)
        if off == 0:
            piece = blocks[b]
        else:
            turn = 128 - off
            piece = pltpu.roll(blocks[b], turn, 1)
            if off + width > 128:
                piece = jnp.where(
                    iota((32, 128), 1) < turn, piece, pltpu.roll(blocks[b + 1], turn, 1)
                )
        tail = piece[24:32]
        last = jnp.concatenate(
            [pltpu.roll(tail, 96, 1), pltpu.roll(tail, 64, 1), pltpu.roll(tail, 32, 1)], axis=0
        )
        w2_send[n] = jnp.where(iota((24, 128), 1) < width, piece[0:24], last).astype(BF)

    def w2_copy(peer, lands):
        return rcopy(w2_send.at[peer], w2_recv.at[lands], w2_s, w2_r, {"clip": peer})

    def w2_all():
        part = pl.ds(0, n_clip - 1)
        return rcopy(w2_send.at[part], w2_recv.at[part], w2_s, w2_r, to_pal)

    @pl.loop(1, n_clip)
    def _(k):
        w2_copy((j + k) % n_clip, j).start()

    w2_recv[j] = w2_send[j]
    send_back(2)

    for h, (start, size) in enumerate(PARTS):
        back_all(h).wait_recv()
        some = iota((NSEQ, CAP, size), 1) < TOP
        returned = jnp.where(some, back_recv[h][...].astype(F32), 0.0).reshape(NMSG, size)
        patch_rows = mm_tn(picker[...], returned.astype(BF))
        patch_out[:, start : start + size] = (patch_rows * count_inv[:, 0:1]).astype(BF)

    stores[1].start()

    w2_all().wait_recv()
    w_rows = jnp.sum(w2_recv[...].astype(F32), axis=0)
    weight_out[0:24] = w_rows[:, 0:width]
    lane = iota((8, 128), 1)
    tail = jnp.where(
        lane < 32,
        pltpu.roll(w_rows[0:8], 32, 1),
        jnp.where(lane < 64, pltpu.roll(w_rows[8:16], 64, 1), pltpu.roll(w_rows[16:24], 96, 1)),
    )
    weight_out[24:32] = tail[:, 0:width]
    stores[2].start()

    slot_all().wait_send()
    token_all().wait_send()
    for h in range(len(PARTS)):
        back_all(h).wait_send()
    kx_all().wait_send()
    seven(q_send, q_recv, q_s, q_r).wait_send()
    seven(do_send, do_recv, do_s, do_r).wait_send()
    seven(att_send, att_recv, at_s, at_r).wait_send()
    seven(g_send, g_recv, g_s, g_r).wait_send()
    seven(gq_send, gq_recv, gq_s, gq_r).wait_send()
    seven(w15_send, w15_recv, w15_s, w15_r).wait_send()
    w2_all().wait_send()
    seven(pq, pq, p_s, p_r.at[0]).wait_send()
    rcopy(kv.at[pl.ds(0, 3)], kv.at[pl.ds(0, 3)], k_s, k_r.at[0], to_xp).wait_send()
    rs[5]()
    ws[5]()
    for store in stores:
        store.wait()


def hand_over(att, patch, weight, att_out, patch_out, weight_out, sems):
    pairs = ((patch, patch_out), (att, att_out), (weight, weight_out))
    moves = [pltpu.make_async_copy(a, b, sems.at[n]) for n, (a, b) in enumerate(pairs)]
    for move in moves:
        move.start()
    for move in moves:
        move.wait()


def local(patches, segment, dest_shard, dest_slot, w_qkv, out_grad):
    n_clip = lax.axis_size("clip")
    v = pltpu.VMEM
    dma = pltpu.SemaphoreType.DMA
    scratch = [
        v((196, D), BF),
        v((1, 196), I32),
        v((1, 192), I32),
        v((1, 192), I32),
        v((R, INNER), BF),
        v((R, INNER), BF),
        v((196, D), BF),
        v((32, 3 * INNER // n_clip), F32),
        v((NSEQ, CAP, D), BF),
        v((NSEQ, CAP, D), BF),
        *[v((NSEQ, CAP, size), BF) for _, size in PARTS],
        *[v((NSEQ, CAP, size), BF) for _, size in PARTS],
        v((D, 3 * INNER), BF),
        v((NMSG, 196), BF),
        v((R, NMSG), BF),
        v((196, 128), F32),
        v((8, R, D), BF),
        v((4, QROWS, 128), BF),
        v((4, 128, QROWS), BF),
        v((QROWS, 128), BF),
        v((QROWS, 128), BF),
        v((128, QROWS), F32),
        v((8, R, 128), BF),
        v((8, 32, 128), BF),
        v((8, 32, 128), BF),
        v((8, 32, 128), BF),
        v((8, 32, 128), BF),
        v((4, QROWS, QROWS), F32),
        v((4, 128, QROWS), F32),
        v((4, 1, QROWS), F32),
        v((4, 1, QROWS), F32),
        v((4, 1, QROWS), F32),
        v((1, QROWS), F32),
        v((8, 32, 128), BF),
        v((8, 32, 128), BF),
        v((4, QROWS, 128), F32),
        v((128, QROWS), F32),
        v((6, 256, 128), BF),
        v((6, 256, 128), BF),
        v((8, R, 128), BF),
        v((8, R, 128), BF),
        v((8, 32, 128), BF),
        v((8, 32, 128), BF),
        v((R, 3 * INNER), BF),
        v((R, D), F32),
        v((4, 192, 256), F32),
        v((6, 96, 256), BF),
        v((6, 96, 256), BF),
        v((8, 48, 128), BF),
        v((8, 48, 128), BF),
        v((n_clip, 24, 128), BF),
        v((n_clip, 24, 128), BF),
        dma((6,)),
        dma((3,)),
        dma,
        dma,
        dma,
        dma,
        dma((3,)),
        dma((3,)),
        dma,
        dma((13,)),
        dma,
        dma((6,)),
        dma,
        dma,
        dma,
        dma,
        dma,
        dma,
        dma,
        dma,
        dma,
        dma((6,)),
        dma,
        dma,
        dma,
        dma,
        dma,
        dma((6,)),
        dma,
        dma,
        dma,
        dma,
    ]
    anywhere = pl.BlockSpec(memory_space=pl.ANY)
    shapes = (
        jax.ShapeDtypeStruct((1, R, INNER), BF),
        jax.ShapeDtypeStruct((1, 196, D), BF),
        jax.ShapeDtypeStruct((32, 3 * INNER // n_clip), F32),
    )
    operands = (patches, segment, dest_shard, dest_slot, w_qkv, out_grad)
    results = pl.pallas_call(
        functools.partial(kernel, n_clip),
        out_shape=shapes,
        in_specs=[anywhere] * 6,
        out_specs=(anywhere,) * 3,
        scratch_shapes=scratch,
        compiler_params=pltpu.CompilerParams(
            collective_id=0, has_side_effects=True, vmem_limit_bytes=40 * 1024 * 1024
        ),
        name="rebalance_attention",
    )(*[pltpu.with_memory_space_constraint(a, pltpu.HBM) for a in operands])
    return pl.pallas_call(
        hand_over,
        out_shape=shapes,
        in_specs=[anywhere] * 3,
        out_specs=(anywhere,) * 3,
        scratch_shapes=[dma((3,))],
        compiler_params=pltpu.CompilerParams(vmem_limit_bytes=2 * 1024 * 1024),
        name="hand_over",
    )(*results)


def solution(mesh):
    return jax.shard_map(
        local,
        mesh=mesh,
        in_specs=(
            P("clip", "seq", None),
            P("clip", "seq"),
            P("clip", "seq"),
            P("clip", "seq"),
            P(),
            P("clip", "seq", None),
        ),
        out_specs=(P("clip", "seq", None), P("clip", "seq", None), P("seq", "clip")),
        check_vma=False,
    )
```
